128 devices in a mesh: lat: 8 (over y_hi, z), lon: 16 (over y_lo, x, core).
Axes of the slice: x: 4, y: 4 (y_hi: 2, y_lo: 2; y = y_hi * 2 + y_lo), z: 4, core: 2. Of those that a mesh axis runs over, the one named last changes fastest.
Arguments:
- satellite_blocks: bfloat16 [16384, 16, 128], P(('lat', 'lon')), may hold values from -6 to 6
- slot_source: int32 [128, 128, 4], P(('lat', 'lon')), may hold values from 0 to 127
- slot_weight: bfloat16 [128, 128, 4, 8, 128], P(('lat', 'lon')), may hold values from -2 to 2
- slot_target: int32 [128, 128, 4], P(('lat', 'lon')), may hold values from 0 to 63
- tile_counts: int32 [128, 128], P(('lat', 'lon')), may hold values from 0 to 4, as said below
- gate_input_weight: bfloat16 [128, 144], replicated, may hold values from -0.5 to 0.5
- gate_state_weight: bfloat16 [128, 288], replicated, may hold values from -0.375 to 0.375
- gate_bias: float32 [128], replicated, may hold values from -4 to 4
- hidden_init: bfloat16 [32, 256, 4096], P(None, 'lat', 'lon'), may hold values from -1 to 1
- cell_init: bfloat16 [32, 256, 4096], P(None, 'lat', 'lon'), may hold values from -6 to 6
Outputs:
- hidden_out: bfloat16 [32, 256, 4096], P(None, 'lat', 'lon')
- cell_out: bfloat16 [32, 256, 4096], P(None, 'lat', 'lon')
The draws below stay inside these ranges and needn't reach their ends.
Inputs may be any that keep to these rules, and one draw needn't show every extreme that they name: slot_source[p, q, s] names one of the 128 blocks held by source device p. slot_target[q, p, s] is the cell block of tile q fed by slot s from device p. Only slots s < tile_counts[q, p] carry data from device p to tile q; at least one tile receives 4 blocks from every source device.
All inputs are finite; a program needn't handle non-finite values.
Results may differ from the reference program's by a relative error of at most 0.0069.
Values may be sent and summed in bfloat16 or wider, within the bound.
A program may use at most 128 MiB of HBM per device.

```python
import jax
import jax.numpy as jnp
from jax import lax

CH = 16
HID = 32
GATES = 128
BLOCK = 128
BAND = 8
CAP = 4
STEPS = 3
TLAT = 32
TLON = 256
SB_DEV = 128
DB_DEV = 64
NLAT = 256
NLON = 4096
SRC = 16384
N_LAT = 8
N_LON = 16
DEVICES = 128


def draw_tile_counts(key, part):
    key_first, key_second, key_third = jax.random.split(key, 3)
    first = jax.random.randint(key_first, (DEVICES, DEVICES), 0, CAP + 1)
    second = jax.random.randint(key_second, (DEVICES, DEVICES), 0, CAP + 1)
    hottest = jax.random.randint(key_third, (), 0, DEVICES)
    tiles = jnp.arange(DEVICES, dtype=jnp.int32)[:, None]
    base = jnp.minimum(first, second)
    return jnp.where(tiles == hottest, CAP, base).astype(jnp.int32)


def with_ends(drawn, rng, low, high):
    shape = drawn.shape
    spot = [jax.random.randint(jax.random.fold_in(rng, axis), (), 0, shape[axis]) for axis in range(len(shape))]
    drawn = drawn.at[tuple(spot)].set(low)
    longest = shape.index(max(shape))
    spot[longest] = (spot[longest] + 1) % shape[longest]
    return drawn.at[tuple(spot)].set(high)


def levels(rng, extent, cuts, least, top_value):
    def one(dim, shards_of):
        heights = jax.random.uniform(jax.random.fold_in(jax.random.fold_in(rng, 6), dim), (shards_of,), jnp.float32, least / len(cuts), top_value / len(cuts))
        return jnp.repeat(jnp.exp(heights), extent[dim] // shards_of).reshape((-1,) + (1,) * (len(extent) - dim - 1))

    level = one(*cuts[0])
    for cut in cuts[1:]:
        level = level * one(*cut)
    return level


def noise(stream_key, dims, spread, most, cuts=(), kind=jnp.bfloat16):
    loudness = levels(stream_key, dims, cuts, -0.22, 0.18) if cuts else 1.0
    values = jax.random.normal(stream_key, dims, jnp.float32) * spread * loudness
    return jnp.minimum(jnp.maximum(values, -most), most).astype(kind)


def setup_inputs(seed: int = 0) -> dict:
    seeds = jax.random.split(jax.random.key(seed), 11)
    return {
        "satellite_blocks": noise(seeds[0], (SRC, CH, BLOCK), 1.0, 6.0, ((0, 128),)),
        "slot_source": with_ends(jax.random.randint(seeds[1], (DEVICES, DEVICES, CAP), 0, SB_DEV), jax.random.fold_in(seeds[1], 1), 0, SB_DEV - 1).astype(jnp.int32),
        "slot_weight": noise(seeds[2], (DEVICES, DEVICES, CAP, BAND, BLOCK), BAND ** -0.5, 2.0, ((0, 128),)),
        "slot_target": with_ends(jax.random.randint(seeds[3], (DEVICES, DEVICES, CAP), 0, DB_DEV), jax.random.fold_in(seeds[3], 1), 0, DB_DEV - 1).astype(jnp.int32),
        "tile_counts": draw_tile_counts(jax.random.fold_in(seeds[10], 71), 0),
        "gate_input_weight": noise(seeds[5], (GATES, 9 * CH), (9 * CH) ** -0.5, 0.5),
        "gate_state_weight": noise(seeds[6], (GATES, 9 * HID), (9 * HID) ** -0.5, 0.375),
        "gate_bias": noise(seeds[7], (GATES,), 1.0, 4.0, (), jnp.float32),
        "hidden_init": jnp.clip(jax.random.uniform(seeds[8], (HID, NLAT, NLON), jnp.float32, -1.0, 1.0) * levels(seeds[8], (HID, NLAT, NLON), ((1, 8), (2, 16)), -0.4, 0.0), -1.0, 1.0).astype(jnp.bfloat16),
        "cell_init": noise(seeds[9], (HID, NLAT, NLON), 1.0, 6.0, ((1, 8), (2, 16))),
    }


def band_apply(picked, weights):
    band_size = weights.shape[-2]
    margin_left = band_size // 2
    values = picked.astype(jnp.float32)
    padded = jnp.pad(values, ((0, 0), (0, 0), (0, 0), (margin_left, band_size - 1 - margin_left)))
    summed = jnp.zeros(values.shape, jnp.float32)
    for offset in range(band_size):
        factor = weights[:, :, offset, :].astype(jnp.float32)[:, :, None, :]
        summed = summed + factor * padded[..., offset:offset + values.shape[-1]]
    return summed.astype(jnp.bfloat16)


def convolve(padded, weights, row_count, column_count):
    shifted_list = [padded[:, row_shift:row_shift + row_count, column_shift:column_shift + column_count]
                    for row_shift in range(3) for column_shift in range(3)]
    stacked = jnp.concatenate(shifted_list, axis=0)
    flattened = stacked.reshape(stacked.shape[0], row_count * column_count)
    result = jnp.dot(weights, flattened, preferred_element_type=jnp.float32)
    return result.reshape(weights.shape[0], row_count, column_count)


def cell_update(gates, memory):
    hidden_units = gates.shape[0] // 4
    ingate = jax.nn.sigmoid(gates[:hidden_units])
    forget = jax.nn.sigmoid(gates[hidden_units:2 * hidden_units])
    outgate = jax.nn.sigmoid(gates[2 * hidden_units:3 * hidden_units])
    candidate = jnp.tanh(gates[3 * hidden_units:])
    memory = forget * memory + ingate * candidate
    hidden = (outgate * jnp.tanh(memory)).astype(jnp.bfloat16)
    return hidden, memory


def wrap_pad(field):
    widened = jnp.pad(field, ((0, 0), (0, 0), (1, 1)), mode="wrap")
    return jnp.pad(widened, ((0, 0), (1, 1), (0, 0)))


def reference(satellite_blocks, slot_source, slot_weight, slot_target, tile_counts,
              gate_input_weight, gate_state_weight, gate_bias, hidden_init, cell_init):
    def one_source(totals, source_index):
        blocks = lax.dynamic_slice_in_dim(satellite_blocks, source_index * SB_DEV, SB_DEV, 0)
        picked = jnp.take(blocks, slot_source[source_index], axis=0)
        contribution = band_apply(picked, slot_weight[source_index]).astype(jnp.float32)
        live_slot = jnp.arange(CAP, dtype=jnp.int32)[None, :] < tile_counts[:, source_index][:, None]
        contribution = jnp.where(live_slot[:, :, None, None], contribution, jnp.zeros_like(contribution))
        tiles = jnp.broadcast_to(jnp.arange(DEVICES, dtype=jnp.int32)[:, None], (DEVICES, CAP))
        totals = totals.at[tiles, slot_target[:, source_index, :]].add(contribution)
        return totals, None

    start_totals = jnp.zeros((DEVICES, DB_DEV, CH, BLOCK), jnp.float32)
    totals, _ = lax.scan(one_source, start_totals, jnp.arange(DEVICES, dtype=jnp.int32))
    forcing_blocks = totals.astype(jnp.bfloat16)
    forcing = forcing_blocks.transpose(0, 2, 1, 3).reshape(N_LAT, N_LON, CH, TLAT, TLON)
    forcing = forcing.transpose(2, 0, 3, 1, 4).reshape(CH, NLAT, NLON)

    forcing_padded = wrap_pad(forcing)
    hidden = hidden_init
    memory = cell_init.astype(jnp.float32)
    for update_index in range(STEPS):
        hidden_padded = wrap_pad(hidden)

        def one_band(band_index):
            start = band_index * TLAT
            forcing_slab = lax.dynamic_slice_in_dim(forcing_padded, start, TLAT + 2, 1)
            hidden_slab = lax.dynamic_slice_in_dim(hidden_padded, start, TLAT + 2, 1)
            memory_slab = lax.dynamic_slice_in_dim(memory, start, TLAT, 1)
            forcing_gates = convolve(forcing_slab, gate_input_weight, TLAT, NLON) + gate_bias[:, None, None]
            gates = forcing_gates + convolve(hidden_slab, gate_state_weight, TLAT, NLON)
            return cell_update(gates, memory_slab)

        band_hidden, band_memory = lax.map(one_band, jnp.arange(N_LAT, dtype=jnp.int32))
        hidden = band_hidden.transpose(1, 0, 2, 3).reshape(HID, NLAT, NLON)
        memory = band_memory.transpose(1, 0, 2, 3).reshape(HID, NLAT, NLON)
    return hidden, memory.astype(jnp.bfloat16)
```

```python
import jax
import jax.numpy as jnp
from jax import lax
from jax.experimental import pallas as pl
from jax.experimental.pallas import tpu as pltpu
from jax.sharding import PartitionSpec as P

STEPS = 3
MESH = pl.DeviceIdType.MESH


def coords():
    i = lax.axis_index("lat")
    j = lax.axis_index("lon")
    return (lax.rem(lax.div(j, 2), 4), lax.div(i, 4) * 2 + lax.div(j, 8), lax.rem(i, 4), lax.rem(j, 2))


def device_at(x, y, z, c):
    return lax.div(y, 2) * 4 + z, lax.rem(y, 2) * 8 + x * 2 + c


def offset_of(n):
    m = lax.rem(n * 45, 128)
    return lax.rem(m, 4), lax.rem(lax.div(m, 4), 4), lax.rem(lax.div(m, 16), 4), lax.div(m, 64)


def peer(n):
    x, y, z, c = coords()
    dx, dy, dz, dc = offset_of(n)
    return device_at(lax.rem(x + dx, 4), lax.rem(y + dy, 4), lax.rem(z + dz, 4), lax.rem(c + dc, 2))


def exchange_kernel(out_ref, in_ref, send_sem, recv_sem, own_sem):
    barrier = pltpu.get_barrier_semaphore()

    def greet(n, carry):
        pl.semaphore_signal(barrier, inc=1, device_id=peer(n), device_id_type=MESH)
        return carry

    lax.fori_loop(1, 128, greet, 0)
    me = lax.axis_index("lat") * 16 + lax.axis_index("lon")
    own = pltpu.make_async_copy(out_ref.at[me], in_ref.at[me], own_sem)
    own.start()
    pl.semaphore_wait(barrier, 127)

    def send(n, carry):
        la, lo = peer(n)
        pltpu.make_async_remote_copy(
            src_ref=out_ref.at[la * 16 + lo],
            dst_ref=in_ref.at[me],
            send_sem=send_sem,
            recv_sem=recv_sem,
            device_id=(la, lo),
            device_id_type=MESH,
        ).start()
        return carry

    lax.fori_loop(1, 128, send, 0)
    own.wait()
    everything = pltpu.make_async_remote_copy(
        src_ref=out_ref.at[pl.ds(0, 127)],
        dst_ref=in_ref.at[pl.ds(0, 127)],
        send_sem=send_sem,
        recv_sem=recv_sem,
        device_id=peer(1),
        device_id_type=MESH,
    )
    everything.wait_send()
    everything.wait_recv()


def exchange(outgoing):
    return pl.pallas_call(
        exchange_kernel,
        out_shape=jax.ShapeDtypeStruct(outgoing.shape, outgoing.dtype),
        in_specs=[pl.BlockSpec(memory_space=pltpu.VMEM)],
        out_specs=pl.BlockSpec(memory_space=pltpu.VMEM),
        scratch_shapes=[pltpu.SemaphoreType.DMA] * 3,
        compiler_params=pltpu.CompilerParams(collective_id=0, has_side_effects=True),
        name="exchange",
    )(outgoing)


def with_halo(cells, sides, width, closed):
    for axis, dim in sides:
        count = lax.axis_size(axis)
        ends = count if closed else count - 1
        head = lax.slice_in_dim(cells, 0, width, axis=dim)
        tail = lax.slice_in_dim(cells, cells.shape[dim] - width, cells.shape[dim], axis=dim)
        cells = jnp.concatenate(
            [
                lax.ppermute(tail, axis, [(i, (i + 1) % count) for i in range(ends)]),
                cells,
                lax.ppermute(head, axis, [((i + 1) % count, i) for i in range(ends)]),
            ],
            axis=dim,
        )
    return cells


def band_apply(picked, weights):
    band_size = weights.shape[-2]
    margin_left = band_size // 2
    values = picked.astype(jnp.float32)
    padded = jnp.pad(values, ((0, 0), (0, 0), (0, 0), (margin_left, band_size - 1 - margin_left)))
    summed = jnp.zeros(values.shape, jnp.float32)
    for offset in range(band_size):
        factor = weights[:, :, offset, :].astype(jnp.float32)[:, :, None, :]
        summed = summed + factor * padded[..., offset : offset + values.shape[-1]]
    return summed.astype(jnp.bfloat16)


def convolve(padded, weights, row_count, column_count):
    shifted_list = [
        padded[:, row_shift : row_shift + row_count, column_shift : column_shift + column_count]
        for row_shift in range(3)
        for column_shift in range(3)
    ]
    stacked = jnp.concatenate(shifted_list, axis=0)
    flattened = stacked.reshape(stacked.shape[0], row_count * column_count)
    result = jnp.dot(weights, flattened, preferred_element_type=jnp.float32)
    return result.reshape(weights.shape[0], row_count, column_count)


def cell_update(gates, memory):
    hidden_units = gates.shape[0] // 4
    ingate = jax.nn.sigmoid(gates[:hidden_units])
    forget = jax.nn.sigmoid(gates[hidden_units : 2 * hidden_units])
    outgate = jax.nn.sigmoid(gates[2 * hidden_units : 3 * hidden_units])
    candidate = jnp.tanh(gates[3 * hidden_units :])
    memory = forget * memory + ingate * candidate
    hidden = (outgate * jnp.tanh(memory)).astype(jnp.bfloat16)
    return (hidden, memory)


def widen(field, halo_width):
    widened = with_halo(field, (("lon", 2),), halo_width, True)
    return with_halo(widened, (("lat", 1),), halo_width, False)


def on_device(
    satellite_blocks,
    slot_source,
    slot_weight,
    slot_target,
    tile_counts,
    gate_input_weight,
    gate_state_weight,
    gate_bias,
    hidden_init,
    cell_init,
):
    channels = satellite_blocks.shape[1]
    picked = jnp.take(satellite_blocks, slot_source[0], axis=0)
    outgoing = band_apply(picked, slot_weight[0])
    incoming = exchange(outgoing)
    tile_rows = hidden_init.shape[1]
    tile_cols = hidden_init.shape[2]
    block_size = incoming.shape[-1]
    block_count = tile_rows * tile_cols // block_size
    slot_total = incoming.shape[0] * incoming.shape[1]
    live_slot = jnp.arange(incoming.shape[1], dtype=jnp.int32)[None, :] < tile_counts[0][:, None]
    chosen = (slot_target[0][:, :, None] == jnp.arange(block_count, dtype=jnp.int32)) & live_slot[
        :, :, None
    ]
    selector = chosen.astype(jnp.bfloat16).reshape(slot_total, block_count)
    summed = jnp.einsum(
        "rcj,rb->cbj",
        incoming.reshape(slot_total, channels, block_size),
        selector,
        preferred_element_type=jnp.float32,
    )
    forcing = summed.astype(jnp.bfloat16).reshape(channels, tile_rows, tile_cols)
    bias_column = gate_bias[:, None, None]
    padded = widen(jnp.concatenate([forcing, hidden_init], axis=0), 1)
    forcing_gates = (
        convolve(padded[:channels], gate_input_weight, tile_rows, tile_cols) + bias_column
    )
    hidden_padded = padded[channels:]
    memory = cell_init.astype(jnp.float32)
    for update_index in range(STEPS):
        if update_index > 0:
            hidden_padded = widen(hidden, 1)
        gates = forcing_gates + convolve(hidden_padded, gate_state_weight, tile_rows, tile_cols)
        hidden, memory = cell_update(gates, memory)
    return (hidden, memory.astype(jnp.bfloat16))


def solution(mesh):
    placed = (
        P(("lat", "lon"), None, None),
        P(("lat", "lon"), None, None),
        P(("lat", "lon"), None, None, None, None),
        P(("lat", "lon"), None, None),
        P(("lat", "lon"), None),
        P(),
        P(),
        P(),
        P(None, "lat", "lon"),
        P(None, "lat", "lon"),
    )
    return jax.shard_map(
        on_device,
        mesh=mesh,
        in_specs=placed,
        out_specs=(P(None, "lat", "lon"), P(None, "lat", "lon")),
        check_vma=False,
    )
```

```python
import functools
import itertools
import random

import jax
import jax.numpy as jnp
import numpy as np
from jax import lax
from jax.experimental import pallas as pl
from jax.experimental.pallas import tpu as pltpu
from jax.sharding import PartitionSpec as P

STEPS = 3
MESH = pl.DeviceIdType.MESH
F32 = jnp.float32
BF16 = jnp.bfloat16
PEERS = 128
SLOTS = 4
CHUNKS = 4
ROWS = 32
COLS = 256
CH = 16
HID = 32


def send_order():
    offsets = [d for d in itertools.product(range(4), range(4), range(4), range(2)) if any(d)]
    random.Random(0).shuffle(offsets)
    return [(0, 0, 0, 0)] + offsets


ORDER = send_order()


def coords():
    i = lax.axis_index("lat")
    j = lax.axis_index("lon")
    return (lax.rem(lax.div(j, 2), 4), lax.div(i, 4) * 2 + lax.div(j, 8), lax.rem(i, 4), lax.rem(j, 2))


def device_at(x, y, z, c):
    return lax.div(y, 2) * 4 + z, lax.rem(y, 2) * 8 + x * 2 + c


def peer(offset):
    return device_at(*(lax.rem(a + d, m) for a, d, m in zip(coords(), offset, (4, 4, 4, 2))))


def peer_table(sign):
    table = np.array(ORDER, np.int32)
    at = [lax.rem(a + jnp.asarray((sign * table[:, k]) % m), m) for k, (a, m) in enumerate(zip(coords(), (4, 4, 4, 2)))]
    lat, lon = device_at(*at)
    return lat * 16 + lon


def lanes(shape):
    return lax.broadcasted_iota(jnp.int32, shape, len(shape) - 1)


def sublanes(shape):
    return lax.broadcasted_iota(jnp.int32, shape, len(shape) - 2)


def roll(x, shift):
    return pltpu.roll(x, shift, 1)


def band(n, to, to_index, ptab, stab, x_ref, w_ref):
    tile = ptab[n]
    lane = lanes((8, 128)) + sublanes((8, 128))
    inside = (lane >= 4) & (lane < 132)
    for s in range(SLOTS):
        x = x_ref[stab[tile * SLOTS + s]].astype(F32)
        w = jnp.where(inside, w_ref[tile, s].astype(F32), 0.0)
        total = w[4:5] * x
        for k in (0, 1, 2, 3, 5, 6, 7):
            total = total + w[k : k + 1] * roll(x, (4 - k) % 128)
        to[to_index, s] = total.astype(BF16)


def pick_columns(rows_ref, count, left_lane, right_lane):
    lane = lanes((count, 128))

    def one(y, total):
        row = pl.ds(pl.multiple_of(y * count, count), count)
        left = roll(rows_ref[0, row], lax.rem(y + 1 - left_lane + 128, 128))
        right = roll(rows_ref[1, row], lax.rem(y + 65 - right_lane + 128, 128))
        total = jnp.where(lane == y + 1, left, total)
        return jnp.where(lane == y + 65, right, total)

    return lax.fori_loop(0, ROWS, one, jnp.zeros((count, 128), F32), unroll=4)


def put_columns(rows_ref, count, columns):
    lane = lanes((count, 128))

    def one(y, carry):
        row = pl.ds(pl.multiple_of(y * count, count), count)
        left = roll(columns, lax.rem(127 - y, 128))
        right = roll(columns, lax.rem(190 - y, 128))
        rows_ref[0, row] = jnp.where(lane == 0, left, rows_ref[0, row])
        rows_ref[1, row] = jnp.where(lane == 127, right, rows_ref[1, row])
        return carry

    lax.fori_loop(0, ROWS, one, 0, unroll=4)


def spread(row, into, count, at):
    where = pl.ds(at, COLS)
    into[0:count, where] = roll(row, 1).astype(BF16)
    into[count : 2 * count, where] = row.astype(BF16)
    into[2 * count : 3 * count, where] = roll(row, COLS - 1).astype(BF16)


def row_at(rows_ref, y, count):
    row = pl.ds(pl.multiple_of(y * count, count), count)
    return jnp.concatenate([rows_ref[0, row], rows_ref[1, row]], axis=1)


def spread_rows(rows_ref, into, count):
    def one(y, carry):
        spread(row_at(rows_ref, y, count), into, count, pl.multiple_of((y + 1) * COLS, COLS))
        return carry

    lax.fori_loop(0, ROWS, one, 0, unroll=4)


def stage(rows_ref, count, edge, near, q_ref):
    last = (ROWS - 1) * count
    q_ref[0] = rows_ref[0, 0:count].astype(BF16)
    q_ref[1] = rows_ref[1, 0:count].astype(BF16)
    q_ref[2] = edge.astype(BF16)
    q_ref[3] = near.astype(BF16)
    q_ref[4] = rows_ref[0, last : last + count].astype(BF16)
    q_ref[5] = rows_ref[1, last : last + count].astype(BF16)


def swap(q_ref, r_ref, send_sem, recv_sem):
    i = lax.axis_index("lat")
    j = lax.axis_index("lon")
    up, down = lax.rem(i + 7, 8), lax.rem(i + 1, 8)
    left, right = lax.rem(j + 15, 16), lax.rem(j + 1, 16)
    plan = (
        ((up, j), 0, 4, 4),
        ((down, j), 2, 4, 0),
        ((i, left), 2, 1, 9),
        ((i, right), 2, 1, 8),
        ((up, left), 2, 1, 13),
        ((up, right), 2, 1, 12),
        ((down, left), 2, 1, 11),
        ((down, right), 2, 1, 10),
    )
    for target, source, size, slot in plan:
        pltpu.make_async_remote_copy(
            src_ref=q_ref.at[pl.ds(source, size)],
            dst_ref=r_ref.at[pl.ds(slot, size)],
            send_sem=send_sem,
            recv_sem=recv_sem,
            device_id=target,
            device_id_type=MESH,
        ).start()


def whole(r_ref, send_sem, recv_sem):
    i = lax.axis_index("lat")
    return pltpu.make_async_remote_copy(
        src_ref=r_ref,
        dst_ref=r_ref,
        send_sem=send_sem,
        recv_sem=recv_sem,
        device_id=(lax.rem(i + 1, 8), lax.axis_index("lon")),
        device_id_type=MESH,
    )


def edge_inputs(edge, near, r_ref, count):
    i = lax.axis_index("lat")
    lane = lanes((count, 128))
    half = lane < 64
    place = jnp.where(half, lane, lane - 64)
    top = (place == 0) & (i > 0)
    bottom = (place == 33) & (i < 7)
    middle = (place >= 1) & (place <= 32)
    got = lambda k: r_ref[k].astype(F32)

    def frame(mid, above, below):
        return jnp.where(middle, mid, jnp.where(top, above, jnp.where(bottom, below, 0.0)))

    edges = frame(edge, roll(got(0), 96), roll(got(6), 32))
    nears = frame(near, roll(got(1), 96), roll(got(7), 32))
    sides = frame(
        jnp.where(half, roll(got(8), 64), roll(got(9), 64)),
        jnp.where(half, roll(got(10), 32), roll(got(11), 32)),
        jnp.where(half, roll(got(12), 96), roll(got(13), 96)),
    )
    three = (jnp.where(half, sides, nears), edges, jnp.where(half, nears, sides))
    above = [roll(v, 1) for v in three]
    below = [roll(v, 127) for v in three]
    return jnp.concatenate([v.astype(BF16) for v in (*above, *three, *below)], axis=0)


def halo_rows(r_ref, into, count):
    i = lax.axis_index("lat")
    for slot, live, at in ((2, i > 0, 0), (4, i < 7, (ROWS + 1) * COLS)):
        row = jnp.concatenate([r_ref[slot].astype(F32), r_ref[slot + 1].astype(F32)], axis=1)
        spread(jnp.where(live, row, 0.0), into, count, at)


def update(gates, memory):
    ingate = jnp.tanh(gates[0:HID]) * 0.5 + 0.5
    forget = jnp.tanh(gates[HID : 2 * HID]) * 0.5 + 0.5
    outgate = jnp.tanh(gates[2 * HID : 3 * HID]) * 0.5 + 0.5
    memory = forget * memory + ingate * jnp.tanh(gates[3 * HID :])
    return outgate * jnp.tanh(memory), memory


def body(
    ptab, stab, x_ref, w_ref, aim_ref, from_ref, weight_ref, bias_ref, hid_ref, cell_ref,
    hout_ref, cout_ref,
    out_buf, in_buf, wide, sums, h0, h1, shifted, fc, fshifted, cells,
    qh, rh, qf, rf, far_send, far_recv, near_send, near_recv,
):
    barrier = pltpu.get_barrier_semaphore()
    for offset in ORDER[1:]:
        pl.semaphore_signal(barrier, inc=1, device_id=peer(offset), device_id_type=MESH)

    band(0, in_buf, 0, ptab, stab, x_ref, w_ref)

    def one_band(n, carry):
        band(n, out_buf, n, ptab, stab, x_ref, w_ref)
        return carry

    lax.fori_loop(1, PEERS, one_band, 0)

    for c in range(HID):
        for half in range(2):
            h0[half, pl.ds(c, ROWS, stride=HID), :] = hid_ref[c, :, half * 128 : half * 128 + 128].astype(F32)
    edge = pick_columns(h0, HID, 0, 127)
    near = pick_columns(h0, HID, 1, 126)
    stage(h0, HID, edge, near, qh.at[0])

    pl.semaphore_wait(barrier, PEERS - 1)
    swap(qh.at[0], rh.at[0], near_send.at[0], near_recv.at[0])
    size = PEERS // CHUNKS
    for n in range(1, PEERS):
        pltpu.make_async_remote_copy(
            src_ref=out_buf.at[n],
            dst_ref=in_buf.at[n],
            send_sem=far_send,
            recv_sem=far_recv.at[n // size],
            device_id=peer(ORDER[n]),
            device_id_type=MESH,
        ).start()

    for c in range(HID):
        for half in range(2):
            cells[half, pl.ds(c, ROWS, stride=HID), :] = cell_ref[c, :, half * 128 : half * 128 + 128].astype(F32)
    edge_cell = pick_columns(cells, HID, 0, 127)
    spread_rows(h0, shifted, HID)

    taken = size * SLOTS
    sums[...] = jnp.zeros_like(sums)
    for g in range(CHUNKS):
        first = 1 if g == 0 else g * size
        count = (g + 1) * size - first
        pltpu.make_async_remote_copy(
            src_ref=in_buf.at[pl.ds(first, count)],
            dst_ref=in_buf.at[pl.ds(first, count)],
            send_sem=far_send,
            recv_sem=far_recv.at[g],
            device_id=peer(ORDER[1]),
            device_id_type=MESH,
        ).wait_recv()

        def unpack(n, carry):
            block = in_buf[g * size + n].astype(F32).reshape(SLOTS * CH, 128)
            wide[pl.ds(pl.multiple_of(n * SLOTS * CH, SLOTS * CH), SLOTS * CH)] = block
            return carry

        lax.fori_loop(0, size, unpack, 0, unroll=4)
        spot = (sublanes((128, 128)) == from_ref[g : g + 1, :]).astype(F32).astype(BF16)
        aims = jnp.dot(aim_ref[...].astype(BF16), spot, preferred_element_type=F32)
        mine = sublanes((8, 128)) == lax.rem(lanes((8, 128)), SLOTS)
        aim = jnp.sum(jnp.where(mine, aims, 0.0), axis=0, keepdims=True)
        chosen = (sublanes((64, 128)).astype(F32) == aim).astype(F32).astype(BF16)
        for c in range(0, CH, 2):
            pair = [wide[pl.ds(c + k, taken, stride=CH), :].astype(BF16) for k in range(2)]
            part = jnp.dot(chosen, jnp.concatenate(pair, axis=1), preferred_element_type=F32)
            sums[c * 64 : c * 64 + 64] += part[:, :128]
            sums[c * 64 + 64 : c * 64 + 128] += part[:, 128:]

    def fill(y, carry):
        where = pl.ds(pl.multiple_of(y * CH, CH), CH)
        fc[0, where] = sums[pl.ds(2 * y, CH, stride=64), :]
        fc[1, where] = sums[pl.ds(2 * y + 1, CH, stride=64), :]
        return carry

    lax.fori_loop(0, ROWS, fill, 0, unroll=4)
    fedge = pick_columns(fc, CH, 0, 127)
    fnear = pick_columns(fc, CH, 1, 126)
    stage(fc, CH, fedge, fnear, qf)
    spread_rows(fc, fshifted, CH)
    swap(qf, rf, near_send.at[STEPS], near_recv.at[STEPS])

    bias = bias_ref[...]
    here, there = h0, h1
    fmini = None
    for t in range(STEPS):

        def one_row(y, carry):
            rhs = jnp.concatenate(
                [shifted[:, pl.ds(pl.multiple_of((y + a) * COLS, COLS), COLS)] for a in range(3)]
                + [fshifted[:, pl.ds(pl.multiple_of((y + a) * COLS, COLS), COLS)] for a in range(3)],
                axis=0,
            )
            gates = jnp.dot(weight_ref[...], rhs, preferred_element_type=F32) + bias
            where = pl.ds(pl.multiple_of(y * HID, HID), HID)
            hidden, memory = update(gates, row_at(cells, y, HID))
            for half in range(2):
                cells[half, where] = memory[:, half * 128 : half * 128 + 128]
                there[half, where] = hidden[:, half * 128 : half * 128 + 128]
            return carry

        lax.fori_loop(1, ROWS - 1, one_row, 0, unroll=2)

        whole(rh.at[t], near_send.at[t], near_recv.at[t]).wait_recv()
        if t == 0:
            whole(rf, near_send.at[STEPS], near_recv.at[STEPS]).wait_recv()
            fmini = edge_inputs(fedge, fnear, rf, CH)
            halo_rows(rf, fshifted, CH)
        mini = jnp.concatenate([edge_inputs(edge, near, rh.at[t], HID), fmini], axis=0)
        gates = jnp.dot(weight_ref[...], mini, preferred_element_type=F32) + bias[:, :128]
        edge, edge_cell = update(gates, edge_cell)
        halo_rows(rh.at[t], shifted, HID)
        one_row(0, 0)
        one_row(ROWS - 1, 0)
        put_columns(there, HID, edge)
        if t < STEPS - 1:
            near = pick_columns(there, HID, 1, 126)
            stage(there, HID, edge, near, qh.at[t + 1])
            spread_rows(there, shifted, HID)
            swap(qh.at[t + 1], rh.at[t + 1], near_send.at[t + 1], near_recv.at[t + 1])
        here, there = there, here

    put_columns(cells, HID, edge_cell)
    for c in range(HID):
        for half in range(2):
            part = slice(half * 128, half * 128 + 128)
            hout_ref[c, :, part] = here[half, pl.ds(c, ROWS, stride=HID), :].astype(BF16)
            cout_ref[c, :, part] = cells[half, pl.ds(c, ROWS, stride=HID), :].astype(BF16)

    pltpu.make_async_remote_copy(
        src_ref=in_buf.at[pl.ds(1, PEERS - 1)],
        dst_ref=in_buf.at[pl.ds(1, PEERS - 1)],
        send_sem=far_send,
        recv_sem=far_recv.at[0],
        device_id=peer(ORDER[1]),
        device_id_type=MESH,
    ).wait_send()
    for t in range(STEPS):
        whole(rh.at[t], near_send.at[t], near_recv.at[t]).wait_send()
    whole(rf, near_send.at[STEPS], near_recv.at[STEPS]).wait_send()


def on_device(
    satellite_blocks, slot_source, slot_weight, slot_target, tile_counts,
    gate_input_weight, gate_state_weight, gate_bias, hidden_init, cell_init,
):
    slot = jnp.arange(8, dtype=jnp.int32)[:, None]
    targets = jnp.pad(slot_target[0].T, ((0, 4), (0, 0)))
    aim = jnp.where(slot < tile_counts, targets, -1).astype(F32)
    sources = jnp.repeat(peer_table(-1).reshape(CHUNKS, -1), SLOTS, axis=1)
    scale = jnp.where(jnp.arange(128) < 96, 0.5, 1.0).astype(F32)
    weight = jnp.concatenate([gate_state_weight, gate_input_weight], axis=1)
    weight = weight * scale.astype(BF16)[:, None]
    bias = jnp.broadcast_to((gate_bias * scale)[:, None], (128, COLS))
    vmem = pl.BlockSpec(memory_space=pltpu.VMEM)
    smem = pl.BlockSpec(memory_space=pltpu.SMEM)
    wide_row = (3 * HID, (ROWS + 2) * COLS)
    return pl.pallas_call(
        body,
        out_shape=[jax.ShapeDtypeStruct((HID, ROWS, COLS), BF16)] * 2,
        in_specs=[smem, smem] + [vmem] * 8,
        out_specs=[vmem, vmem],
        scratch_shapes=[
            pltpu.VMEM((PEERS, SLOTS, CH, 128), BF16),
            pltpu.VMEM((PEERS, SLOTS, CH, 128), BF16),
            pltpu.VMEM((PEERS // CHUNKS * SLOTS * CH, 128), F32),
            pltpu.VMEM((CH * 64, 128), F32),
            pltpu.VMEM((2, ROWS * HID, 128), F32),
            pltpu.VMEM((2, ROWS * HID, 128), F32),
            pltpu.VMEM(wide_row, BF16),
            pltpu.VMEM((2, ROWS * CH, 128), F32),
            pltpu.VMEM((3 * CH, (ROWS + 2) * COLS), BF16),
            pltpu.VMEM((2, ROWS * HID, 128), F32),
            pltpu.VMEM((STEPS, 6, HID, 128), BF16),
            pltpu.VMEM((STEPS, 14, HID, 128), BF16),
            pltpu.VMEM((6, CH, 128), BF16),
            pltpu.VMEM((14, CH, 128), BF16),
            pltpu.SemaphoreType.DMA,
            pltpu.SemaphoreType.DMA((CHUNKS,)),
            pltpu.SemaphoreType.DMA((STEPS + 1,)),
            pltpu.SemaphoreType.DMA((STEPS + 1,)),
        ],
        compiler_params=pltpu.CompilerParams(
            collective_id=0, has_side_effects=True, vmem_limit_bytes=60 * 2**20
        ),
        name="reproject_and_step",
    )(
        peer_table(1), slot_source.reshape(-1), satellite_blocks, slot_weight[0], aim, sources,
        weight, bias, hidden_init, cell_init,
    )


def solution(mesh):
    placed = (
        P(("lat", "lon"), None, None),
        P(("lat", "lon"), None, None),
        P(("lat", "lon"), None, None, None, None),
        P(("lat", "lon"), None, None),
        P(("lat", "lon"), None),
        P(),
        P(),
        P(),
        P(None, "lat", "lon"),
        P(None, "lat", "lon"),
    )
    return jax.shard_map(
        on_device,
        mesh=mesh,
        in_specs=placed,
        out_specs=(P(None, "lat", "lon"), P(None, "lat", "lon")),
        check_vma=False,
    )
```

```python
import itertools
import random

import jax
import jax.numpy as jnp
import numpy as np
from jax import lax
from jax.experimental import pallas as pl
from jax.experimental.pallas import tpu as pltpu
from jax.sharding import PartitionSpec as P

STEPS = 3
MESH = pl.DeviceIdType.MESH
F32 = jnp.float32
BF16 = jnp.bfloat16
PEERS = 128
SLOTS = 4
SIZES = (64, 32, 16, 16)
STARTS = (0, 64, 96, 112)
GROUP = 8
BARRIER_AT = 16
UNROLL = 2
ROWS = 32
COLS = 256
CH = 16
HID = 32


def send_order():
    offsets = [d for d in itertools.product(range(4), range(4), range(4), range(2)) if any(d)]
    random.Random(0).shuffle(offsets)
    return [(0, 0, 0, 0)] + offsets


ORDER = send_order()


def coords():
    i = lax.axis_index("lat")
    j = lax.axis_index("lon")
    return (lax.rem(lax.div(j, 2), 4), lax.div(i, 4) * 2 + lax.div(j, 8), lax.rem(i, 4), lax.rem(j, 2))


def device_at(x, y, z, c):
    return lax.div(y, 2) * 4 + z, lax.rem(y, 2) * 8 + x * 2 + c


class Places:
    def __init__(self):
        x, y, z, c = coords()
        self.x = [lax.rem(x + d, 4) * 2 for d in range(4)]
        ys = [lax.rem(y + d, 4) for d in range(4)]
        self.y_lat = [lax.div(v, 2) * 4 for v in ys]
        self.y_lon = [lax.rem(v, 2) * 8 for v in ys]
        self.z = [lax.rem(z + d, 4) for d in range(4)]
        self.c = [lax.rem(c + d, 2) for d in range(2)]

    def __call__(self, offset, sign=1):
        dx, dy, dz, dc = ((sign * d) % m for d, m in zip(offset, (4, 4, 4, 2)))
        return self.y_lat[dy] + self.z[dz], self.y_lon[dy] + self.x[dx] + self.c[dc]

    def index(self, offset, sign=1):
        lat, lon = self(offset, sign)
        return lat * 16 + lon


def lanes(shape):
    return lax.broadcasted_iota(jnp.int32, shape, len(shape) - 1)


def sublanes(shape):
    return lax.broadcasted_iota(jnp.int32, shape, len(shape) - 2)


def roll(x, shift):
    return pltpu.roll(x, shift, 1)


def band(n, to, to_index, tab, stab, x_ref, w_ref):
    tile = tab[n]
    lane = lanes((8, 128)) + sublanes((8, 128))
    inside = (lane >= 4) & (lane < 132)
    for s in range(SLOTS):
        x = x_ref[stab[0, s, tile]].astype(F32)
        w = jnp.where(inside, w_ref[tile, s].astype(F32), 0.0)
        total = w[4:5] * x
        for k in (0, 1, 2, 3, 5, 6, 7):
            total = total + w[k : k + 1] * roll(x, (4 - k) % 128)
        to[to_index, s] = total.astype(BF16)


def row_at(rows_ref, y, count):
    row = pl.ds(pl.multiple_of(y * count, count), count)
    return rows_ref[0, row], rows_ref[1, row]


def spread(halves, into, count, at):
    row = jnp.concatenate(halves, axis=1)
    where = pl.ds(at, COLS)
    into[0:count, where] = roll(row, 1).astype(BF16)
    into[count : 2 * count, where] = row.astype(BF16)
    into[2 * count : 3 * count, where] = roll(row, COLS - 1).astype(BF16)


def padded_at(y):
    return (y + 1) * COLS if isinstance(y, int) else pl.multiple_of((y + 1) * COLS, COLS)


class Picker:
    def __init__(self, left_lane, right_lane, count):
        self.left, self.right = left_lane, right_lane
        self.shape = (count, 128)

    def empty(self):
        return jnp.zeros(self.shape, F32), jnp.zeros(self.shape, F32)

    def take(self, state, halves):
        lane = lanes(self.shape)
        return (
            jnp.where(lane == self.left, halves[0], roll(state[0], 1)),
            jnp.where(lane == self.right, halves[1], roll(state[1], 1)),
        )

    def place(self, state):
        lane = lanes(self.shape)
        left = roll(state[0], (1 - self.left) % 128)
        right = roll(state[1], (65 - self.right) % 128)
        return jnp.where((lane >= 1) & (lane <= 32), left, jnp.where((lane >= 65) & (lane <= 96), right, 0.0))


def corners(edge, y, halves):
    lane = lanes(edge.shape)
    left = roll(edge, (-(y + 1)) % 128)
    right = roll(edge, (62 - y) % 128)
    return jnp.where(lane == 0, left, halves[0]), jnp.where(lane == 127, right, halves[1])


def stage(q_ref, top, bottom, edge, near):
    for k, v in enumerate((top[0], top[1], edge, near, bottom[0], bottom[1])):
        q_ref[k] = v.astype(BF16)


def swap(q_ref, r_ref, send_sem, recv_sem):
    i = lax.axis_index("lat")
    j = lax.axis_index("lon")
    up, down = lax.rem(i + 7, 8), lax.rem(i + 1, 8)
    left, right = lax.rem(j + 15, 16), lax.rem(j + 1, 16)
    plan = (
        ((up, j), 0, 4, 4),
        ((down, j), 2, 4, 0),
        ((i, left), 2, 1, 9),
        ((i, right), 2, 1, 8),
        ((up, left), 2, 1, 13),
        ((up, right), 2, 1, 12),
        ((down, left), 2, 1, 11),
        ((down, right), 2, 1, 10),
    )
    for target, source, size, slot in plan:
        pltpu.make_async_remote_copy(
            src_ref=q_ref.at[pl.ds(source, size)],
            dst_ref=r_ref.at[pl.ds(slot, size)],
            send_sem=send_sem,
            recv_sem=recv_sem,
            device_id=target,
            device_id_type=MESH,
        ).start()


def whole(r_ref, send_sem, recv_sem):
    i = lax.axis_index("lat")
    return pltpu.make_async_remote_copy(
        src_ref=r_ref,
        dst_ref=r_ref,
        send_sem=send_sem,
        recv_sem=recv_sem,
        device_id=(lax.rem(i + 1, 8), lax.axis_index("lon")),
        device_id_type=MESH,
    )


def edge_inputs(edge, near, r_ref, count):
    i = lax.axis_index("lat")
    lane = lanes((count, 128))
    half = lane < 64
    place = jnp.where(half, lane, lane - 64)
    top = (place == 0) & (i > 0)
    bottom = (place == 33) & (i < 7)
    middle = (place >= 1) & (place <= 32)
    got = lambda k: r_ref[k].astype(F32)

    def frame(mid, above, below):
        return jnp.where(middle, mid, jnp.where(top, above, jnp.where(bottom, below, 0.0)))

    edges = frame(edge, roll(got(0), 96), roll(got(6), 32))
    nears = frame(near, roll(got(1), 96), roll(got(7), 32))
    sides = frame(
        jnp.where(half, roll(got(8), 64), roll(got(9), 64)),
        jnp.where(half, roll(got(10), 32), roll(got(11), 32)),
        jnp.where(half, roll(got(12), 96), roll(got(13), 96)),
    )
    three = (jnp.where(half, sides, nears), edges, jnp.where(half, nears, sides))
    above = [roll(v, 1) for v in three]
    below = [roll(v, 127) for v in three]
    return jnp.concatenate([v.astype(BF16) for v in (*above, *three, *below)], axis=0)


def halo_rows(r_ref, into, count):
    i = lax.axis_index("lat")
    for slot, live, at in ((2, i > 0, 0), (4, i < 7, (ROWS + 1) * COLS)):
        halves = [jnp.where(live, r_ref[slot + k].astype(F32), 0.0) for k in range(2)]
        spread(halves, into, count, at)


def update(gates, memory):
    ingate = jnp.tanh(gates[0:HID]) * 0.5 + 0.5
    forget = jnp.tanh(gates[HID : 2 * HID]) * 0.5 + 0.5
    outgate = jnp.tanh(gates[2 * HID : 3 * HID]) * 0.5 + 0.5
    memory = forget * memory + ingate * jnp.tanh(gates[3 * HID :])
    return outgate * jnp.tanh(memory), memory


def halves_of(v):
    return v[:, :128], v[:, 128:]


def body(
    stab, x_hbm, w_hbm, target_ref, count_ref, state_ref, input_ref, bias_ref, hid_hbm, cell_hbm,
    hout_ref, cout_ref,
    tab, x_ref, w_ref, hid_ref, cell_ref, weight, out_buf, in_buf, wide, sums, rows, s0, s1, fshifted, cells,
    qh, rh, qf, rf, load_sem, far_send, far_recv, near_send, near_recv,
):
    loads = [
        pltpu.make_async_copy(a, b, load_sem.at[k])
        for k, (a, b) in enumerate(((x_hbm, x_ref), (w_hbm, w_ref), (hid_hbm, hid_ref), (cell_hbm, cell_ref)))
    ]
    for copy in loads:
        copy.start()
    at = Places()
    barrier = pltpu.get_barrier_semaphore()
    tab[0] = at.index(ORDER[0])
    for n in range(1, PEERS):
        pl.semaphore_signal(barrier, inc=1, device_id=at(ORDER[n]), device_id_type=MESH)
        tab[n] = at.index(ORDER[n])
    loads[0].wait()
    loads[1].wait()

    def one_band(n, carry):
        band(n, out_buf, n, tab, stab, x_ref, w_ref)
        return carry

    def send(first, last):
        for n in range(max(first, 1), last):
            chunk = max(k for k in range(len(SIZES)) if STARTS[k] <= n)
            pltpu.make_async_remote_copy(
                src_ref=out_buf.at[n],
                dst_ref=in_buf.at[n],
                send_sem=far_send,
                recv_sem=far_recv.at[chunk],
                device_id=at(ORDER[n]),
                device_id_type=MESH,
            ).start()

    band(0, in_buf, 0, tab, stab, x_ref, w_ref)
    lax.fori_loop(1, GROUP, one_band, 0)
    for first in range(GROUP, PEERS, GROUP):
        lax.fori_loop(first, first + GROUP, one_band, 0)
        if first == BARRIER_AT:
            pl.semaphore_wait(barrier, PEERS - 1)
            send(0, first)
        elif first > BARRIER_AT:
            send(first - GROUP, first)
    send(PEERS - GROUP, PEERS)

    loads[2].wait()
    for c in range(HID):
        for half in range(2):
            rows[half, pl.ds(c, ROWS, stride=HID), :] = hid_ref[c, :, half * 128 : half * 128 + 128].astype(F32)
    outer, inner = Picker(0, 127, HID), Picker(1, 126, HID)

    def prepare(k, state):
        y = ROWS - 1 - k
        halves = row_at(rows, y, HID)
        spread(halves, s0, HID, padded_at(y))
        return outer.take(state[0], halves), inner.take(state[1], halves)

    state = lax.fori_loop(0, ROWS, prepare, (outer.empty(), inner.empty()), unroll=2)
    edge, near = outer.place(state[0]), inner.place(state[1])
    stage(qh.at[0], row_at(rows, 0, HID), row_at(rows, ROWS - 1, HID), edge, near)
    loads[3].wait()
    for c in range(HID):
        for half in range(2):
            cells[half, pl.ds(c, ROWS, stride=HID), :] = cell_ref[c, :, half * 128 : half * 128 + 128].astype(F32)
    swap(qh.at[0], rh.at[0], near_send.at[0], near_recv.at[0])

    def prepare_cell(k, state):
        return outer.take(state, row_at(cells, ROWS - 1 - k, HID))

    edge_cell = outer.place(lax.fori_loop(0, ROWS, prepare_cell, outer.empty(), unroll=2))

    scale = jnp.where(sublanes((128, 1)) < 3 * HID, 0.5, 1.0)
    bias = jnp.sum(jnp.where(sublanes((128, 128)) == lanes((128, 128)), bias_ref[...], 0.0), axis=1, keepdims=True)
    bias = bias * scale
    high = bias.astype(BF16).astype(F32)
    middle = (bias - high).astype(BF16).astype(F32)
    low = bias - high - middle
    lane = lanes((128, 128))
    extra = jnp.where(lane == 0, high, jnp.where(lane == 1, middle, jnp.where(lane == 2, low, 0.0)))
    taps = jnp.concatenate([state_ref[...].astype(F32), input_ref[...].astype(F32), extra.T[:80]], axis=0)
    deep = lax.broadcasted_iota(jnp.int32, (128, 128), 1)
    for k in range(4):
        part = taps[k * 128 : k * 128 + 128].T
        mult = jnp.where((deep + k * 128 < 432), scale, 1.0)
        weight[:, k * 128 : k * 128 + 128] = (part * mult).astype(BF16)
    ones = jnp.ones((16, COLS), BF16)

    counts = count_ref[...]
    aim4 = jnp.where(sublanes((SLOTS, 128)) < counts, target_ref[0], -1).astype(F32)
    aim8 = jnp.concatenate([aim4, aim4], axis=0).astype(BF16)
    sums[...] = jnp.zeros_like(sums)
    for g, (start, size) in enumerate(zip(STARTS, SIZES)):
        taken = size * SLOTS
        first = max(start, 1)
        got = in_buf.at[pl.ds(first, start + size - first)]
        pltpu.make_async_remote_copy(
            src_ref=got, dst_ref=got, send_sem=far_send, recv_sem=far_recv.at[g],
            device_id=at(ORDER[1]), device_id_type=MESH,
        ).wait_recv()

        def unpack(n, carry):
            block = in_buf[start + n].astype(F32).reshape(SLOTS * CH, 128)
            wide[pl.ds(pl.multiple_of(n * SLOTS * CH, SLOTS * CH), SLOTS * CH)] = block
            return carry

        lax.fori_loop(0, size, unpack, 0, unroll=4)
        which = lax.shift_right_logical(lanes((1, taken)), 2)
        origin = jnp.zeros((1, taken), jnp.int32)
        for n in range(size):
            origin = jnp.where(which == n, at.index(ORDER[start + n], -1), origin)
        spot = (sublanes((128, taken)) == origin).astype(F32).astype(BF16)
        aims = jnp.dot(aim8, spot, preferred_element_type=F32)
        mine = sublanes((8, taken)) == lanes((8, taken)) % SLOTS
        aim = jnp.sum(jnp.where(mine, aims, 0.0), axis=0, keepdims=True)
        chosen = (sublanes((64, taken)).astype(F32) == aim).astype(F32).astype(BF16)
        for c in range(0, CH, 2):
            pair = [wide[pl.ds(c + k, taken, stride=CH), :].astype(BF16) for k in range(2)]
            part = jnp.dot(chosen, jnp.concatenate(pair, axis=1), preferred_element_type=F32)
            sums[c * 64 : c * 64 + 64] += part[:, :128]
            sums[c * 64 + 64 : c * 64 + 128] += part[:, 128:]

    fouter, finner = Picker(0, 127, CH), Picker(1, 126, CH)

    def cell_row(y):
        return sums[pl.ds(2 * y, CH, stride=64), :], sums[pl.ds(2 * y + 1, CH, stride=64), :]

    def fill(k, state):
        y = ROWS - 1 - k
        halves = cell_row(y)
        spread(halves, fshifted, CH, padded_at(y))
        return fouter.take(state[0], halves), finner.take(state[1], halves)

    state = lax.fori_loop(0, ROWS, fill, (fouter.empty(), finner.empty()), unroll=2)
    fedge, fnear = fouter.place(state[0]), finner.place(state[1])
    stage(qf, cell_row(0), cell_row(ROWS - 1), fedge, fnear)
    swap(qf, rf, near_send.at[STEPS], near_recv.at[STEPS])

    fmini = None
    for t in range(STEPS):
        here, there = (s0, s1) if t % 2 == 0 else (s1, s0)
        last = t == STEPS - 1

        def one_row(y):
            spans = [pl.ds(padded_at(y - 1 + a), COLS) for a in range(3)]
            rhs = jnp.concatenate([here[:, w] for w in spans] + [fshifted[:, w] for w in spans] + [ones], axis=0)
            gates = jnp.dot(weight[:, :448], rhs, preferred_element_type=F32)
            hidden, memory = update(gates, jnp.concatenate(row_at(cells, y, HID), axis=1))
            halves = halves_of(hidden)
            where = pl.ds(pl.multiple_of(y * HID, HID), HID)
            for half, v in enumerate(halves_of(memory)):
                cells[half, where] = v
            if last:
                for half, v in enumerate(halves):
                    rows[half, where] = v
            else:
                spread(halves, there, HID, padded_at(y))
            return halves

        def inside(k, state):
            halves = one_row(ROWS - 2 - k)
            return state if last else inner.take(state, halves)

        state = lax.fori_loop(0, ROWS - 2, inside, 0 if last else inner.empty(), unroll=UNROLL)

        whole(rh.at[t], near_send.at[t], near_recv.at[t]).wait_recv()
        if t == 0:
            whole(rf, near_send.at[STEPS], near_recv.at[STEPS]).wait_recv()
            fmini = edge_inputs(fedge, fnear, rf, CH)
            halo_rows(rf, fshifted, CH)
        mini = jnp.concatenate([edge_inputs(edge, near, rh.at[t], HID), fmini, ones[:, :128]], axis=0)
        halo_rows(rh.at[t], here, HID)
        gates = jnp.dot(weight[:, :448], mini, preferred_element_type=F32)
        edge, edge_cell = update(gates, edge_cell)
        top = one_row(0)
        bottom = one_row(ROWS - 1)
        if last:
            break
        state = inner.take(state, top)
        far_left = roll(bottom[0], 31)
        far_right = roll(bottom[1], (96 - 126) % 128)
        spot = lanes((HID, 128))
        near = jnp.where(spot == 32, far_left, jnp.where(spot == 96, far_right, inner.place(state)))
        stage(qh.at[t + 1], corners(edge, 0, top), corners(edge, ROWS - 1, bottom), edge, near)
        swap(qh.at[t + 1], rh.at[t + 1], near_send.at[t + 1], near_recv.at[t + 1])

        def mend(y, state):
            v, u = state
            v_next, u_next = roll(v, 127), roll(u, 127)
            lane = lanes((HID, 128))
            first = pl.ds(padded_at(y), 128)
            second = pl.ds(pl.multiple_of((y + 1) * COLS + 128, 128), 128)
            for block, where, spot, value in (
                (0, first, 1, v), (1, first, 0, v_next), (1, second, 127, u), (2, second, 126, u_next),
            ):
                part = there.at[block * HID : block * HID + HID, where]
                part[...] = jnp.where(lane == spot, value, part[...].astype(F32)).astype(BF16)
            return v_next, u_next

        lax.fori_loop(0, ROWS, mend, (edge, roll(edge, 62)), unroll=4)

    def finish(y, state):
        v, u, vc, uc = state
        lane = lanes((HID, 128))
        for source, a, b, to in ((rows, v, u, hout_ref), (cells, vc, uc, cout_ref)):
            one, two = row_at(source, y, HID)
            to[y, :, :128] = jnp.where(lane == 0, a, one).astype(BF16)
            to[y, :, 128:] = jnp.where(lane == 127, b, two).astype(BF16)
        return tuple(roll(x, 127) for x in state)

    lax.fori_loop(
        0, ROWS, finish, (roll(edge, 127), roll(edge, 62), roll(edge_cell, 127), roll(edge_cell, 62)), unroll=4
    )

    sent = out_buf.at[pl.ds(1, PEERS - 1)]
    pltpu.make_async_remote_copy(
        src_ref=sent, dst_ref=sent, send_sem=far_send, recv_sem=far_recv.at[0],
        device_id=at(ORDER[1]), device_id_type=MESH,
    ).wait_send()
    for t in range(STEPS):
        whole(rh.at[t], near_send.at[t], near_recv.at[t]).wait_send()
    whole(rf, near_send.at[STEPS], near_recv.at[STEPS]).wait_send()


def on_device(
    satellite_blocks, slot_source, slot_weight, slot_target, tile_counts,
    gate_input_weight, gate_state_weight, gate_bias, hidden_init, cell_init,
):
    vmem = pl.BlockSpec(memory_space=pltpu.VMEM)
    smem = pl.BlockSpec(memory_space=pltpu.SMEM)
    hbm = pl.BlockSpec(memory_space=pl.ANY)
    padded = (ROWS + 2) * COLS
    hidden, memory = pl.pallas_call(
        body,
        out_shape=[jax.ShapeDtypeStruct((ROWS, HID, COLS), BF16)] * 2,
        in_specs=[smem, hbm, hbm] + [vmem] * 5 + [hbm, hbm],
        out_specs=[vmem, vmem],
        scratch_shapes=[
            pltpu.SMEM((PEERS,), jnp.int32),
            pltpu.VMEM((PEERS, CH, 128), BF16),
            pltpu.VMEM((PEERS, SLOTS, 8, 128), BF16),
            pltpu.VMEM((HID, ROWS, COLS), BF16),
            pltpu.VMEM((HID, ROWS, COLS), BF16),
            pltpu.VMEM((128, 512), BF16),
            pltpu.VMEM((PEERS, SLOTS, CH, 128), BF16),
            pltpu.VMEM((PEERS, SLOTS, CH, 128), BF16),
            pltpu.VMEM((max(SIZES) * SLOTS * CH, 128), F32),
            pltpu.VMEM((CH * 64, 128), F32),
            pltpu.VMEM((2, ROWS * HID, 128), F32),
            pltpu.VMEM((3 * HID, padded), BF16),
            pltpu.VMEM((3 * HID, padded), BF16),
            pltpu.VMEM((3 * CH, padded), BF16),
            pltpu.VMEM((2, ROWS * HID, 128), F32),
            pltpu.VMEM((STEPS, 6, HID, 128), BF16),
            pltpu.VMEM((STEPS, 14, HID, 128), BF16),
            pltpu.VMEM((6, CH, 128), BF16),
            pltpu.VMEM((14, CH, 128), BF16),
            pltpu.SemaphoreType.DMA((4,)),
            pltpu.SemaphoreType.DMA,
            pltpu.SemaphoreType.DMA((len(SIZES),)),
            pltpu.SemaphoreType.DMA((STEPS + 1,)),
            pltpu.SemaphoreType.DMA((STEPS + 1,)),
        ],
        compiler_params=pltpu.CompilerParams(
            collective_id=0, has_side_effects=True, vmem_limit_bytes=60 * 2**20
        ),
        name="reproject_and_step",
    )(
        slot_source.transpose(0, 2, 1), satellite_blocks, slot_weight[0], slot_target.transpose(0, 2, 1), tile_counts,
        gate_state_weight.T, gate_input_weight.T, gate_bias.reshape(1, -1), hidden_init, cell_init,
    )
    return hidden.transpose(1, 0, 2), memory.transpose(1, 0, 2)


def solution(mesh):
    placed = (
        P(("lat", "lon"), None, None),
        P(("lat", "lon"), None, None),
        P(("lat", "lon"), None, None, None, None),
        P(("lat", "lon"), None, None),
        P(("lat", "lon"), None),
        P(),
        P(),
        P(),
        P(None, "lat", "lon"),
        P(None, "lat", "lon"),
    )
    return jax.shard_map(
        on_device,
        mesh=mesh,
        in_specs=placed,
        out_specs=(P(None, "lat", "lon"), P(None, "lat", "lon")),
        check_vma=False,
    )
```

```python
import itertools
import random

import jax
import jax.numpy as jnp
import numpy as np
from jax import lax
from jax.experimental import pallas as pl
from jax.experimental.pallas import tpu as pltpu
from jax.sharding import PartitionSpec as P

STEPS = 3
MESH = pl.DeviceIdType.MESH
F32 = jnp.float32
BF16 = jnp.bfloat16
PEERS = 128
SLOTS = 4
SIZES = (64, 32, 16, 16)
STARTS = (0, 64, 96, 112)
GROUP = 8
BARRIER_AT = 16
BLOCK = 5
ROWS = 32
COLS = 256
CH = 16
HID = 32


def send_order():
    offsets = [d for d in itertools.product(range(4), range(4), range(4), range(2)) if any(d)]
    random.Random(0).shuffle(offsets)
    return [(0, 0, 0, 0)] + offsets


ORDER = send_order()


def coords():
    i = lax.axis_index("lat")
    j = lax.axis_index("lon")
    return (lax.rem(lax.div(j, 2), 4), lax.div(i, 4) * 2 + lax.div(j, 8), lax.rem(i, 4), lax.rem(j, 2))


def device_at(x, y, z, c):
    return lax.div(y, 2) * 4 + z, lax.rem(y, 2) * 8 + x * 2 + c


class Places:
    def __init__(self):
        x, y, z, c = coords()
        self.x = [lax.rem(x + d, 4) * 2 for d in range(4)]
        ys = [lax.rem(y + d, 4) for d in range(4)]
        self.y_lat = [lax.div(v, 2) * 4 for v in ys]
        self.y_lon = [lax.rem(v, 2) * 8 for v in ys]
        self.z = [lax.rem(z + d, 4) for d in range(4)]
        self.c = [lax.rem(c + d, 2) for d in range(2)]

    def __call__(self, offset, sign=1):
        dx, dy, dz, dc = ((sign * d) % m for d, m in zip(offset, (4, 4, 4, 2)))
        return self.y_lat[dy] + self.z[dz], self.y_lon[dy] + self.x[dx] + self.c[dc]

    def index(self, offset, sign=1):
        lat, lon = self(offset, sign)
        return lat * 16 + lon


def lanes(shape):
    return lax.broadcasted_iota(jnp.int32, shape, len(shape) - 1)


def sublanes(shape):
    return lax.broadcasted_iota(jnp.int32, shape, len(shape) - 2)


def roll(x, shift):
    return pltpu.roll(x, shift, 1)


def band(n, to, to_index, tab, stab, x_ref, w_ref):
    tile = tab[n]
    lane = lanes((8, 128)) + sublanes((8, 128))
    inside = (lane >= 4) & (lane < 132)
    for s in range(SLOTS):
        x = x_ref[stab[0, s, tile]].astype(F32)
        w = jnp.where(inside, w_ref[tile, s].astype(F32), 0.0)
        total = w[4:5] * x
        for k in (0, 1, 2, 3, 5, 6, 7):
            total = total + w[k : k + 1] * roll(x, (4 - k) % 128)
        to[to_index, s] = total.astype(BF16)


def row_at(rows_ref, y, count):
    row = pl.ds(pl.multiple_of(y * count, count), count)
    return rows_ref[0, row], rows_ref[1, row]


def spread(halves, into, count, at):
    row = jnp.concatenate(halves, axis=1)
    where = pl.ds(at, COLS)
    into[0:count, where] = roll(row, 1).astype(BF16)
    into[count : 2 * count, where] = row.astype(BF16)
    into[2 * count : 3 * count, where] = roll(row, COLS - 1).astype(BF16)


def padded_at(y):
    return (y + 1) * COLS if isinstance(y, int) else pl.multiple_of((y + 1) * COLS, COLS)


class Picker:
    def __init__(self, left_lane, right_lane, count):
        self.left, self.right = left_lane, right_lane
        self.shape = (count, 128)

    def empty(self):
        return jnp.zeros(self.shape, F32), jnp.zeros(self.shape, F32)

    def take(self, state, halves):
        lane = lanes(self.shape)
        return (
            jnp.where(lane == self.left, halves[0], roll(state[0], 1)),
            jnp.where(lane == self.right, halves[1], roll(state[1], 1)),
        )

    def place(self, state):
        lane = lanes(self.shape)
        left = roll(state[0], (1 - self.left) % 128)
        right = roll(state[1], (65 - self.right) % 128)
        return jnp.where((lane >= 1) & (lane <= 32), left, jnp.where((lane >= 65) & (lane <= 96), right, 0.0))


def corners(edge, y, halves):
    lane = lanes(edge.shape)
    left = roll(edge, (-(y + 1)) % 128)
    right = roll(edge, (62 - y) % 128)
    return jnp.where(lane == 0, left, halves[0]), jnp.where(lane == 127, right, halves[1])


def stage(q_ref, top, bottom, edge, near):
    for k, v in enumerate((top[0], top[1], edge, near, bottom[0], bottom[1])):
        q_ref[k] = v.astype(BF16)


def swap(q_ref, r_ref, send_sem, recv_sem):
    i = lax.axis_index("lat")
    j = lax.axis_index("lon")
    up, down = lax.rem(i + 7, 8), lax.rem(i + 1, 8)
    left, right = lax.rem(j + 15, 16), lax.rem(j + 1, 16)
    plan = (
        ((up, j), 0, 4, 4),
        ((down, j), 2, 4, 0),
        ((i, left), 2, 1, 9),
        ((i, right), 2, 1, 8),
        ((up, left), 2, 1, 13),
        ((up, right), 2, 1, 12),
        ((down, left), 2, 1, 11),
        ((down, right), 2, 1, 10),
    )
    for target, source, size, slot in plan:
        pltpu.make_async_remote_copy(
            src_ref=q_ref.at[pl.ds(source, size)],
            dst_ref=r_ref.at[pl.ds(slot, size)],
            send_sem=send_sem,
            recv_sem=recv_sem,
            device_id=target,
            device_id_type=MESH,
        ).start()


def whole(r_ref, send_sem, recv_sem):
    i = lax.axis_index("lat")
    return pltpu.make_async_remote_copy(
        src_ref=r_ref,
        dst_ref=r_ref,
        send_sem=send_sem,
        recv_sem=recv_sem,
        device_id=(lax.rem(i + 1, 8), lax.axis_index("lon")),
        device_id_type=MESH,
    )


def edge_inputs(edge, near, r_ref, count):
    i = lax.axis_index("lat")
    lane = lanes((count, 128))
    half = lane < 64
    place = jnp.where(half, lane, lane - 64)
    top = (place == 0) & (i > 0)
    bottom = (place == 33) & (i < 7)
    middle = (place >= 1) & (place <= 32)
    got = lambda k: r_ref[k].astype(F32)

    def frame(mid, above, below):
        return jnp.where(middle, mid, jnp.where(top, above, jnp.where(bottom, below, 0.0)))

    edges = frame(edge, roll(got(0), 96), roll(got(6), 32))
    nears = frame(near, roll(got(1), 96), roll(got(7), 32))
    sides = frame(
        jnp.where(half, roll(got(8), 64), roll(got(9), 64)),
        jnp.where(half, roll(got(10), 32), roll(got(11), 32)),
        jnp.where(half, roll(got(12), 96), roll(got(13), 96)),
    )
    three = (jnp.where(half, sides, nears), edges, jnp.where(half, nears, sides))
    above = [roll(v, 1) for v in three]
    below = [roll(v, 127) for v in three]
    return jnp.concatenate([v.astype(BF16) for v in (*above, *three, *below)], axis=0)


def halo_rows(r_ref, into, count):
    i = lax.axis_index("lat")
    for slot, live, at in ((2, i > 0, 0), (4, i < 7, (ROWS + 1) * COLS)):
        halves = [jnp.where(live, r_ref[slot + k].astype(F32), 0.0) for k in range(2)]
        spread(halves, into, count, at)


def update(gates, memory):
    ingate = jnp.tanh(gates[0:HID]) * 0.5 + 0.5
    forget = jnp.tanh(gates[HID : 2 * HID]) * 0.5 + 0.5
    outgate = jnp.tanh(gates[2 * HID : 3 * HID]) * 0.5 + 0.5
    memory = forget * memory + ingate * jnp.tanh(gates[3 * HID :])
    return outgate * jnp.tanh(memory), memory


def halves_of(v):
    return v[:, :128], v[:, 128:]


def body(
    stab, x_hbm, w_hbm, target_ref, count_ref, state_ref, input_ref, bias_ref, hid_hbm, cell_hbm,
    hout_ref, cout_ref,
    tab, x_ref, w_ref, hid_ref, cell_ref, weight, out_buf, in_buf, wide, sums, rows, s0, s1, fshifted, cells, ga, gb,
    qh, rh, qf, rf, load_sem, far_send, far_recv, near_send, near_recv,
):
    loads = [
        pltpu.make_async_copy(a, b, load_sem.at[k])
        for k, (a, b) in enumerate(((x_hbm, x_ref), (w_hbm, w_ref), (hid_hbm, hid_ref), (cell_hbm, cell_ref)))
    ]
    for copy in loads:
        copy.start()
    at = Places()
    barrier = pltpu.get_barrier_semaphore()
    tab[0] = at.index(ORDER[0])
    for offset in sorted(ORDER[1:], key=lambda d: -sum(min(a, 4 - a) for a in d[:3])):
        pl.semaphore_signal(barrier, inc=1, device_id=at(offset), device_id_type=MESH)
    for n in range(1, PEERS):
        tab[n] = at.index(ORDER[n])
    loads[0].wait()
    loads[1].wait()

    def one_band(n, carry):
        band(n, out_buf, n, tab, stab, x_ref, w_ref)
        return carry

    def send(first, last):
        for n in range(max(first, 1), last):
            chunk = max(k for k in range(len(SIZES)) if STARTS[k] <= n)
            pltpu.make_async_remote_copy(
                src_ref=out_buf.at[n],
                dst_ref=in_buf.at[n],
                send_sem=far_send,
                recv_sem=far_recv.at[chunk],
                device_id=at(ORDER[n]),
                device_id_type=MESH,
            ).start()

    band(0, in_buf, 0, tab, stab, x_ref, w_ref)
    lax.fori_loop(1, GROUP, one_band, 0)
    for first in range(GROUP, PEERS, GROUP):
        lax.fori_loop(first, first + GROUP, one_band, 0)
        if first == BARRIER_AT:
            pl.semaphore_wait(barrier, PEERS - 1)
            send(0, first)
        elif first > BARRIER_AT:
            send(first - GROUP, first)
    send(PEERS - GROUP, PEERS)

    loads[2].wait()
    for c in range(HID):
        for half in range(2):
            rows[half, pl.ds(c, ROWS, stride=HID), :] = hid_ref[c, :, half * 128 : half * 128 + 128].astype(F32)
    outer, inner = Picker(0, 127, HID), Picker(1, 126, HID)

    def prepare(k, state):
        y = ROWS - 1 - k
        halves = row_at(rows, y, HID)
        spread(halves, s0, HID, padded_at(y))
        return outer.take(state[0], halves), inner.take(state[1], halves)

    state = lax.fori_loop(0, ROWS, prepare, (outer.empty(), inner.empty()), unroll=2)
    edge, near = outer.place(state[0]), inner.place(state[1])
    stage(qh.at[0], row_at(rows, 0, HID), row_at(rows, ROWS - 1, HID), edge, near)
    loads[3].wait()
    for c in range(HID):
        for half in range(2):
            cells[half, pl.ds(c, ROWS, stride=HID), :] = cell_ref[c, :, half * 128 : half * 128 + 128].astype(F32)
    swap(qh.at[0], rh.at[0], near_send.at[0], near_recv.at[0])

    def prepare_cell(k, state):
        return outer.take(state, row_at(cells, ROWS - 1 - k, HID))

    edge_cell = outer.place(lax.fori_loop(0, ROWS, prepare_cell, outer.empty(), unroll=2))

    scale = jnp.where(sublanes((128, 1)) < 3 * HID, 0.5, 1.0)
    bias = jnp.sum(jnp.where(sublanes((128, 128)) == lanes((128, 128)), bias_ref[...], 0.0), axis=1, keepdims=True)
    bias = bias * scale
    high = bias.astype(BF16).astype(F32)
    middle = (bias - high).astype(BF16).astype(F32)
    low = bias - high - middle
    lane = lanes((128, 128))
    extra = jnp.where(lane == 0, high, jnp.where(lane == 1, middle, jnp.where(lane == 2, low, 0.0)))
    taps = jnp.concatenate([state_ref[...].astype(F32), input_ref[...].astype(F32), extra.T[:80]], axis=0)
    deep = lax.broadcasted_iota(jnp.int32, (128, 128), 1)
    for k in range(4):
        part = taps[k * 128 : k * 128 + 128].T
        mult = jnp.where((deep + k * 128 < 432), scale, 1.0)
        weight[:, k * 128 : k * 128 + 128] = (part * mult).astype(BF16)
    ones = jnp.ones((16, COLS), BF16)

    counts = count_ref[...]
    aim4 = jnp.where(sublanes((SLOTS, 128)) < counts, target_ref[0], -1).astype(F32)
    aim8 = jnp.concatenate([aim4, aim4], axis=0).astype(BF16)
    sums[...] = jnp.zeros_like(sums)
    for g, (start, size) in enumerate(zip(STARTS, SIZES)):
        taken = size * SLOTS
        first = max(start, 1)
        got = in_buf.at[pl.ds(first, start + size - first)]
        pltpu.make_async_remote_copy(
            src_ref=got, dst_ref=got, send_sem=far_send, recv_sem=far_recv.at[g],
            device_id=at(ORDER[1]), device_id_type=MESH,
        ).wait_recv()

        def unpack(n, carry):
            block = in_buf[start + n].astype(F32).reshape(SLOTS * CH, 128)
            wide[pl.ds(pl.multiple_of(n * SLOTS * CH, SLOTS * CH), SLOTS * CH)] = block
            return carry

        lax.fori_loop(0, size, unpack, 0, unroll=4)
        which = lax.shift_right_logical(lanes((1, taken)), 2)
        origin = jnp.zeros((1, taken), jnp.int32)
        for n in range(size):
            origin = jnp.where(which == n, at.index(ORDER[start + n], -1), origin)
        spot = (sublanes((128, taken)) == origin).astype(F32).astype(BF16)
        aims = jnp.dot(aim8, spot, preferred_element_type=F32)
        mine = sublanes((8, taken)) == lanes((8, taken)) % SLOTS
        aim = jnp.sum(jnp.where(mine, aims, 0.0), axis=0, keepdims=True)
        chosen = (sublanes((64, taken)).astype(F32) == aim).astype(F32).astype(BF16)
        for c in range(0, CH, 2):
            pair = [wide[pl.ds(c + k, taken, stride=CH), :].astype(BF16) for k in range(2)]
            part = jnp.dot(chosen, jnp.concatenate(pair, axis=1), preferred_element_type=F32)
            sums[c * 64 : c * 64 + 64] += part[:, :128]
            sums[c * 64 + 64 : c * 64 + 128] += part[:, 128:]

    def cell_row(y):
        return sums[pl.ds(2 * y, CH, stride=64), :], sums[pl.ds(2 * y + 1, CH, stride=64), :]

    spot = lanes((CH, 128))
    fedge = fnear = jnp.zeros((CH, 128), F32)
    for y in range(ROWS):
        halves = cell_row(y)
        spread(halves, fshifted, CH, padded_at(y))
        fedge = jnp.where(spot == y + 1, roll(halves[0], y + 1), fedge)
        fedge = jnp.where(spot == y + 65, roll(halves[1], (y + 66) % 128), fedge)
        fnear = jnp.where(spot == y + 1, roll(halves[0], y), fnear)
        fnear = jnp.where(spot == y + 65, roll(halves[1], (y + 67) % 128), fnear)
    stage(qf, cell_row(0), cell_row(ROWS - 1), fedge, fnear)
    swap(qf, rf, near_send.at[STEPS], near_recv.at[STEPS])

    fmini = None
    for t in range(STEPS):
        here, there = (s0, s1) if t % 2 == 0 else (s1, s0)
        last = t == STEPS - 1

        def gates_of(y, count=1):
            spans = [pl.ds(padded_at(y - 1 + a), COLS * count) for a in range(3)]
            fixed = jnp.ones((16, COLS * count), BF16)
            rhs = jnp.concatenate([here[:, w] for w in spans] + [fshifted[:, w] for w in spans] + [fixed], axis=0)
            return jnp.dot(weight[:, :448], rhs, preferred_element_type=F32)

        def finish_row(y, gates):
            hidden, memory = update(gates, jnp.concatenate(row_at(cells, y, HID), axis=1))
            halves = halves_of(hidden)
            where = pl.ds(pl.multiple_of(y * HID, HID), HID)
            for half, v in enumerate(halves_of(memory)):
                cells[half, where] = v
            if last:
                for half, v in enumerate(halves):
                    rows[half, where] = v
            else:
                spread(halves, there, HID, padded_at(y))
            return halves

        def block(low, buffer, state):
            for r in range(BLOCK - 1, -1, -1):
                halves = finish_row(low + r, buffer[:, r * COLS : r * COLS + COLS])
                state = state if last else inner.take(state, halves)
            return state

        def inside(k, state):
            low = ROWS - 1 - BLOCK - 2 * BLOCK * k
            gb[...] = gates_of(low - BLOCK, BLOCK)
            state = block(low, ga, state)
            ga[...] = gates_of(lax.max(low - 2 * BLOCK, 1), BLOCK)
            return block(low - BLOCK, gb, state)

        ga[...] = gates_of(ROWS - 1 - BLOCK, BLOCK)
        state = 0 if last else inner.empty()
        state = lax.fori_loop(0, (ROWS - 2) // (2 * BLOCK), inside, state)

        whole(rh.at[t], near_send.at[t], near_recv.at[t]).wait_recv()
        if t == 0:
            whole(rf, near_send.at[STEPS], near_recv.at[STEPS]).wait_recv()
            fmini = edge_inputs(fedge, fnear, rf, CH)
            halo_rows(rf, fshifted, CH)
        mini = jnp.concatenate([edge_inputs(edge, near, rh.at[t], HID), fmini, ones[:, :128]], axis=0)
        halo_rows(rh.at[t], here, HID)
        gates = jnp.dot(weight[:, :448], mini, preferred_element_type=F32)
        edge, edge_cell = update(gates, edge_cell)
        tops, bottoms = gates_of(0), gates_of(ROWS - 1)
        top = finish_row(0, tops)
        bottom = finish_row(ROWS - 1, bottoms)
        if last:
            break
        state = inner.take(state, top)
        far_left = roll(bottom[0], 31)
        far_right = roll(bottom[1], (96 - 126) % 128)
        spot = lanes((HID, 128))
        near = jnp.where(spot == 32, far_left, jnp.where(spot == 96, far_right, inner.place(state)))
        stage(qh.at[t + 1], corners(edge, 0, top), corners(edge, ROWS - 1, bottom), edge, near)
        swap(qh.at[t + 1], rh.at[t + 1], near_send.at[t + 1], near_recv.at[t + 1])

        lane = lanes((HID, 128))
        left = [roll(edge, -y % 128).astype(BF16) for y in range(ROWS + 1)]
        right = [roll(edge, (62 - y) % 128).astype(BF16) for y in range(ROWS + 1)]
        for y in range(ROWS):
            first = pl.ds((y + 1) * COLS, 128)
            second = pl.ds((y + 1) * COLS + 128, 128)
            for block_at, where, spot, value in (
                (0, first, 1, left[y]), (1, first, 0, left[y + 1]),
                (1, second, 127, right[y]), (2, second, 126, right[y + 1]),
            ):
                part = there.at[block_at * HID : block_at * HID + HID, where]
                part[...] = jnp.where(lane == spot, value, part[...])

    for source, columns, to in ((rows, edge, hout_ref), (cells, edge_cell, cout_ref)):
        for y in range(ROWS):
            one, two = corners(columns, y, row_at(source, y, HID))
            to[y, :, :128] = one.astype(BF16)
            to[y, :, 128:] = two.astype(BF16)

    sent = out_buf.at[pl.ds(1, PEERS - 1)]
    pltpu.make_async_remote_copy(
        src_ref=sent, dst_ref=sent, send_sem=far_send, recv_sem=far_recv.at[0],
        device_id=at(ORDER[1]), device_id_type=MESH,
    ).wait_send()
    for t in range(STEPS):
        whole(rh.at[t], near_send.at[t], near_recv.at[t]).wait_send()
    whole(rf, near_send.at[STEPS], near_recv.at[STEPS]).wait_send()


def on_device(
    satellite_blocks, slot_source, slot_weight, slot_target, tile_counts,
    gate_input_weight, gate_state_weight, gate_bias, hidden_init, cell_init,
):
    vmem = pl.BlockSpec(memory_space=pltpu.VMEM)
    smem = pl.BlockSpec(memory_space=pltpu.SMEM)
    hbm = pl.BlockSpec(memory_space=pltpu.HBM)
    padded = (ROWS + 2) * COLS
    hidden, memory = pl.pallas_call(
        body,
        out_shape=[jax.ShapeDtypeStruct((ROWS, HID, COLS), BF16)] * 2,
        in_specs=[smem, hbm, hbm] + [vmem] * 5 + [hbm, hbm],
        out_specs=[vmem, vmem],
        scratch_shapes=[
            pltpu.SMEM((PEERS,), jnp.int32),
            pltpu.VMEM((PEERS, CH, 128), BF16),
            pltpu.VMEM((PEERS, SLOTS, 8, 128), BF16),
            pltpu.VMEM((HID, ROWS, COLS), BF16),
            pltpu.VMEM((HID, ROWS, COLS), BF16),
            pltpu.VMEM((128, 512), BF16),
            pltpu.VMEM((PEERS, SLOTS, CH, 128), BF16),
            pltpu.VMEM((PEERS, SLOTS, CH, 128), BF16),
            pltpu.VMEM((max(SIZES) * SLOTS * CH, 128), F32),
            pltpu.VMEM((CH * 64, 128), F32),
            pltpu.VMEM((2, ROWS * HID, 128), F32),
            pltpu.VMEM((3 * HID, padded), BF16),
            pltpu.VMEM((3 * HID, padded), BF16),
            pltpu.VMEM((3 * CH, padded), BF16),
            pltpu.VMEM((2, ROWS * HID, 128), F32),
            pltpu.VMEM((128, COLS * BLOCK), F32),
            pltpu.VMEM((128, COLS * BLOCK), F32),
            pltpu.VMEM((STEPS, 6, HID, 128), BF16),
            pltpu.VMEM((STEPS, 14, HID, 128), BF16),
            pltpu.VMEM((6, CH, 128), BF16),
            pltpu.VMEM((14, CH, 128), BF16),
            pltpu.SemaphoreType.DMA((4,)),
            pltpu.SemaphoreType.DMA,
            pltpu.SemaphoreType.DMA((len(SIZES),)),
            pltpu.SemaphoreType.DMA((STEPS + 1,)),
            pltpu.SemaphoreType.DMA((STEPS + 1,)),
        ],
        compiler_params=pltpu.CompilerParams(
            collective_id=0, has_side_effects=True, vmem_limit_bytes=30 * 2**20
        ),
        name="reproject_and_step",
    )(
        slot_source.transpose(0, 2, 1), satellite_blocks, slot_weight[0], slot_target.transpose(0, 2, 1), tile_counts,
        gate_state_weight.T, gate_input_weight.T, gate_bias.reshape(1, -1), hidden_init, cell_init,
    )
    return hidden.transpose(1, 0, 2), memory.transpose(1, 0, 2)


def solution(mesh):
    placed = (
        P(("lat", "lon"), None, None),
        P(("lat", "lon"), None, None),
        P(("lat", "lon"), None, None, None, None),
        P(("lat", "lon"), None, None),
        P(("lat", "lon"), None),
        P(),
        P(),
        P(),
        P(None, "lat", "lon"),
        P(None, "lat", "lon"),
    )
    return jax.shard_map(
        on_device,
        mesh=mesh,
        in_specs=placed,
        out_specs=(P(None, "lat", "lon"), P(None, "lat", "lon")),
        check_vma=False,
    )
```

```python
import itertools
import random

import jax
import jax.numpy as jnp
import numpy as np
from jax import lax
from jax.experimental import pallas as pl
from jax.experimental.pallas import tpu as pltpu
from jax.sharding import PartitionSpec as P

STEPS = 3
MESH = pl.DeviceIdType.MESH
LOGICAL = pl.DeviceIdType.LOGICAL
F32 = jnp.float32
BF16 = jnp.bfloat16
PEERS = 128
SLOTS = 4
SIZES = (64, 32, 16, 16)
STARTS = (0, 64, 96, 112)
GROUP = 8
BARRIER_AT = 16
BLOCK = 5
ROWS = 32
COLS = 256
CH = 16
HID = 32


def send_order():
    offsets = [d for d in itertools.product(range(4), range(4), range(4), range(2)) if any(d)]
    random.Random(0).shuffle(offsets)
    return [(0, 0, 0, 0)] + offsets


ORDER = send_order()


def coords():
    i = lax.axis_index("lat")
    j = lax.axis_index("lon")
    return (lax.rem(lax.div(j, 2), 4), lax.div(i, 4) * 2 + lax.div(j, 8), lax.rem(i, 4), lax.rem(j, 2))


class Places:
    def __init__(self):
        x, y, z, c = coords()
        ys = [lax.rem(y + d, 4) for d in range(4)]
        self.x = [lax.rem(x + d, 4) * 2 for d in range(4)]
        self.y = [lax.div(v, 2) * 64 + lax.rem(v, 2) * 8 for v in ys]
        self.z = [lax.rem(z + d, 4) * 16 for d in range(4)]
        self.c = [lax.rem(c + d, 2) for d in range(2)]
        self.sums = {}

    def __call__(self, offset, sign=1):
        dx, dy, dz, dc = ((sign * d) % m for d, m in zip(offset, (4, 4, 4, 2)))
        key = (dy, dz, dc)
        if key not in self.sums:
            self.sums[key] = self.z[dz] + self.y[dy] + self.c[dc]
        return self.sums[key] + self.x[dx]


def lanes(shape):
    return lax.broadcasted_iota(jnp.int32, shape, len(shape) - 1)


def sublanes(shape):
    return lax.broadcasted_iota(jnp.int32, shape, len(shape) - 2)


def roll(x, shift):
    return pltpu.roll(x, shift, 1)


def band(n, to, to_index, tab, stab, x_ref, w_ref):
    tile = tab[n]
    lane = lanes((8, 128)) + sublanes((8, 128))
    inside = (lane >= 4) & (lane < 132)
    for s in range(SLOTS):
        x = x_ref[stab[0, s, tile]].astype(F32)
        w = jnp.where(inside, w_ref[tile, s].astype(F32), 0.0)
        total = w[4:5] * x
        for k in (0, 1, 2, 3, 5, 6, 7):
            total = total + w[k : k + 1] * roll(x, (4 - k) % 128)
        to[to_index, s] = total.astype(BF16)


def row_at(rows_ref, y, count):
    row = pl.ds(pl.multiple_of(y * count, count), count)
    return rows_ref[0, row], rows_ref[1, row]


def spread(halves, into, count, at):
    row = jnp.concatenate(halves, axis=1)
    where = pl.ds(at, COLS)
    into[0:count, where] = roll(row, 1).astype(BF16)
    into[count : 2 * count, where] = row.astype(BF16)
    into[2 * count : 3 * count, where] = roll(row, COLS - 1).astype(BF16)


def padded_at(y):
    return (y + 1) * COLS if isinstance(y, int) else pl.multiple_of((y + 1) * COLS, COLS)


class Picker:
    def __init__(self, left_lane, right_lane, count):
        self.left, self.right = left_lane, right_lane
        self.shape = (count, 128)

    def empty(self):
        return jnp.zeros(self.shape, F32), jnp.zeros(self.shape, F32)

    def take(self, state, halves):
        lane = lanes(self.shape)
        return (
            jnp.where(lane == self.left, halves[0], roll(state[0], 1)),
            jnp.where(lane == self.right, halves[1], roll(state[1], 1)),
        )

    def place(self, state):
        lane = lanes(self.shape)
        left = roll(state[0], (1 - self.left) % 128)
        right = roll(state[1], (65 - self.right) % 128)
        return jnp.where((lane >= 1) & (lane <= 32), left, jnp.where((lane >= 65) & (lane <= 96), right, 0.0))


def corners(edge, y, halves):
    lane = lanes(edge.shape)
    left = roll(edge, (-(y + 1)) % 128)
    right = roll(edge, (62 - y) % 128)
    return jnp.where(lane == 0, left, halves[0]), jnp.where(lane == 127, right, halves[1])


def stage(q_ref, top, bottom, edge, near):
    for k, v in enumerate((top[0], top[1], edge, near, bottom[0], bottom[1])):
        q_ref[k] = v.astype(BF16)


def swap(q_ref, r_ref, send_sem, recv_sem):
    i = lax.axis_index("lat")
    j = lax.axis_index("lon")
    up, down = lax.rem(i + 7, 8), lax.rem(i + 1, 8)
    left, right = lax.rem(j + 15, 16), lax.rem(j + 1, 16)
    plan = (
        ((up, j), 0, 4, 4),
        ((down, j), 2, 4, 0),
        ((i, left), 2, 1, 9),
        ((i, right), 2, 1, 8),
        ((up, left), 2, 1, 13),
        ((up, right), 2, 1, 12),
        ((down, left), 2, 1, 11),
        ((down, right), 2, 1, 10),
    )
    for target, source, size, slot in plan:
        pltpu.make_async_remote_copy(
            src_ref=q_ref.at[pl.ds(source, size)],
            dst_ref=r_ref.at[pl.ds(slot, size)],
            send_sem=send_sem,
            recv_sem=recv_sem,
            device_id=target,
            device_id_type=MESH,
        ).start()


def whole(r_ref, send_sem, recv_sem):
    i = lax.axis_index("lat")
    return pltpu.make_async_remote_copy(
        src_ref=r_ref,
        dst_ref=r_ref,
        send_sem=send_sem,
        recv_sem=recv_sem,
        device_id=(lax.rem(i + 1, 8), lax.axis_index("lon")),
        device_id_type=MESH,
    )


def edge_inputs(edge, near, r_ref, count):
    i = lax.axis_index("lat")
    lane = lanes((count, 128))
    half = lane < 64
    place = jnp.where(half, lane, lane - 64)
    top = (place == 0) & (i > 0)
    bottom = (place == 33) & (i < 7)
    middle = (place >= 1) & (place <= 32)
    got = lambda k: r_ref[k].astype(F32)

    def frame(mid, above, below):
        return jnp.where(middle, mid, jnp.where(top, above, jnp.where(bottom, below, 0.0)))

    edges = frame(edge, roll(got(0), 96), roll(got(6), 32))
    nears = frame(near, roll(got(1), 96), roll(got(7), 32))
    sides = frame(
        jnp.where(half, roll(got(8), 64), roll(got(9), 64)),
        jnp.where(half, roll(got(10), 32), roll(got(11), 32)),
        jnp.where(half, roll(got(12), 96), roll(got(13), 96)),
    )
    three = (jnp.where(half, sides, nears), edges, jnp.where(half, nears, sides))
    above = [roll(v, 1) for v in three]
    below = [roll(v, 127) for v in three]
    return jnp.concatenate([v.astype(BF16) for v in (*above, *three, *below)], axis=0)


def halo_rows(r_ref, into, count):
    i = lax.axis_index("lat")
    for slot, live, at in ((2, i > 0, 0), (4, i < 7, (ROWS + 1) * COLS)):
        halves = [jnp.where(live, r_ref[slot + k].astype(F32), 0.0) for k in range(2)]
        spread(halves, into, count, at)


def update(gates, memory):
    ingate = jnp.tanh(gates[0:HID]) * 0.5 + 0.5
    forget = jnp.tanh(gates[HID : 2 * HID]) * 0.5 + 0.5
    outgate = jnp.tanh(gates[2 * HID : 3 * HID]) * 0.5 + 0.5
    memory = forget * memory + ingate * jnp.tanh(gates[3 * HID :])
    return outgate * jnp.tanh(memory), memory


def halves_of(v):
    return v[:, :128], v[:, 128:]


def body(
    stab_hbm, x_hbm, w_hbm, hid_hbm, cell_hbm, target_hbm, count_hbm, state_hbm, input_hbm, bias_hbm,
    hout_ref, cout_ref,
    tab, stab, x_ref, w_ref, hid_ref, cell_ref, target_ref, count_ref, state_ref, input_ref, bias_ref, weight, out_buf, in_buf, wide, sums, rows, s0, s1, fshifted, cells, ga, gb,
    qh, rh, qf, rf, load_sem, far_send, far_recv, near_send, near_recv,
):
    loads = [
        pltpu.make_async_copy(a, b, load_sem.at[k])
        for k, (a, b) in enumerate(
            (
                (stab_hbm, stab), (x_hbm, x_ref), (w_hbm, w_ref), (hid_hbm, hid_ref), (cell_hbm, cell_ref),
                (target_hbm, target_ref), (count_hbm, count_ref), (state_hbm, state_ref), (input_hbm, input_ref),
                (bias_hbm, bias_ref),
            )
        )
    ]
    for copy in loads:
        copy.start()
    at = Places()
    barrier = pltpu.get_barrier_semaphore()
    tab[0] = at(ORDER[0])
    for offset in sorted(ORDER[1:], key=lambda d: -sum(min(a, 4 - a) for a in d[:3])):
        pl.semaphore_signal(barrier, inc=1, device_id=at(offset), device_id_type=LOGICAL)
    for n in range(1, PEERS):
        tab[n] = at(ORDER[n])
    for copy in loads[:3]:
        copy.wait()

    def one_band(n, carry):
        band(n, out_buf, n, tab, stab, x_ref, w_ref)
        return carry

    def send(first, last):
        for n in range(max(first, 1), last):
            chunk = max(k for k in range(len(SIZES)) if STARTS[k] <= n)
            pltpu.make_async_remote_copy(
                src_ref=out_buf.at[n],
                dst_ref=in_buf.at[n],
                send_sem=far_send,
                recv_sem=far_recv.at[chunk],
                device_id=at(ORDER[n]),
                device_id_type=LOGICAL,
            ).start()

    band(0, in_buf, 0, tab, stab, x_ref, w_ref)
    lax.fori_loop(1, GROUP, one_band, 0)
    for first in range(GROUP, PEERS, GROUP):
        lax.fori_loop(first, first + GROUP, one_band, 0)
        if first == BARRIER_AT:
            pl.semaphore_wait(barrier, PEERS - 1)
            send(0, first)
        elif first > BARRIER_AT:
            send(first - GROUP, first)
    send(PEERS - GROUP, PEERS)

    loads[3].wait()
    for c in range(HID):
        for half in range(2):
            rows[half, pl.ds(c, ROWS, stride=HID), :] = hid_ref[c, :, half * 128 : half * 128 + 128].astype(F32)
    outer, inner = Picker(0, 127, HID), Picker(1, 126, HID)

    def prepare(k, state):
        y = ROWS - 1 - k
        halves = row_at(rows, y, HID)
        spread(halves, s0, HID, padded_at(y))
        return outer.take(state[0], halves), inner.take(state[1], halves)

    state = lax.fori_loop(0, ROWS, prepare, (outer.empty(), inner.empty()), unroll=2)
    edge, near = outer.place(state[0]), inner.place(state[1])
    stage(qh.at[0], row_at(rows, 0, HID), row_at(rows, ROWS - 1, HID), edge, near)
    for copy in loads[4:]:
        copy.wait()
    for c in range(HID):
        for half in range(2):
            cells[half, pl.ds(c, ROWS, stride=HID), :] = cell_ref[c, :, half * 128 : half * 128 + 128].astype(F32)
    swap(qh.at[0], rh.at[0], near_send.at[0], near_recv.at[0])

    def prepare_cell(k, state):
        return outer.take(state, row_at(cells, ROWS - 1 - k, HID))

    edge_cell = outer.place(lax.fori_loop(0, ROWS, prepare_cell, outer.empty(), unroll=2))

    scale = jnp.where(sublanes((128, 1)) < 3 * HID, 0.5, 1.0)
    bias = jnp.sum(jnp.where(sublanes((128, 128)) == lanes((128, 128)), bias_ref[...], 0.0), axis=1, keepdims=True)
    bias = bias * scale
    high = bias.astype(BF16).astype(F32)
    middle = (bias - high).astype(BF16).astype(F32)
    low = bias - high - middle
    lane = lanes((128, 128))
    extra = jnp.where(lane == 0, high, jnp.where(lane == 1, middle, jnp.where(lane == 2, low, 0.0)))
    taps = jnp.concatenate([state_ref[...].astype(F32), input_ref[...].astype(F32), extra.T[:80]], axis=0)
    deep = lax.broadcasted_iota(jnp.int32, (128, 128), 1)
    for k in range(4):
        part = taps[k * 128 : k * 128 + 128].T
        mult = jnp.where((deep + k * 128 < 432), scale, 1.0)
        weight[:, k * 128 : k * 128 + 128] = (part * mult).astype(BF16)
    ones = jnp.ones((16, COLS), BF16)

    counts = count_ref[...]
    aim4 = jnp.where(sublanes((SLOTS, 128)) < counts, target_ref[0], -1).astype(F32)
    aim8 = jnp.concatenate([aim4, aim4], axis=0).astype(BF16)
    sums[...] = jnp.zeros_like(sums)
    for g, (start, size) in enumerate(zip(STARTS, SIZES)):
        taken = size * SLOTS
        first = max(start, 1)
        got = in_buf.at[pl.ds(first, start + size - first)]
        pltpu.make_async_remote_copy(
            src_ref=got, dst_ref=got, send_sem=far_send, recv_sem=far_recv.at[g],
            device_id=at(ORDER[1]), device_id_type=LOGICAL,
        ).wait_recv()

        def unpack(n, carry):
            block = in_buf[start + n].astype(F32).reshape(SLOTS * CH, 128)
            wide[pl.ds(pl.multiple_of(n * SLOTS * CH, SLOTS * CH), SLOTS * CH)] = block
            return carry

        lax.fori_loop(0, size, unpack, 0, unroll=4)
        which = lax.shift_right_logical(lanes((1, taken)), 2)
        origin = jnp.zeros((1, taken), jnp.int32)
        for n in range(size):
            origin = jnp.where(which == n, at(ORDER[start + n], -1), origin)
        spot = (sublanes((128, taken)) == origin).astype(F32).astype(BF16)
        aims = jnp.dot(aim8, spot, preferred_element_type=F32)
        mine = sublanes((8, taken)) == lanes((8, taken)) % SLOTS
        aim = jnp.sum(jnp.where(mine, aims, 0.0), axis=0, keepdims=True)
        chosen = (sublanes((64, taken)).astype(F32) == aim).astype(F32).astype(BF16)
        for c in range(0, CH, 2):
            pair = [wide[pl.ds(c + k, taken, stride=CH), :].astype(BF16) for k in range(2)]
            part = jnp.dot(chosen, jnp.concatenate(pair, axis=1), preferred_element_type=F32)
            sums[c * 64 : c * 64 + 64] += part[:, :128]
            sums[c * 64 + 64 : c * 64 + 128] += part[:, 128:]

    def cell_row(y):
        return sums[pl.ds(2 * y, CH, stride=64), :], sums[pl.ds(2 * y + 1, CH, stride=64), :]

    spot = lanes((CH, 128))
    fedge = fnear = jnp.zeros((CH, 128), F32)
    for y in range(ROWS):
        halves = cell_row(y)
        spread(halves, fshifted, CH, padded_at(y))
        fedge = jnp.where(spot == y + 1, roll(halves[0], y + 1), fedge)
        fedge = jnp.where(spot == y + 65, roll(halves[1], (y + 66) % 128), fedge)
        fnear = jnp.where(spot == y + 1, roll(halves[0], y), fnear)
        fnear = jnp.where(spot == y + 65, roll(halves[1], (y + 67) % 128), fnear)
    stage(qf, cell_row(0), cell_row(ROWS - 1), fedge, fnear)
    swap(qf, rf, near_send.at[STEPS], near_recv.at[STEPS])

    fmini = None
    for t in range(STEPS):
        here, there = (s0, s1) if t % 2 == 0 else (s1, s0)
        last = t == STEPS - 1

        def gates_of(y, count=1):
            spans = [pl.ds(padded_at(y - 1 + a), COLS * count) for a in range(3)]
            fixed = jnp.ones((16, COLS * count), BF16)
            rhs = jnp.concatenate([here[:, w] for w in spans] + [fshifted[:, w] for w in spans] + [fixed], axis=0)
            return jnp.dot(weight[:, :448], rhs, preferred_element_type=F32)

        def finish_row(y, gates):
            hidden, memory = update(gates, jnp.concatenate(row_at(cells, y, HID), axis=1))
            halves = halves_of(hidden)
            where = pl.ds(pl.multiple_of(y * HID, HID), HID)
            for half, v in enumerate(halves_of(memory)):
                cells[half, where] = v
            if last:
                for half, v in enumerate(halves):
                    rows[half, where] = v
            else:
                spread(halves, there, HID, padded_at(y))
            return halves

        def block(low, buffer, state):
            for r in range(BLOCK - 1, -1, -1):
                halves = finish_row(low + r, buffer[:, r * COLS : r * COLS + COLS])
                state = state if last else inner.take(state, halves)
            return state

        def inside(k, state):
            low = ROWS - 1 - BLOCK - 2 * BLOCK * k
            gb[...] = gates_of(low - BLOCK, BLOCK)
            state = block(low, ga, state)
            ga[...] = gates_of(lax.max(low - 2 * BLOCK, 1), BLOCK)
            return block(low - BLOCK, gb, state)

        ga[...] = gates_of(ROWS - 1 - BLOCK, BLOCK)
        state = 0 if last else inner.empty()
        state = lax.fori_loop(0, (ROWS - 2) // (2 * BLOCK), inside, state)

        whole(rh.at[t], near_send.at[t], near_recv.at[t]).wait_recv()
        if t == 0:
            whole(rf, near_send.at[STEPS], near_recv.at[STEPS]).wait_recv()
            fmini = edge_inputs(fedge, fnear, rf, CH)
            halo_rows(rf, fshifted, CH)
        mini = jnp.concatenate([edge_inputs(edge, near, rh.at[t], HID), fmini, ones[:, :128]], axis=0)
        halo_rows(rh.at[t], here, HID)
        gates = jnp.dot(weight[:, :448], mini, preferred_element_type=F32)
        edge, edge_cell = update(gates, edge_cell)
        tops, bottoms = gates_of(0), gates_of(ROWS - 1)
        top = finish_row(0, tops)
        bottom = finish_row(ROWS - 1, bottoms)
        if last:
            break
        state = inner.take(state, top)
        far_left = roll(bottom[0], 31)
        far_right = roll(bottom[1], (96 - 126) % 128)
        spot = lanes((HID, 128))
        near = jnp.where(spot == 32, far_left, jnp.where(spot == 96, far_right, inner.place(state)))
        stage(qh.at[t + 1], corners(edge, 0, top), corners(edge, ROWS - 1, bottom), edge, near)
        swap(qh.at[t + 1], rh.at[t + 1], near_send.at[t + 1], near_recv.at[t + 1])

        lane = lanes((HID, 128))
        left = [roll(edge, -y % 128).astype(BF16) for y in range(ROWS + 1)]
        right = [roll(edge, (62 - y) % 128).astype(BF16) for y in range(ROWS + 1)]
        for y in range(ROWS):
            first = pl.ds((y + 1) * COLS, 128)
            second = pl.ds((y + 1) * COLS + 128, 128)
            for block_at, where, spot, value in (
                (0, first, 1, left[y]), (1, first, 0, left[y + 1]),
                (1, second, 127, right[y]), (2, second, 126, right[y + 1]),
            ):
                part = there.at[block_at * HID : block_at * HID + HID, where]
                part[...] = jnp.where(lane == spot, value, part[...])

    for source, columns, to in ((rows, edge, hout_ref), (cells, edge_cell, cout_ref)):
        for y in range(ROWS):
            one, two = corners(columns, y, row_at(source, y, HID))
            to[y, :, :128] = one.astype(BF16)
            to[y, :, 128:] = two.astype(BF16)

    sent = out_buf.at[pl.ds(1, PEERS - 1)]
    pltpu.make_async_remote_copy(
        src_ref=sent, dst_ref=sent, send_sem=far_send, recv_sem=far_recv.at[0],
        device_id=at(ORDER[1]), device_id_type=LOGICAL,
    ).wait_send()
    for t in range(STEPS):
        whole(rh.at[t], near_send.at[t], near_recv.at[t]).wait_send()
    whole(rf, near_send.at[STEPS], near_recv.at[STEPS]).wait_send()


def in_hbm(x):
    return pltpu.with_memory_space_constraint(x, pltpu.HBM)


def on_device(
    satellite_blocks, slot_source, slot_weight, slot_target, tile_counts,
    gate_input_weight, gate_state_weight, gate_bias, hidden_init, cell_init,
):
    operands = (
        slot_source.transpose(0, 2, 1), satellite_blocks, slot_weight[0], hidden_init, cell_init,
        slot_target.transpose(0, 2, 1), tile_counts, gate_state_weight.T, gate_input_weight.T, gate_bias.reshape(1, -1),
    )
    vmem = pl.BlockSpec(memory_space=pltpu.VMEM)
    hbm = pl.BlockSpec(memory_space=pltpu.HBM)
    padded = (ROWS + 2) * COLS
    hidden, memory = pl.pallas_call(
        body,
        out_shape=[jax.ShapeDtypeStruct((ROWS, HID, COLS), BF16)] * 2,
        in_specs=[hbm] * 10,
        out_specs=[vmem, vmem],
        scratch_shapes=[
            pltpu.SMEM((PEERS,), jnp.int32),
            pltpu.SMEM((1, SLOTS, PEERS), jnp.int32),
            pltpu.VMEM((PEERS, CH, 128), BF16),
            pltpu.VMEM((PEERS, SLOTS, 8, 128), BF16),
            pltpu.VMEM((HID, ROWS, COLS), BF16),
            pltpu.VMEM((HID, ROWS, COLS), BF16),
            pltpu.VMEM((1, SLOTS, PEERS), jnp.int32),
            pltpu.VMEM((1, PEERS), jnp.int32),
            pltpu.VMEM((9 * HID, 128), BF16),
            pltpu.VMEM((9 * CH, 128), BF16),
            pltpu.VMEM((1, 128), F32),
            pltpu.VMEM((128, 512), BF16),
            pltpu.VMEM((PEERS, SLOTS, CH, 128), BF16),
            pltpu.VMEM((PEERS, SLOTS, CH, 128), BF16),
            pltpu.VMEM((max(SIZES) * SLOTS * CH, 128), F32),
            pltpu.VMEM((CH * 64, 128), F32),
            pltpu.VMEM((2, ROWS * HID, 128), F32),
            pltpu.VMEM((3 * HID, padded), BF16),
            pltpu.VMEM((3 * HID, padded), BF16),
            pltpu.VMEM((3 * CH, padded), BF16),
            pltpu.VMEM((2, ROWS * HID, 128), F32),
            pltpu.VMEM((128, COLS * BLOCK), F32),
            pltpu.VMEM((128, COLS * BLOCK), F32),
            pltpu.VMEM((STEPS, 6, HID, 128), BF16),
            pltpu.VMEM((STEPS, 14, HID, 128), BF16),
            pltpu.VMEM((6, CH, 128), BF16),
            pltpu.VMEM((14, CH, 128), BF16),
            pltpu.SemaphoreType.DMA((10,)),
            pltpu.SemaphoreType.DMA,
            pltpu.SemaphoreType.DMA((len(SIZES),)),
            pltpu.SemaphoreType.DMA((STEPS + 1,)),
            pltpu.SemaphoreType.DMA((STEPS + 1,)),
        ],
        compiler_params=pltpu.CompilerParams(
            collective_id=0, has_side_effects=True, vmem_limit_bytes=30 * 2**20
        ),
        name="reproject_and_step",
    )(*[in_hbm(v) for v in operands])
    return hidden.transpose(1, 0, 2), memory.transpose(1, 0, 2)


def solution(mesh):
    placed = (
        P(("lat", "lon"), None, None),
        P(("lat", "lon"), None, None),
        P(("lat", "lon"), None, None, None, None),
        P(("lat", "lon"), None, None),
        P(("lat", "lon"), None),
        P(),
        P(),
        P(),
        P(None, "lat", "lon"),
        P(None, "lat", "lon"),
    )
    return jax.shard_map(
        on_device,
        mesh=mesh,
        in_specs=placed,
        out_specs=(P(None, "lat", "lon"), P(None, "lat", "lon")),
        check_vma=False,
    )
```

```python
import itertools
import random

import jax
import jax.numpy as jnp
import numpy as np
from jax import lax
from jax.experimental import pallas as pl
from jax.experimental.pallas import tpu as pltpu
from jax.sharding import PartitionSpec as P

STEPS = 3
MESH = pl.DeviceIdType.MESH
LOGICAL = pl.DeviceIdType.LOGICAL
F32 = jnp.float32
BF16 = jnp.bfloat16
PEERS = 128
SLOTS = 4
SIZES = (64, 32, 16, 16)
STARTS = (0, 64, 96, 112)
GROUP = 8
BARRIER_AT = 16
BLOCK = 5
HALO = 3
ROWS = 32
COLS = 256
CH = 16
HID = 32


def send_order():
    offsets = [d for d in itertools.product(range(4), range(4), range(4), range(2)) if any(d)]
    random.Random(0).shuffle(offsets)
    return [(0, 0, 0, 0)] + offsets


ORDER = send_order()


def coords():
    i = lax.axis_index("lat")
    j = lax.axis_index("lon")
    return (lax.rem(lax.div(j, 2), 4), lax.div(i, 4) * 2 + lax.div(j, 8), lax.rem(i, 4), lax.rem(j, 2))


class Places:
    def __init__(self):
        x, y, z, c = coords()
        ys = [lax.rem(y + d, 4) for d in range(4)]
        self.x = [lax.rem(x + d, 4) * 2 for d in range(4)]
        self.y = [lax.div(v, 2) * 64 + lax.rem(v, 2) * 8 for v in ys]
        self.z = [lax.rem(z + d, 4) * 16 for d in range(4)]
        self.c = [lax.rem(c + d, 2) for d in range(2)]
        self.sums = {}

    def __call__(self, offset, sign=1):
        dx, dy, dz, dc = ((sign * d) % m for d, m in zip(offset, (4, 4, 4, 2)))
        key = (dy, dz, dc)
        if key not in self.sums:
            self.sums[key] = self.z[dz] + self.y[dy] + self.c[dc]
        return self.sums[key] + self.x[dx]


def lanes(shape):
    return lax.broadcasted_iota(jnp.int32, shape, len(shape) - 1)


def sublanes(shape):
    return lax.broadcasted_iota(jnp.int32, shape, len(shape) - 2)


def roll(x, shift):
    return pltpu.roll(x, shift, 1)


def band(n, to, to_index, tab, stab, x_ref, w_ref):
    tile = tab[n]
    lane = lanes((8, 128)) + sublanes((8, 128))
    inside = (lane >= 4) & (lane < 132)
    for s in range(SLOTS):
        x = x_ref[stab[0, s, tile]].astype(F32)
        w = jnp.where(inside, w_ref[tile, s].astype(F32), 0.0)
        total = w[4:5] * x
        for k in (0, 1, 2, 3, 5, 6, 7):
            total = total + w[k : k + 1] * roll(x, (4 - k) % 128)
        to[to_index, s] = total.astype(BF16)


def row_at(rows_ref, y, count):
    row = pl.ds(pl.multiple_of(y * count, count), count)
    return rows_ref[0, row], rows_ref[1, row]


def spread(halves, into, count, at):
    row = jnp.concatenate(halves, axis=1)
    where = pl.ds(at, COLS)
    into[0:count, where] = roll(row, 1).astype(BF16)
    into[count : 2 * count, where] = row.astype(BF16)
    into[2 * count : 3 * count, where] = roll(row, COLS - 1).astype(BF16)


def padded_at(y):
    return (y + HALO) * COLS if isinstance(y, int) else pl.multiple_of((y + HALO) * COLS, COLS)


class Picker:
    def __init__(self, left_lane, right_lane, count):
        self.left, self.right = left_lane, right_lane
        self.shape = (count, 128)

    def empty(self):
        return jnp.zeros(self.shape, F32), jnp.zeros(self.shape, F32)

    def take(self, state, halves):
        lane = lanes(self.shape)
        return (
            jnp.where(lane == self.left, halves[0], roll(state[0], 1)),
            jnp.where(lane == self.right, halves[1], roll(state[1], 1)),
        )

    def place(self, state, lowest=0):
        lane = lanes(self.shape)
        left = roll(state[0], (lowest + HALO - self.left) % 128)
        right = roll(state[1], (lowest + HALO + 64 - self.right) % 128)
        first, last = lowest + HALO, HALO + ROWS - 1
        return jnp.where(
            (lane >= first) & (lane <= last),
            left,
            jnp.where((lane >= first + 64) & (lane <= last + 64), right, 0.0),
        )

    def insert(self, value, y, halves):
        lane = lanes(self.shape)
        at = y + HALO
        value = jnp.where(lane == at, roll(halves[0], (at - self.left) % 128), value)
        return jnp.where(lane == at + 64, roll(halves[1], (at + 64 - self.right) % 128), value)


def corners(edge, y, halves):
    lane = lanes(edge.shape)
    left = roll(edge, (-(y + HALO)) % 128)
    right = roll(edge, (63 - HALO - y) % 128)
    return jnp.where(lane == 0, left, halves[0]), jnp.where(lane == 127, right, halves[1])


def stage(q_ref, row_of, depth, columns):
    top = [h for y in range(depth) for h in row_of(y)]
    bottom = [h for y in range(ROWS - depth, ROWS) for h in row_of(y)]
    for k, v in enumerate((*top, *columns, *bottom)):
        q_ref[k] = v.astype(BF16)


def swap(plan, q_ref, r_ref, send_sem, recv_sem):
    i = lax.axis_index("lat")
    j = lax.axis_index("lon")
    lat = {0: i, -1: lax.rem(i + 7, 8), 1: lax.rem(i + 1, 8)}
    lon = {0: j, -1: lax.rem(j + 15, 16), 1: lax.rem(j + 1, 16)}
    for di, dj, source, size, slot in plan:
        pltpu.make_async_remote_copy(
            src_ref=q_ref.at[pl.ds(source, size)],
            dst_ref=r_ref.at[pl.ds(slot, size)],
            send_sem=send_sem,
            recv_sem=recv_sem,
            device_id=(lat[di], lon[dj]),
            device_id_type=MESH,
        ).start()


DEEP = (
    (-1, 0, 0, 8, 8), (1, 0, 6, 8, 0), (0, -1, 6, 1, 17), (0, 1, 6, 1, 16),
    (-1, -1, 6, 1, 21), (-1, 1, 6, 1, 20), (1, -1, 6, 1, 19), (1, 1, 6, 1, 18),
)
CELLS = ((-1, 0, 0, 5, 5), (1, 0, 4, 5, 0))
SIDES = ((0, -1, 0, 1, 1), (0, 1, 0, 1, 0))


def whole(r_ref, send_sem, recv_sem):
    i = lax.axis_index("lat")
    return pltpu.make_async_remote_copy(
        src_ref=r_ref,
        dst_ref=r_ref,
        send_sem=send_sem,
        recv_sem=recv_sem,
        device_id=(lax.rem(i + 1, 8), lax.axis_index("lon")),
        device_id_type=MESH,
    )


def in_globe(y):
    i = lax.axis_index("lat")
    return ((y >= 0) | (i > 0)) & ((y < ROWS) | (i < 7))


def frame(count, middle, above, below):
    lane = lanes((count, 128))
    y = jnp.where(lane < 64, lane, lane - 64) - HALO
    live = in_globe(y) & (y < ROWS + HALO)
    picked = jnp.where(y < 0, roll(above, 96), jnp.where(y < ROWS, middle, roll(below, 32)))
    return jnp.where(live, picked, 0.0)


def taps_of(edges, nears, sides):
    half = lanes(edges.shape) < 64
    three = (jnp.where(half, sides, nears), edges, jnp.where(half, nears, sides))
    above = [roll(v, 1) for v in three]
    below = [roll(v, 127) for v in three]
    return jnp.concatenate([v.astype(BF16) for v in (*above, *three, *below)], axis=0)


def deep_taps(edge, near, r_ref, count):
    got = lambda k: r_ref[k].astype(F32)
    half = lanes((count, 128)) < 64
    swapped = [roll(jnp.where(half, got(k + 1), got(k)), 64) for k in (16, 18, 20)]
    return taps_of(
        frame(count, edge, got(0), got(14)), frame(count, near, got(1), got(15)), frame(count, *swapped)
    )


def halo_rows(r_ref, into, count):
    for slot, y in ((2, -3), (4, -2), (6, -1), (8, 32), (10, 33), (12, 34)):
        halves = [jnp.where(in_globe(y), r_ref[slot + k].astype(F32), 0.0) for k in range(2)]
        spread(halves, into, count, padded_at(y))


def update(gates, memory):
    ingate = jnp.tanh(gates[0:HID]) * 0.5 + 0.5
    forget = jnp.tanh(gates[HID : 2 * HID]) * 0.5 + 0.5
    outgate = jnp.tanh(gates[2 * HID : 3 * HID]) * 0.5 + 0.5
    memory = forget * memory + ingate * jnp.tanh(gates[3 * HID :])
    return outgate * jnp.tanh(memory), memory


def halves_of(v):
    return v[:, :128], v[:, 128:]


def body(
    stab_hbm, x_hbm, w_hbm, hid_hbm, cell_hbm, target_hbm, count_hbm, state_hbm, input_hbm, bias_hbm,
    hout_ref, cout_ref,
    tab, stab, x_ref, w_ref, hid_ref, cell_ref, target_ref, count_ref, state_ref, input_ref, bias_ref, weight, out_buf, in_buf, wide, sums, rows, s0, s1, fshifted, cells, ga, gb,
    qh, rh, qe, re, qf, rf, qc, rc, load_sem, far_send, far_recv, near_send, near_recv,
):
    loads = [
        pltpu.make_async_copy(a, b, load_sem.at[k])
        for k, (a, b) in enumerate(
            (
                (stab_hbm, stab), (x_hbm, x_ref), (w_hbm, w_ref), (hid_hbm, hid_ref), (cell_hbm, cell_ref),
                (target_hbm, target_ref), (count_hbm, count_ref), (state_hbm, state_ref), (input_hbm, input_ref),
                (bias_hbm, bias_ref),
            )
        )
    ]
    for copy in loads:
        copy.start()
    at = Places()
    barrier = pltpu.get_barrier_semaphore()
    tab[0] = at(ORDER[0])
    for offset in sorted(ORDER[1:], key=lambda d: -sum(min(a, 4 - a) for a in d[:3])):
        pl.semaphore_signal(barrier, inc=1, device_id=at(offset), device_id_type=LOGICAL)
    for n in range(1, PEERS):
        tab[n] = at(ORDER[n])
    for copy in loads[:3]:
        copy.wait()

    def one_band(n, carry):
        band(n, out_buf, n, tab, stab, x_ref, w_ref)
        return carry

    def send(first, last):
        for n in range(max(first, 1), last):
            chunk = max(k for k in range(len(SIZES)) if STARTS[k] <= n)
            pltpu.make_async_remote_copy(
                src_ref=out_buf.at[n],
                dst_ref=in_buf.at[n],
                send_sem=far_send,
                recv_sem=far_recv.at[chunk],
                device_id=at(ORDER[n]),
                device_id_type=LOGICAL,
            ).start()

    band(0, in_buf, 0, tab, stab, x_ref, w_ref)
    lax.fori_loop(1, GROUP, one_band, 0)
    for first in range(GROUP, PEERS, GROUP):
        lax.fori_loop(first, first + GROUP, one_band, 0)
        if first == BARRIER_AT:
            pl.semaphore_wait(barrier, PEERS - 1)
            send(0, first)
        elif first > BARRIER_AT:
            send(first - GROUP, first)
    send(PEERS - GROUP, PEERS)

    loads[3].wait()
    for c in range(HID):
        for half in range(2):
            rows[half, pl.ds(c, ROWS, stride=HID), :] = hid_ref[c, :, half * 128 : half * 128 + 128].astype(F32)
    outer, inner = Picker(0, 127, HID), Picker(1, 126, HID)

    def prepare(k, state):
        y = ROWS - 1 - k
        halves = row_at(rows, y, HID)
        spread(halves, s0, HID, padded_at(y))
        return outer.take(state[0], halves), inner.take(state[1], halves)

    state = lax.fori_loop(0, ROWS, prepare, (outer.empty(), inner.empty()), unroll=2)
    edge, near = outer.place(state[0]), inner.place(state[1])
    stage(qh, lambda y: row_at(rows, y, HID), HALO, (edge, near))
    swap(DEEP, qh, rh, near_send.at[0], near_recv.at[0])
    for copy in loads[4:]:
        copy.wait()
    for c in range(HID):
        for half in range(2):
            cells[half, pl.ds(c + 2 * HID, ROWS, stride=HID), :] = cell_ref[c, :, half * 128 : half * 128 + 128].astype(F32)

    def prepare_cell(k, state):
        return outer.take(state, row_at(cells, ROWS + 1 - k, HID))

    edge_cell = outer.place(lax.fori_loop(0, ROWS, prepare_cell, outer.empty(), unroll=2))

    stage(qc, lambda y: row_at(cells, y + 2, HID), 2, (edge_cell,))
    swap(CELLS, qc, rc, near_send.at[STEPS + 1], near_recv.at[STEPS + 1])

    scale = jnp.where(sublanes((128, 1)) < 3 * HID, 0.5, 1.0)
    bias = jnp.sum(jnp.where(sublanes((128, 128)) == lanes((128, 128)), bias_ref[...], 0.0), axis=1, keepdims=True)
    bias = bias * scale
    high = bias.astype(BF16).astype(F32)
    middle = (bias - high).astype(BF16).astype(F32)
    low = bias - high - middle
    lane = lanes((128, 128))
    extra = jnp.where(lane == 0, high, jnp.where(lane == 1, middle, jnp.where(lane == 2, low, 0.0)))
    taps = jnp.concatenate([state_ref[...].astype(F32), input_ref[...].astype(F32), extra.T[:80]], axis=0)
    deep = lax.broadcasted_iota(jnp.int32, (128, 128), 1)
    for k in range(4):
        part = taps[k * 128 : k * 128 + 128].T
        mult = jnp.where((deep + k * 128 < 432), scale, 1.0)
        weight[:, k * 128 : k * 128 + 128] = (part * mult).astype(BF16)
    ones = jnp.ones((16, COLS), BF16)

    counts = count_ref[...]
    aim4 = jnp.where(sublanes((SLOTS, 128)) < counts, target_ref[0], -1).astype(F32)
    aim8 = jnp.concatenate([aim4, aim4], axis=0).astype(BF16)
    sums[...] = jnp.zeros_like(sums)
    for g, (start, size) in enumerate(zip(STARTS, SIZES)):
        taken = size * SLOTS
        first = max(start, 1)
        got = in_buf.at[pl.ds(first, start + size - first)]
        pltpu.make_async_remote_copy(
            src_ref=got, dst_ref=got, send_sem=far_send, recv_sem=far_recv.at[g],
            device_id=at(ORDER[1]), device_id_type=LOGICAL,
        ).wait_recv()

        def unpack(n, carry):
            block = in_buf[start + n].astype(F32).reshape(SLOTS * CH, 128)
            wide[pl.ds(pl.multiple_of(n * SLOTS * CH, SLOTS * CH), SLOTS * CH)] = block
            return carry

        lax.fori_loop(0, size, unpack, 0, unroll=4)
        which = lax.shift_right_logical(lanes((1, taken)), 2)
        origin = jnp.zeros((1, taken), jnp.int32)
        for n in range(size):
            origin = jnp.where(which == n, at(ORDER[start + n], -1), origin)
        spot = (sublanes((128, taken)) == origin).astype(F32).astype(BF16)
        aims = jnp.dot(aim8, spot, preferred_element_type=F32)
        mine = sublanes((8, taken)) == lanes((8, taken)) % SLOTS
        aim = jnp.sum(jnp.where(mine, aims, 0.0), axis=0, keepdims=True)
        chosen = (sublanes((64, taken)).astype(F32) == aim).astype(F32).astype(BF16)
        for c in range(0, CH, 2):
            pair = [wide[pl.ds(c + k, taken, stride=CH), :].astype(BF16) for k in range(2)]
            part = jnp.dot(chosen, jnp.concatenate(pair, axis=1), preferred_element_type=F32)
            sums[c * 64 : c * 64 + 64] += part[:, :128]
            sums[c * 64 + 64 : c * 64 + 128] += part[:, 128:]

    def cell_row(y):
        return sums[pl.ds(2 * y, CH, stride=64), :], sums[pl.ds(2 * y + 1, CH, stride=64), :]

    fouter, finner = Picker(0, 127, CH), Picker(1, 126, CH)
    fedge = fnear = jnp.zeros((CH, 128), F32)
    for y in range(ROWS):
        halves = cell_row(y)
        spread(halves, fshifted, CH, padded_at(y))
        fedge = fouter.insert(fedge, y, halves)
        fnear = finner.insert(fnear, y, halves)
    stage(qf, cell_row, HALO, (fedge, fnear))
    swap(DEEP, qf, rf, near_send.at[STEPS], near_recv.at[STEPS])

    fmini = None
    for t in range(STEPS):
        here, there = (s0, s1) if t % 2 == 0 else (s1, s0)
        last = t == STEPS - 1

        def gates_of(y, count=1):
            spans = [pl.ds(padded_at(y - 1 + a), COLS * count) for a in range(3)]
            fixed = jnp.ones((16, COLS * count), BF16)
            rhs = jnp.concatenate([here[:, w] for w in spans] + [fshifted[:, w] for w in spans] + [fixed], axis=0)
            return jnp.dot(weight[:, :448], rhs, preferred_element_type=F32)

        def finish_row(y, gates):
            hidden, memory = update(gates, jnp.concatenate(row_at(cells, y + 2, HID), axis=1))
            if not (isinstance(y, int) and 0 <= y < ROWS):
                hidden = jnp.where(in_globe(y), hidden, 0.0) if isinstance(y, int) else hidden
            halves = halves_of(hidden)
            for half, v in enumerate(halves_of(memory)):
                cells[half, pl.ds(pl.multiple_of((y + 2) * HID, HID), HID)] = v
            if last:
                for half, v in enumerate(halves):
                    rows[half, pl.ds(pl.multiple_of(y * HID, HID), HID)] = v
            else:
                spread(halves, there, HID, padded_at(y))
            return halves

        def block(low, buffer, state):
            for r in range(BLOCK - 1, -1, -1):
                halves = finish_row(low + r, buffer[:, r * COLS : r * COLS + COLS])
                state = state if last else inner.take(state, halves)
            return state

        def inside(k, state):
            low = ROWS - 1 - BLOCK - 2 * BLOCK * k
            gb[...] = gates_of(low - BLOCK, BLOCK)
            state = block(low, ga, state)
            ga[...] = gates_of(lax.max(low - 2 * BLOCK, 1), BLOCK)
            return block(low - BLOCK, gb, state)

        ga[...] = gates_of(ROWS - 1 - BLOCK, BLOCK)
        state = 0 if last else inner.empty()
        state = lax.fori_loop(0, (ROWS - 2) // (2 * BLOCK), inside, state)

        if t == 0:
            for k, got in ((0, rh), (STEPS + 1, rc), (STEPS, rf)):
                whole(got, near_send.at[k], near_recv.at[k]).wait_recv()
            halo_rows(rh, here, HID)
            halo_rows(rf, fshifted, CH)
            for slot, y in ((1, -2), (3, -1), (5, 32), (7, 33)):
                for half in range(2):
                    cells[half, (y + 2) * HID : (y + 3) * HID] = rc[slot + half].astype(F32)
            edge_cell = frame(HID, edge_cell, rc[0].astype(F32), rc[9].astype(F32))
            fmini = deep_taps(fedge, fnear, rf, CH)
        depth = STEPS - t
        low, high = gates_of(1 - depth, depth), gates_of(ROWS - 1, depth)
        above = [finish_row(-r, low[:, (depth - 1 - r) * COLS : (depth - r) * COLS]) for r in range(depth)]
        below = [finish_row(ROWS - 1 + r, high[:, r * COLS : (r + 1) * COLS]) for r in range(depth)]
        if t == 0:
            mini = deep_taps(edge, near, rh, HID)
        else:
            whole(re.at[t - 1], near_send.at[t], near_recv.at[t]).wait_recv()
            half = lanes((HID, 128)) < 64
            sides = roll(jnp.where(half, re[t - 1, 1].astype(F32), re[t - 1, 0].astype(F32)), 64)
            mini = taps_of(edge, near, sides)
        mini = jnp.concatenate([mini, fmini, ones[:, :128]], axis=0)
        gates = jnp.dot(weight[:, :448], mini, preferred_element_type=F32)
        edge, edge_cell = update(gates, edge_cell)
        if last:
            break
        lane = lanes((HID, 128))
        edge = jnp.where(in_globe(jnp.where(lane < 64, lane, lane - 64) - HALO), edge, 0.0)
        qe[t, 0] = edge.astype(BF16)
        for halves in above:
            state = inner.take(state, halves)
        near = inner.place(state, 1 - depth)
        near = jnp.where((lane == 34) | (lane == 98), 0.0, near)
        for r, halves in enumerate(below):
            near = inner.insert(near, ROWS - 1 + r, halves)
        left = {y: roll(edge, (1 - HALO - y) % 128).astype(BF16) for y in range(1 - depth, ROWS + depth)}
        right = {y: roll(edge, (63 - HALO - y) % 128).astype(BF16) for y in range(1 - depth, ROWS + depth)}
        swap(SIDES, qe.at[t], re.at[t], near_send.at[t + 1], near_recv.at[t + 1])
        for y in range(1 - depth, ROWS + depth - 1):
            first = pl.ds(padded_at(y), 128)
            second = pl.ds(padded_at(y) + 128, 128)
            for block_at, where, spot, value in (
                (0, first, 1, left[y]), (1, first, 0, left[y + 1]),
                (1, second, 127, right[y]), (2, second, 126, right[y + 1]),
            ):
                part = there.at[block_at * HID : block_at * HID + HID, where]
                part[...] = jnp.where(lane == spot, value, part[...])

    for source, skip, columns, to in ((rows, 0, edge, hout_ref), (cells, 2, edge_cell, cout_ref)):
        for y in range(ROWS):
            one, two = corners(columns, y, row_at(source, y + skip, HID))
            to[y, :, :128] = one.astype(BF16)
            to[y, :, 128:] = two.astype(BF16)

    sent = out_buf.at[pl.ds(1, PEERS - 1)]
    pltpu.make_async_remote_copy(
        src_ref=sent, dst_ref=sent, send_sem=far_send, recv_sem=far_recv.at[0],
        device_id=at(ORDER[1]), device_id_type=LOGICAL,
    ).wait_send()
    for k, got in ((0, rh), (1, re.at[0]), (2, re.at[1]), (STEPS, rf), (STEPS + 1, rc)):
        whole(got, near_send.at[k], near_recv.at[k]).wait_send()


def in_hbm(x):
    return pltpu.with_memory_space_constraint(x, pltpu.HBM)


def on_device(
    satellite_blocks, slot_source, slot_weight, slot_target, tile_counts,
    gate_input_weight, gate_state_weight, gate_bias, hidden_init, cell_init,
):
    operands = (
        slot_source.transpose(0, 2, 1), satellite_blocks, slot_weight[0], hidden_init, cell_init,
        slot_target.transpose(0, 2, 1), tile_counts, gate_state_weight.T, gate_input_weight.T, gate_bias.reshape(1, -1),
    )
    vmem = pl.BlockSpec(memory_space=pltpu.VMEM)
    hbm = pl.BlockSpec(memory_space=pltpu.HBM)
    padded = (ROWS + 2 * HALO) * COLS
    hidden, memory = pl.pallas_call(
        body,
        out_shape=[jax.ShapeDtypeStruct((ROWS, HID, COLS), BF16)] * 2,
        in_specs=[hbm] * 10,
        out_specs=[vmem, vmem],
        scratch_shapes=[
            pltpu.SMEM((PEERS,), jnp.int32),
            pltpu.SMEM((1, SLOTS, PEERS), jnp.int32),
            pltpu.VMEM((PEERS, CH, 128), BF16),
            pltpu.VMEM((PEERS, SLOTS, 8, 128), BF16),
            pltpu.VMEM((HID, ROWS, COLS), BF16),
            pltpu.VMEM((HID, ROWS, COLS), BF16),
            pltpu.VMEM((1, SLOTS, PEERS), jnp.int32),
            pltpu.VMEM((1, PEERS), jnp.int32),
            pltpu.VMEM((9 * HID, 128), BF16),
            pltpu.VMEM((9 * CH, 128), BF16),
            pltpu.VMEM((1, 128), F32),
            pltpu.VMEM((128, 512), BF16),
            pltpu.VMEM((PEERS, SLOTS, CH, 128), BF16),
            pltpu.VMEM((PEERS, SLOTS, CH, 128), BF16),
            pltpu.VMEM((max(SIZES) * SLOTS * CH, 128), F32),
            pltpu.VMEM((CH * 64, 128), F32),
            pltpu.VMEM((2, ROWS * HID, 128), F32),
            pltpu.VMEM((3 * HID, padded), BF16),
            pltpu.VMEM((3 * HID, padded), BF16),
            pltpu.VMEM((3 * CH, padded), BF16),
            pltpu.VMEM((2, (ROWS + 4) * HID, 128), F32),
            pltpu.VMEM((128, COLS * BLOCK), F32),
            pltpu.VMEM((128, COLS * BLOCK), F32),
            pltpu.VMEM((14, HID, 128), BF16),
            pltpu.VMEM((22, HID, 128), BF16),
            pltpu.VMEM((2, 1, HID, 128), BF16),
            pltpu.VMEM((2, 2, HID, 128), BF16),
            pltpu.VMEM((14, CH, 128), BF16),
            pltpu.VMEM((22, CH, 128), BF16),
            pltpu.VMEM((9, HID, 128), BF16),
            pltpu.VMEM((10, HID, 128), BF16),
            pltpu.SemaphoreType.DMA((10,)),
            pltpu.SemaphoreType.DMA,
            pltpu.SemaphoreType.DMA((len(SIZES),)),
            pltpu.SemaphoreType.DMA((STEPS + 2,)),
            pltpu.SemaphoreType.DMA((STEPS + 2,)),
        ],
        compiler_params=pltpu.CompilerParams(
            collective_id=0, has_side_effects=True, vmem_limit_bytes=30 * 2**20
        ),
        name="reproject_and_step",
    )(*[in_hbm(v) for v in operands])
    return hidden.transpose(1, 0, 2), memory.transpose(1, 0, 2)


def solution(mesh):
    placed = (
        P(("lat", "lon"), None, None),
        P(("lat", "lon"), None, None),
        P(("lat", "lon"), None, None, None, None),
        P(("lat", "lon"), None, None),
        P(("lat", "lon"), None),
        P(),
        P(),
        P(),
        P(None, "lat", "lon"),
        P(None, "lat", "lon"),
    )
    return jax.shard_map(
        on_device,
        mesh=mesh,
        in_specs=placed,
        out_specs=(P(None, "lat", "lon"), P(None, "lat", "lon")),
        check_vma=False,
    )
```

```python
import itertools
import random

import jax
import jax.numpy as jnp
import numpy as np
from jax import lax
from jax.experimental import pallas as pl
from jax.experimental.pallas import tpu as pltpu
from jax.sharding import PartitionSpec as P

STEPS = 3
MESH = pl.DeviceIdType.MESH
LOGICAL = pl.DeviceIdType.LOGICAL
F32 = jnp.float32
BF16 = jnp.bfloat16
PEERS = 128
SLOTS = 4
SIZES = (64, 32, 16, 16)
STARTS = (0, 64, 96, 112)
GROUP = 8
BARRIER_AT = 16
HALO = 3
ROWS = 32
COLS = 256
CH = 16
HID = 32


def send_order():
    offsets = [d for d in itertools.product(range(4), range(4), range(4), range(2)) if any(d)]
    random.Random(0).shuffle(offsets)
    return [(0, 0, 0, 0)] + offsets


ORDER = send_order()


def coords():
    i = lax.axis_index("lat")
    j = lax.axis_index("lon")
    return (lax.rem(lax.div(j, 2), 4), lax.div(i, 4) * 2 + lax.div(j, 8), lax.rem(i, 4), lax.rem(j, 2))


class Places:
    def __init__(self):
        x, y, z, c = coords()
        ys = [lax.rem(y + d, 4) for d in range(4)]
        self.x = [lax.rem(x + d, 4) * 2 for d in range(4)]
        self.y = [lax.div(v, 2) * 64 + lax.rem(v, 2) * 8 for v in ys]
        self.z = [lax.rem(z + d, 4) * 16 for d in range(4)]
        self.c = [lax.rem(c + d, 2) for d in range(2)]
        self.sums = {}

    def __call__(self, offset, sign=1):
        dx, dy, dz, dc = ((sign * d) % m for d, m in zip(offset, (4, 4, 4, 2)))
        key = (dy, dz, dc)
        if key not in self.sums:
            self.sums[key] = self.z[dz] + self.y[dy] + self.c[dc]
        return self.sums[key] + self.x[dx]


def lanes(shape):
    return lax.broadcasted_iota(jnp.int32, shape, len(shape) - 1)


def sublanes(shape):
    return lax.broadcasted_iota(jnp.int32, shape, len(shape) - 2)


def roll(x, shift):
    return pltpu.roll(x, shift, 1)


def band(n, to, to_index, tab, stab, x_ref, w_ref):
    tile = tab[n]
    lane = lanes((8, 128)) + sublanes((8, 128))
    inside = (lane >= 4) & (lane < 132)
    for s in range(SLOTS):
        x = x_ref[stab[0, s, tile]].astype(F32)
        w = jnp.where(inside, w_ref[tile, s].astype(F32), 0.0)
        total = w[4:5] * x
        for k in (0, 1, 2, 3, 5, 6, 7):
            total = total + w[k : k + 1] * roll(x, (4 - k) % 128)
        to[to_index, s] = total.astype(BF16)


def row_at(rows_ref, y, count):
    row = pl.ds(pl.multiple_of(y * count, count), count)
    return rows_ref[0, row], rows_ref[1, row]


def spread(halves, into, count, at):
    row = jnp.concatenate(halves, axis=1)
    where = pl.ds(at, COLS)
    into[0:count, where] = roll(row, 1).astype(BF16)
    into[count : 2 * count, where] = row.astype(BF16)
    into[2 * count : 3 * count, where] = roll(row, COLS - 1).astype(BF16)


def padded_at(y):
    return (y + HALO) * COLS if isinstance(y, int) else pl.multiple_of((y + HALO) * COLS, COLS)


class Picker:
    def __init__(self, left_lane, right_lane, count):
        self.left, self.right = left_lane, right_lane
        self.shape = (count, 128)

    def empty(self):
        return jnp.zeros(self.shape, F32), jnp.zeros(self.shape, F32)

    def take(self, state, halves):
        lane = lanes(self.shape)
        return (
            jnp.where(lane == self.left, halves[0], roll(state[0], 1)),
            jnp.where(lane == self.right, halves[1], roll(state[1], 1)),
        )

    def place(self, state, lowest=0, highest=ROWS - 1):
        lane = lanes(self.shape)
        left = roll(state[0], (lowest + HALO - self.left) % 128)
        right = roll(state[1], (lowest + HALO + 64 - self.right) % 128)
        first, last = lowest + HALO, highest + HALO
        return jnp.where(
            (lane >= first) & (lane <= last),
            left,
            jnp.where((lane >= first + 64) & (lane <= last + 64), right, 0.0),
        )

    def insert(self, value, y, halves):
        lane = lanes(self.shape)
        at = y + HALO
        value = jnp.where(lane == at, roll(halves[0], (at - self.left) % 128), value)
        return jnp.where(lane == at + 64, roll(halves[1], (at + 64 - self.right) % 128), value)


def stage(q_ref, row_of, depth, columns):
    top = [h for y in range(depth) for h in row_of(y)]
    bottom = [h for y in range(ROWS - depth, ROWS) for h in row_of(y)]
    for k, v in enumerate((*top, *columns, *bottom)):
        q_ref[k] = v.astype(BF16)


def swap(plan, q_ref, r_ref, send_sem, recv_sem):
    i = lax.axis_index("lat")
    j = lax.axis_index("lon")
    lat = {0: i, -1: lax.rem(i + 7, 8), 1: lax.rem(i + 1, 8)}
    lon = {0: j, -1: lax.rem(j + 15, 16), 1: lax.rem(j + 1, 16)}
    for di, dj, source, size, slot in plan:
        pltpu.make_async_remote_copy(
            src_ref=q_ref.at[pl.ds(source, size)],
            dst_ref=r_ref.at[pl.ds(slot, size)],
            send_sem=send_sem,
            recv_sem=recv_sem,
            device_id=(lat[di], lon[dj]),
            device_id_type=MESH,
        ).start()


DEEP = (
    (-1, 0, 0, 8, 8), (1, 0, 6, 8, 0), (0, -1, 6, 1, 17), (0, 1, 6, 1, 16),
    (-1, -1, 6, 1, 21), (-1, 1, 6, 1, 20), (1, -1, 6, 1, 19), (1, 1, 6, 1, 18),
)
CELLS = ((-1, 0, 0, 5, 5), (1, 0, 4, 5, 0))
SIDES = ((0, -1, 0, 1, 1), (0, 1, 0, 1, 0))


def whole(r_ref, send_sem, recv_sem):
    i = lax.axis_index("lat")
    return pltpu.make_async_remote_copy(
        src_ref=r_ref,
        dst_ref=r_ref,
        send_sem=send_sem,
        recv_sem=recv_sem,
        device_id=(lax.rem(i + 1, 8), lax.axis_index("lon")),
        device_id_type=MESH,
    )


def in_globe(y):
    i = lax.axis_index("lat")
    return ((y >= 0) | (i > 0)) & ((y < ROWS) | (i < 7))


def frame(count, middle, above, below):
    lane = lanes((count, 128))
    y = jnp.where(lane < 64, lane, lane - 64) - HALO
    live = in_globe(y) & (y < ROWS + HALO)
    picked = jnp.where(y < 0, roll(above, 96), jnp.where(y < ROWS, middle, roll(below, 32)))
    return jnp.where(live, picked, 0.0)


def taps_of(edges, nears, sides):
    half = lanes(edges.shape) < 64
    three = (jnp.where(half, sides, nears), edges, jnp.where(half, nears, sides))
    above = [roll(v, 1) for v in three]
    below = [roll(v, 127) for v in three]
    return jnp.concatenate([v.astype(BF16) for v in (*above, *three, *below)], axis=0)


def deep_taps(edge, near, r_ref, count):
    got = lambda k: r_ref[k].astype(F32)
    half = lanes((count, 128)) < 64
    swapped = [roll(jnp.where(half, got(k + 1), got(k)), 64) for k in (16, 18, 20)]
    return taps_of(
        frame(count, edge, got(0), got(14)), frame(count, near, got(1), got(15)), frame(count, *swapped)
    )


def halo_rows(r_ref, into, count):
    for slot, y in ((2, -3), (4, -2), (6, -1), (8, 32), (10, 33), (12, 34)):
        halves = [jnp.where(in_globe(y), r_ref[slot + k].astype(F32), 0.0) for k in range(2)]
        spread(halves, into, count, padded_at(y))


def update(gates, memory):
    ingate = jnp.tanh(gates[0:HID]) * 0.5 + 0.5
    forget = jnp.tanh(gates[HID : 2 * HID]) * 0.5 + 0.5
    outgate = jnp.tanh(gates[2 * HID : 3 * HID]) * 0.5 + 0.5
    memory = forget * memory + ingate * jnp.tanh(gates[3 * HID :])
    return outgate * jnp.tanh(memory), memory


def halves_of(v):
    return v[:, :128], v[:, 128:]


def body(
    stab_hbm, x_hbm, w_hbm, hid_hbm, cell_hbm, target_hbm, count_hbm, state_hbm, input_hbm, bias_hbm,
    hout_ref, cout_ref,
    tab, stab, x_ref, w_ref, hid_ref, cell_ref, target_ref, count_ref, state_ref, input_ref, bias_ref, weight, out_buf, in_buf, wide, sums, rows, s0, s1, fshifted, cells, ga, gb,
    qh, rh, qe, re, qf, rf, qc, rc, load_sem, far_send, far_recv, near_send, near_recv,
):
    loads = [
        pltpu.make_async_copy(a, b, load_sem.at[k])
        for k, (a, b) in enumerate(
            (
                (stab_hbm, stab), (x_hbm, x_ref), (w_hbm, w_ref), (hid_hbm, hid_ref), (cell_hbm, cell_ref),
                (target_hbm, target_ref), (count_hbm, count_ref), (state_hbm, state_ref), (input_hbm, input_ref),
                (bias_hbm, bias_ref),
            )
        )
    ]
    for copy in loads:
        copy.start()
    at = Places()
    barrier = pltpu.get_barrier_semaphore()
    tab[0] = at(ORDER[0])
    for offset in sorted(ORDER[1:], key=lambda d: -sum(min(a, 4 - a) for a in d[:3])):
        pl.semaphore_signal(barrier, inc=1, device_id=at(offset), device_id_type=LOGICAL)
    for n in range(1, PEERS):
        tab[n] = at(ORDER[n])
    for copy in loads[:3]:
        copy.wait()

    def one_band(n, carry):
        band(n, out_buf, n, tab, stab, x_ref, w_ref)
        return carry

    def send(first, last):
        for n in range(max(first, 1), last):
            chunk = max(k for k in range(len(SIZES)) if STARTS[k] <= n)
            pltpu.make_async_remote_copy(
                src_ref=out_buf.at[n],
                dst_ref=in_buf.at[n],
                send_sem=far_send,
                recv_sem=far_recv.at[chunk],
                device_id=at(ORDER[n]),
                device_id_type=LOGICAL,
            ).start()

    band(0, in_buf, 0, tab, stab, x_ref, w_ref)
    lax.fori_loop(1, GROUP, one_band, 0)
    for first in range(GROUP, PEERS, GROUP):
        lax.fori_loop(first, first + GROUP, one_band, 0)
        if first == BARRIER_AT:
            pl.semaphore_wait(barrier, PEERS - 1)
            send(0, first)
        elif first > BARRIER_AT:
            send(first - GROUP, first)
    send(PEERS - GROUP, PEERS)

    loads[3].wait()
    for c in range(HID):
        for half in range(2):
            rows[half, pl.ds(c, ROWS, stride=HID), :] = hid_ref[c, :, half * 128 : half * 128 + 128].astype(F32)
    outer, inner = Picker(0, 127, HID), Picker(1, 126, HID)

    def prepare(k, state):
        y = ROWS - 1 - k
        halves = row_at(rows, y, HID)
        spread(halves, s0, HID, padded_at(y))
        return outer.take(state[0], halves), inner.take(state[1], halves)

    state = lax.fori_loop(0, ROWS, prepare, (outer.empty(), inner.empty()), unroll=2)
    edge, near = outer.place(state[0]), inner.place(state[1])
    stage(qh, lambda y: row_at(rows, y, HID), HALO, (edge, near))
    swap(DEEP, qh, rh, near_send.at[0], near_recv.at[0])
    for copy in loads[4:]:
        copy.wait()
    for c in range(HID):
        for half in range(2):
            cells[half, pl.ds(c + 2 * HID, ROWS, stride=HID), :] = cell_ref[c, :, half * 128 : half * 128 + 128].astype(F32)

    def prepare_cell(k, state):
        return outer.take(state, row_at(cells, ROWS + 1 - k, HID))

    edge_cell = outer.place(lax.fori_loop(0, ROWS, prepare_cell, outer.empty(), unroll=2))

    stage(qc, lambda y: row_at(cells, y + 2, HID), 2, (edge_cell,))
    swap(CELLS, qc, rc, near_send.at[STEPS + 1], near_recv.at[STEPS + 1])

    scale = jnp.where(sublanes((128, 1)) < 3 * HID, 0.5, 1.0)
    bias = jnp.sum(jnp.where(sublanes((128, 128)) == lanes((128, 128)), bias_ref[...], 0.0), axis=1, keepdims=True)
    bias = bias * scale
    high = bias.astype(BF16).astype(F32)
    middle = (bias - high).astype(BF16).astype(F32)
    low = bias - high - middle
    lane = lanes((128, 128))
    extra = jnp.where(lane == 0, high, jnp.where(lane == 1, middle, jnp.where(lane == 2, low, 0.0)))
    taps = jnp.concatenate([state_ref[...].astype(F32), input_ref[...].astype(F32), extra.T[:80]], axis=0)
    deep = lax.broadcasted_iota(jnp.int32, (128, 128), 1)
    for k in range(4):
        part = taps[k * 128 : k * 128 + 128].T
        mult = jnp.where((deep + k * 128 < 432), scale, 1.0)
        weight[:, k * 128 : k * 128 + 128] = (part * mult).astype(BF16)
    ones = jnp.ones((16, COLS), BF16)

    counts = count_ref[...]
    aim4 = jnp.where(sublanes((SLOTS, 128)) < counts, target_ref[0], -1).astype(F32)
    aim8 = jnp.concatenate([aim4, aim4], axis=0).astype(BF16)
    sums[...] = jnp.zeros_like(sums)
    for g, (start, size) in enumerate(zip(STARTS, SIZES)):
        taken = size * SLOTS
        first = max(start, 1)
        got = in_buf.at[pl.ds(first, start + size - first)]
        pltpu.make_async_remote_copy(
            src_ref=got, dst_ref=got, send_sem=far_send, recv_sem=far_recv.at[g],
            device_id=at(ORDER[1]), device_id_type=LOGICAL,
        ).wait_recv()

        def unpack(n, carry):
            block = in_buf[start + n].astype(F32).reshape(SLOTS * CH, 128)
            wide[pl.ds(pl.multiple_of(n * SLOTS * CH, SLOTS * CH), SLOTS * CH)] = block
            return carry

        lax.fori_loop(0, size, unpack, 0, unroll=4)
        which = lax.shift_right_logical(lanes((1, taken)), 2)
        origin = jnp.zeros((1, taken), jnp.int32)
        for n in range(size):
            origin = jnp.where(which == n, at(ORDER[start + n], -1), origin)
        spot = (sublanes((128, taken)) == origin).astype(F32).astype(BF16)
        aims = jnp.dot(aim8, spot, preferred_element_type=F32)
        mine = sublanes((8, taken)) == lanes((8, taken)) % SLOTS
        aim = jnp.sum(jnp.where(mine, aims, 0.0), axis=0, keepdims=True)
        chosen = (sublanes((64, taken)).astype(F32) == aim).astype(F32).astype(BF16)
        for c in range(0, CH, 2):
            pair = [wide[pl.ds(c + k, taken, stride=CH), :].astype(BF16) for k in range(2)]
            part = jnp.dot(chosen, jnp.concatenate(pair, axis=1), preferred_element_type=F32)
            sums[c * 64 : c * 64 + 64] += part[:, :128]
            sums[c * 64 + 64 : c * 64 + 128] += part[:, 128:]

    def cell_row(y):
        return sums[pl.ds(2 * y, CH, stride=64), :], sums[pl.ds(2 * y + 1, CH, stride=64), :]

    fouter, finner = Picker(0, 127, CH), Picker(1, 126, CH)
    fedge = fnear = jnp.zeros((CH, 128), F32)
    for y in range(ROWS):
        halves = cell_row(y)
        fedge = fouter.insert(fedge, y, halves)
        fnear = finner.insert(fnear, y, halves)
    stage(qf, cell_row, HALO, (fedge, fnear))
    swap(DEEP, qf, rf, near_send.at[STEPS], near_recv.at[STEPS])
    for y in range(ROWS):
        spread(cell_row(y), fshifted, CH, padded_at(y))

    fmini = None
    for t in range(STEPS):
        here, there = (s0, s1) if t % 2 == 0 else (s1, s0)
        last = t == STEPS - 1

        def gates_of(y, count=1):
            spans = [pl.ds(padded_at(y - 1 + a), COLS * count) for a in range(3)]
            fixed = jnp.ones((16, COLS * count), BF16)
            rhs = jnp.concatenate([here[:, w] for w in spans] + [fshifted[:, w] for w in spans] + [fixed], axis=0)
            return jnp.dot(weight[:, :448], rhs, preferred_element_type=F32)

        def finish_row(y, gates):
            hidden, memory = update(gates, jnp.concatenate(row_at(cells, y + 2, HID), axis=1))
            if not (isinstance(y, int) and 0 <= y < ROWS):
                hidden = jnp.where(in_globe(y), hidden, 0.0) if isinstance(y, int) else hidden
            halves = halves_of(hidden)
            for half, v in enumerate(halves_of(memory)):
                if last:
                    part = slice(half * 128, half * 128 + 128)
                    hout_ref[y, :, part] = halves[half].astype(BF16)
                    cout_ref[y, :, part] = v.astype(BF16)
                else:
                    cells[half, (y + 2) * HID : (y + 3) * HID] = v
            if not last:
                spread(halves, there, HID, padded_at(y))
            return halves

        depth = STEPS - t
        lowest, highest = (1, ROWS - 2) if t == 0 else (1 - depth, ROWS - 2 + depth)
        count = (highest - lowest + 1) // 2
        wide_gates = count * COLS
        state = inner.empty()
        ga[:, :wide_gates] = gates_of(lowest + count, count)
        gb[:, :wide_gates] = gates_of(lowest, count)
        for buffer, start in ((ga, lowest + count), (gb, lowest)):
            for r in range(count - 1, -1, -1):
                halves = finish_row(start + r, buffer[:, r * COLS : r * COLS + COLS])
                state = state if last else inner.take(state, halves)

        if t == 0:
            for k, got in ((0, rh), (STEPS + 1, rc), (STEPS, rf)):
                whole(got, near_send.at[k], near_recv.at[k]).wait_recv()
            halo_rows(rh, here, HID)
            halo_rows(rf, fshifted, CH)
            for slot, y in ((1, -2), (3, -1), (5, 32), (7, 33)):
                for half in range(2):
                    cells[half, (y + 2) * HID : (y + 3) * HID] = rc[slot + half].astype(F32)
            edge_cell = frame(HID, edge_cell, rc[0].astype(F32), rc[9].astype(F32))
            fmini = deep_taps(fedge, fnear, rf, CH)
            low, high = gates_of(1 - depth, depth), gates_of(ROWS - 1, depth)
            above = [finish_row(-r, low[:, (depth - 1 - r) * COLS : (depth - r) * COLS]) for r in range(depth)]
            below = [finish_row(ROWS - 1 + r, high[:, r * COLS : (r + 1) * COLS]) for r in range(depth)]
            mini = deep_taps(edge, near, rh, HID)
        else:
            whole(re.at[t - 1], near_send.at[t], near_recv.at[t]).wait_recv()
            half = lanes((HID, 128)) < 64
            sides = roll(jnp.where(half, re[t - 1, 1].astype(F32), re[t - 1, 0].astype(F32)), 64)
            mini = taps_of(edge, near, sides)
        mini = jnp.concatenate([mini, fmini, ones[:, :128]], axis=0)
        gates = jnp.dot(weight[:, :448], mini, preferred_element_type=F32)
        edge, edge_cell = update(gates, edge_cell)
        if last:
            break
        lane = lanes((HID, 128))
        edge = jnp.where(in_globe(jnp.where(lane < 64, lane, lane - 64) - HALO), edge, 0.0)
        qe[t, 0] = edge.astype(BF16)
        if t == 0:
            for halves in above:
                state = inner.take(state, halves)
        near = inner.place(state, 1 - depth, highest)
        if t == 0:
            for r, halves in enumerate(below):
                near = inner.insert(near, ROWS - 1 + r, halves)
        left = {y: roll(edge, (1 - HALO - y) % 128).astype(BF16) for y in range(1 - depth, ROWS + depth)}
        right = {y: roll(edge, (63 - HALO - y) % 128).astype(BF16) for y in range(1 - depth, ROWS + depth)}
        swap(SIDES, qe.at[t], re.at[t], near_send.at[t + 1], near_recv.at[t + 1])
        for y in range(1 - depth, ROWS + depth - 1):
            first = pl.ds(padded_at(y), 128)
            second = pl.ds(padded_at(y) + 128, 128)
            for block_at, where, spot, value in (
                (0, first, 1, left[y]), (1, first, 0, left[y + 1]),
                (1, second, 127, right[y]), (2, second, 126, right[y + 1]),
            ):
                part = there.at[block_at * HID : block_at * HID + HID, where]
                part[...] = jnp.where(lane == spot, value, part[...])

    lane = lanes((HID, 128))
    for columns, to in ((edge, hout_ref), (edge_cell, cout_ref)):
        for y in range(ROWS):
            left = roll(columns, (-(y + HALO)) % 128).astype(BF16)
            right = roll(columns, (63 - HALO - y) % 128).astype(BF16)
            to[y, :, :128] = jnp.where(lane == 0, left, to[y, :, :128])
            to[y, :, 128:] = jnp.where(lane == 127, right, to[y, :, 128:])

    sent = out_buf.at[pl.ds(1, PEERS - 1)]
    pltpu.make_async_remote_copy(
        src_ref=sent, dst_ref=sent, send_sem=far_send, recv_sem=far_recv.at[0],
        device_id=at(ORDER[1]), device_id_type=LOGICAL,
    ).wait_send()
    for k, got in ((0, rh), (1, re.at[0]), (2, re.at[1]), (STEPS, rf), (STEPS + 1, rc)):
        whole(got, near_send.at[k], near_recv.at[k]).wait_send()


def in_hbm(x):
    return pltpu.with_memory_space_constraint(x, pltpu.HBM)


def on_device(
    satellite_blocks, slot_source, slot_weight, slot_target, tile_counts,
    gate_input_weight, gate_state_weight, gate_bias, hidden_init, cell_init,
):
    operands = (
        slot_source.transpose(0, 2, 1), satellite_blocks, slot_weight[0], hidden_init, cell_init,
        slot_target.transpose(0, 2, 1), tile_counts, gate_state_weight.T, gate_input_weight.T, gate_bias.reshape(1, -1),
    )
    vmem = pl.BlockSpec(memory_space=pltpu.VMEM)
    hbm = pl.BlockSpec(memory_space=pltpu.HBM)
    padded = (ROWS + 2 * HALO) * COLS
    hidden, memory = pl.pallas_call(
        body,
        out_shape=[jax.ShapeDtypeStruct((ROWS, HID, COLS), BF16)] * 2,
        in_specs=[hbm] * 10,
        out_specs=[vmem, vmem],
        scratch_shapes=[
            pltpu.SMEM((PEERS,), jnp.int32),
            pltpu.SMEM((1, SLOTS, PEERS), jnp.int32),
            pltpu.VMEM((PEERS, CH, 128), BF16),
            pltpu.VMEM((PEERS, SLOTS, 8, 128), BF16),
            pltpu.VMEM((HID, ROWS, COLS), BF16),
            pltpu.VMEM((HID, ROWS, COLS), BF16),
            pltpu.VMEM((1, SLOTS, PEERS), jnp.int32),
            pltpu.VMEM((1, PEERS), jnp.int32),
            pltpu.VMEM((9 * HID, 128), BF16),
            pltpu.VMEM((9 * CH, 128), BF16),
            pltpu.VMEM((1, 128), F32),
            pltpu.VMEM((128, 512), BF16),
            pltpu.VMEM((PEERS, SLOTS, CH, 128), BF16),
            pltpu.VMEM((PEERS, SLOTS, CH, 128), BF16),
            pltpu.VMEM((max(SIZES) * SLOTS * CH, 128), F32),
            pltpu.VMEM((CH * 64, 128), F32),
            pltpu.VMEM((2, ROWS * HID, 128), F32),
            pltpu.VMEM((3 * HID, padded), BF16),
            pltpu.VMEM((3 * HID, padded), BF16),
            pltpu.VMEM((3 * CH, padded), BF16),
            pltpu.VMEM((2, (ROWS + 4) * HID, 128), F32),
            pltpu.VMEM((128, COLS * (ROWS // 2 + 1)), F32),
            pltpu.VMEM((128, COLS * (ROWS // 2 + 1)), F32),
            pltpu.VMEM((14, HID, 128), BF16),
            pltpu.VMEM((22, HID, 128), BF16),
            pltpu.VMEM((2, 1, HID, 128), BF16),
            pltpu.VMEM((2, 2, HID, 128), BF16),
            pltpu.VMEM((14, CH, 128), BF16),
            pltpu.VMEM((22, CH, 128), BF16),
            pltpu.VMEM((9, HID, 128), BF16),
            pltpu.VMEM((10, HID, 128), BF16),
            pltpu.SemaphoreType.DMA((10,)),
            pltpu.SemaphoreType.DMA,
            pltpu.SemaphoreType.DMA((len(SIZES),)),
            pltpu.SemaphoreType.DMA((STEPS + 2,)),
            pltpu.SemaphoreType.DMA((STEPS + 2,)),
        ],
        compiler_params=pltpu.CompilerParams(
            collective_id=0, has_side_effects=True, vmem_limit_bytes=30 * 2**20
        ),
        name="reproject_and_step",
    )(*[in_hbm(v) for v in operands])
    return hidden.transpose(1, 0, 2), memory.transpose(1, 0, 2)


def solution(mesh):
    placed = (
        P(("lat", "lon"), None, None),
        P(("lat", "lon"), None, None),
        P(("lat", "lon"), None, None, None, None),
        P(("lat", "lon"), None, None),
        P(("lat", "lon"), None),
        P(),
        P(),
        P(),
        P(None, "lat", "lon"),
        P(None, "lat", "lon"),
    )
    return jax.shard_map(
        on_device,
        mesh=mesh,
        in_specs=placed,
        out_specs=(P(None, "lat", "lon"), P(None, "lat", "lon")),
        check_vma=False,
    )
```

```python
import itertools
import random

import jax
import jax.numpy as jnp
import numpy as np
from jax import lax
from jax.experimental import pallas as pl
from jax.experimental.pallas import tpu as pltpu
from jax.sharding import PartitionSpec as P

STEPS = 3
MESH = pl.DeviceIdType.MESH
LOGICAL = pl.DeviceIdType.LOGICAL
F32 = jnp.float32
BF16 = jnp.bfloat16
PEERS = 128
SLOTS = 4
SIZES = (64, 32, 16, 16)
STARTS = (0, 64, 96, 112)
GROUP = 8
BARRIER_AT = 16
BLOCK = 5
HALO = 3
ROWS = 32
COLS = 256
CH = 16
HID = 32


def send_order():
    offsets = [d for d in itertools.product(range(4), range(4), range(4), range(2)) if any(d)]
    random.Random(0).shuffle(offsets)
    return [(0, 0, 0, 0)] + offsets


ORDER = send_order()


def coords():
    i = lax.axis_index("lat")
    j = lax.axis_index("lon")
    return (lax.rem(lax.div(j, 2), 4), lax.div(i, 4) * 2 + lax.div(j, 8), lax.rem(i, 4), lax.rem(j, 2))


class Places:
    def __init__(self):
        x, y, z, c = coords()
        ys = [lax.rem(y + d, 4) for d in range(4)]
        self.x = [lax.rem(x + d, 4) * 2 for d in range(4)]
        self.y = [lax.div(v, 2) * 64 + lax.rem(v, 2) * 8 for v in ys]
        self.z = [lax.rem(z + d, 4) * 16 for d in range(4)]
        self.c = [lax.rem(c + d, 2) for d in range(2)]
        self.sums = {}

    def __call__(self, offset, sign=1):
        dx, dy, dz, dc = ((sign * d) % m for d, m in zip(offset, (4, 4, 4, 2)))
        key = (dy, dz, dc)
        if key not in self.sums:
            self.sums[key] = self.z[dz] + self.y[dy] + self.c[dc]
        return self.sums[key] + self.x[dx]


def lanes(shape):
    return lax.broadcasted_iota(jnp.int32, shape, len(shape) - 1)


def sublanes(shape):
    return lax.broadcasted_iota(jnp.int32, shape, len(shape) - 2)


def roll(x, shift):
    return pltpu.roll(x, shift, 1)


def band(n, to, to_index, tab, stab, x_ref, w_ref):
    tile = tab[n]
    lane = lanes((8, 128)) + sublanes((8, 128))
    inside = (lane >= 4) & (lane < 132)
    for s in range(SLOTS):
        x = x_ref[stab[0, s, tile]].astype(F32)
        w = jnp.where(inside, w_ref[tile, s].astype(F32), 0.0)
        total = w[4:5] * x
        for k in (0, 1, 2, 3, 5, 6, 7):
            total = total + w[k : k + 1] * roll(x, (4 - k) % 128)
        to[to_index, s] = total.astype(BF16)


def row_at(rows_ref, y, count):
    row = pl.ds(pl.multiple_of(y * count, count), count)
    return rows_ref[0, row], rows_ref[1, row]


def spread(halves, into, count, at):
    row = jnp.concatenate(halves, axis=1).astype(BF16)
    where = pl.ds(at, COLS)
    into[0:count, where] = roll(row, 1)
    into[count : 2 * count, where] = row
    into[2 * count : 3 * count, where] = roll(row, COLS - 1)


def padded_at(y):
    return (y + HALO) * COLS if isinstance(y, int) else pl.multiple_of((y + HALO) * COLS, COLS)


class Picker:
    def __init__(self, left_lane, right_lane, count):
        self.left, self.right = left_lane, right_lane
        self.shape = (count, 128)

    def empty(self):
        return jnp.zeros(self.shape, F32), jnp.zeros(self.shape, F32)

    def take(self, state, halves):
        lane = lanes(self.shape)
        return (
            jnp.where(lane == self.left, halves[0], roll(state[0], 1)),
            jnp.where(lane == self.right, halves[1], roll(state[1], 1)),
        )

    def place(self, state, lowest=0):
        lane = lanes(self.shape)
        left = roll(state[0], (lowest + HALO - self.left) % 128)
        right = roll(state[1], (lowest + HALO + 64 - self.right) % 128)
        first, last = lowest + HALO, HALO + ROWS - 1
        return jnp.where(
            (lane >= first) & (lane <= last),
            left,
            jnp.where((lane >= first + 64) & (lane <= last + 64), right, 0.0),
        )

    def insert(self, value, y, halves):
        lane = lanes(self.shape)
        at = y + HALO
        value = jnp.where(lane == at, roll(halves[0], (at - self.left) % 128), value)
        return jnp.where(lane == at + 64, roll(halves[1], (at + 64 - self.right) % 128), value)


def corners(edge, y, halves):
    lane = lanes(edge.shape)
    left = roll(edge, (-(y + HALO)) % 128)
    right = roll(edge, (63 - HALO - y) % 128)
    return jnp.where(lane == 0, left, halves[0]), jnp.where(lane == 127, right, halves[1])


def stage(q_ref, row_of, depth, columns):
    top = [h for y in range(depth) for h in row_of(y)]
    bottom = [h for y in range(ROWS - depth, ROWS) for h in row_of(y)]
    for k, v in enumerate((*top, *columns, *bottom)):
        q_ref[k] = v.astype(BF16)


def swap(plan, q_ref, r_ref, send_sem, recv_sem):
    i = lax.axis_index("lat")
    j = lax.axis_index("lon")
    lat = {0: i, -1: lax.rem(i + 7, 8), 1: lax.rem(i + 1, 8)}
    lon = {0: j, -1: lax.rem(j + 15, 16), 1: lax.rem(j + 1, 16)}
    for di, dj, source, size, slot in plan:
        pltpu.make_async_remote_copy(
            src_ref=q_ref.at[pl.ds(source, size)],
            dst_ref=r_ref.at[pl.ds(slot, size)],
            send_sem=send_sem,
            recv_sem=recv_sem,
            device_id=(lat[di], lon[dj]),
            device_id_type=MESH,
        ).start()


DEEP = (
    (-1, 0, 0, 8, 8), (1, 0, 6, 8, 0), (0, -1, 6, 1, 17), (0, 1, 6, 1, 16),
    (-1, -1, 6, 1, 21), (-1, 1, 6, 1, 20), (1, -1, 6, 1, 19), (1, 1, 6, 1, 18),
)
CELLS = ((-1, 0, 0, 5, 5), (1, 0, 4, 5, 0))
SIDES = ((0, -1, 0, 1, 1), (0, 1, 0, 1, 0))


def whole(r_ref, send_sem, recv_sem):
    i = lax.axis_index("lat")
    return pltpu.make_async_remote_copy(
        src_ref=r_ref,
        dst_ref=r_ref,
        send_sem=send_sem,
        recv_sem=recv_sem,
        device_id=(lax.rem(i + 1, 8), lax.axis_index("lon")),
        device_id_type=MESH,
    )


def in_globe(y):
    i = lax.axis_index("lat")
    return ((y >= 0) | (i > 0)) & ((y < ROWS) | (i < 7))


def frame(count, middle, above, below):
    lane = lanes((count, 128))
    y = jnp.where(lane < 64, lane, lane - 64) - HALO
    live = in_globe(y) & (y < ROWS + HALO)
    picked = jnp.where(y < 0, roll(above, 96), jnp.where(y < ROWS, middle, roll(below, 32)))
    return jnp.where(live, picked, 0.0)


def taps_of(edges, nears, sides):
    half = lanes(edges.shape) < 64
    three = (jnp.where(half, sides, nears), edges, jnp.where(half, nears, sides))
    above = [roll(v, 1) for v in three]
    below = [roll(v, 127) for v in three]
    return jnp.concatenate([v.astype(BF16) for v in (*above, *three, *below)], axis=0)


def deep_taps(edge, near, r_ref, count):
    got = lambda k: r_ref[k].astype(F32)
    half = lanes((count, 128)) < 64
    swapped = [roll(jnp.where(half, got(k + 1), got(k)), 64) for k in (16, 18, 20)]
    return taps_of(
        frame(count, edge, got(0), got(14)), frame(count, near, got(1), got(15)), frame(count, *swapped)
    )


def halo_rows(r_ref, into, count):
    for slot, y in ((2, -3), (4, -2), (6, -1), (8, 32), (10, 33), (12, 34)):
        halves = [jnp.where(in_globe(y), r_ref[slot + k].astype(F32), 0.0) for k in range(2)]
        spread(halves, into, count, padded_at(y))


def update(gates, memory):
    ingate = jnp.tanh(gates[0:HID]) * 0.5 + 0.5
    forget = jnp.tanh(gates[HID : 2 * HID]) * 0.5 + 0.5
    outgate = jnp.tanh(gates[2 * HID : 3 * HID]) * 0.5 + 0.5
    memory = forget * memory + ingate * jnp.tanh(gates[3 * HID :])
    return outgate * jnp.tanh(memory), memory


def halves_of(v):
    return v[:, :128], v[:, 128:]


def body(
    stab_hbm, x_hbm, w_hbm, hid_hbm, cell_hbm, target_hbm, count_hbm, state_hbm, input_hbm, bias_hbm,
    hout_ref, cout_ref,
    tab, stab, x_ref, w_ref, hid_ref, cell_ref, target_ref, count_ref, state_ref, input_ref, bias_ref, weight, out_buf, in_buf, wide, sums, rows, s0, s1, fshifted, cells, ga, gb,
    qh, rh, qe, re, qf, rf, qc, rc, load_sem, far_send, far_recv, near_send, near_recv,
):
    loads = [
        pltpu.make_async_copy(a, b, load_sem.at[k])
        for k, (a, b) in enumerate(
            (
                (stab_hbm, stab), (x_hbm, x_ref), (w_hbm, w_ref), (hid_hbm, hid_ref), (cell_hbm, cell_ref),
                (target_hbm, target_ref), (count_hbm, count_ref), (state_hbm, state_ref), (input_hbm, input_ref),
                (bias_hbm, bias_ref),
            )
        )
    ]
    for copy in loads:
        copy.start()
    at = Places()
    barrier = pltpu.get_barrier_semaphore()
    tab[0] = at(ORDER[0])
    for offset in sorted(ORDER[1:], key=lambda d: -sum(min(a, 4 - a) for a in d[:3])):
        pl.semaphore_signal(barrier, inc=1, device_id=at(offset), device_id_type=LOGICAL)
    for n in range(1, PEERS):
        tab[n] = at(ORDER[n])
    for copy in loads[:3]:
        copy.wait()

    def one_band(n, carry):
        band(n, out_buf, n, tab, stab, x_ref, w_ref)
        return carry

    def send(first, last):
        for n in range(max(first, 1), last):
            chunk = max(k for k in range(len(SIZES)) if STARTS[k] <= n)
            pltpu.make_async_remote_copy(
                src_ref=out_buf.at[n],
                dst_ref=in_buf.at[n],
                send_sem=far_send,
                recv_sem=far_recv.at[chunk],
                device_id=at(ORDER[n]),
                device_id_type=LOGICAL,
            ).start()

    band(0, in_buf, 0, tab, stab, x_ref, w_ref)
    lax.fori_loop(1, GROUP, one_band, 0)
    for first in range(GROUP, PEERS, GROUP):
        lax.fori_loop(first, first + GROUP, one_band, 0)
        if first == BARRIER_AT:
            pl.semaphore_wait(barrier, PEERS - 1)
            send(0, first)
        elif first > BARRIER_AT:
            send(first - GROUP, first)
    send(PEERS - GROUP, PEERS)

    loads[3].wait()
    for c in range(HID):
        for half in range(2):
            rows[half, pl.ds(c, ROWS, stride=HID), :] = hid_ref[c, :, half * 128 : half * 128 + 128].astype(F32)
    outer, inner = Picker(0, 127, HID), Picker(1, 126, HID)

    def prepare(k, state):
        y = ROWS - 1 - k
        halves = row_at(rows, y, HID)
        spread(halves, s0, HID, padded_at(y))
        return outer.take(state[0], halves), inner.take(state[1], halves)

    state = lax.fori_loop(0, ROWS, prepare, (outer.empty(), inner.empty()), unroll=2)
    edge, near = outer.place(state[0]), inner.place(state[1])
    stage(qh, lambda y: row_at(rows, y, HID), HALO, (edge, near))
    swap(DEEP, qh, rh, near_send.at[0], near_recv.at[0])
    for copy in loads[4:]:
        copy.wait()
    for c in range(HID):
        for half in range(2):
            cells[half, pl.ds(c + 2 * HID, ROWS, stride=HID), :] = cell_ref[c, :, half * 128 : half * 128 + 128].astype(F32)

    def prepare_cell(k, state):
        return outer.take(state, row_at(cells, ROWS + 1 - k, HID))

    edge_cell = outer.place(lax.fori_loop(0, ROWS, prepare_cell, outer.empty(), unroll=2))

    stage(qc, lambda y: row_at(cells, y + 2, HID), 2, (edge_cell,))
    swap(CELLS, qc, rc, near_send.at[STEPS + 1], near_recv.at[STEPS + 1])

    scale = jnp.where(sublanes((128, 1)) < 3 * HID, 0.5, 1.0)
    bias = jnp.sum(jnp.where(sublanes((128, 128)) == lanes((128, 128)), bias_ref[...], 0.0), axis=1, keepdims=True)
    bias = bias * scale
    high = bias.astype(BF16).astype(F32)
    middle = (bias - high).astype(BF16).astype(F32)
    low = bias - high - middle
    lane = lanes((128, 128))
    extra = jnp.where(lane == 0, high, jnp.where(lane == 1, middle, jnp.where(lane == 2, low, 0.0)))
    taps = jnp.concatenate([state_ref[...].astype(F32), input_ref[...].astype(F32), extra.T[:80]], axis=0)
    deep = lax.broadcasted_iota(jnp.int32, (128, 128), 1)
    for k in range(4):
        part = taps[k * 128 : k * 128 + 128].T
        mult = jnp.where((deep + k * 128 < 432), scale, 1.0)
        weight[:, k * 128 : k * 128 + 128] = (part * mult).astype(BF16)
    ones = jnp.ones((16, COLS), BF16)

    counts = count_ref[...]
    aim4 = jnp.where(sublanes((SLOTS, 128)) < counts, target_ref[0], -1).astype(F32)
    aim8 = jnp.concatenate([aim4, aim4], axis=0).astype(BF16)
    sums[...] = jnp.zeros_like(sums)
    for g, (start, size) in enumerate(zip(STARTS, SIZES)):
        taken = size * SLOTS
        first = max(start, 1)
        got = in_buf.at[pl.ds(first, start + size - first)]
        pltpu.make_async_remote_copy(
            src_ref=got, dst_ref=got, send_sem=far_send, recv_sem=far_recv.at[g],
            device_id=at(ORDER[1]), device_id_type=LOGICAL,
        ).wait_recv()

        def unpack(n, carry):
            block = in_buf[start + n].astype(F32).reshape(SLOTS * CH, 128)
            wide[pl.ds(pl.multiple_of(n * SLOTS * CH, SLOTS * CH), SLOTS * CH)] = block
            return carry

        lax.fori_loop(0, size, unpack, 0, unroll=4)
        which = lax.shift_right_logical(lanes((1, taken)), 2)
        origin = jnp.zeros((1, taken), jnp.int32)
        for n in range(size):
            origin = jnp.where(which == n, at(ORDER[start + n], -1), origin)
        spot = (sublanes((128, taken)) == origin).astype(F32).astype(BF16)
        aims = jnp.dot(aim8, spot, preferred_element_type=F32)
        mine = sublanes((8, taken)) == lanes((8, taken)) % SLOTS
        aim = jnp.sum(jnp.where(mine, aims, 0.0), axis=0, keepdims=True)
        chosen = (sublanes((64, taken)).astype(F32) == aim).astype(F32).astype(BF16)
        for c in range(0, CH, 2):
            pair = [wide[pl.ds(c + k, taken, stride=CH), :].astype(BF16) for k in range(2)]
            part = jnp.dot(chosen, jnp.concatenate(pair, axis=1), preferred_element_type=F32)
            sums[c * 64 : c * 64 + 64] += part[:, :128]
            sums[c * 64 + 64 : c * 64 + 128] += part[:, 128:]

    def cell_row(y):
        return sums[pl.ds(2 * y, CH, stride=64), :], sums[pl.ds(2 * y + 1, CH, stride=64), :]

    fouter, finner = Picker(0, 127, CH), Picker(1, 126, CH)
    fedge = fnear = jnp.zeros((CH, 128), F32)
    for y in range(ROWS):
        halves = cell_row(y)
        fedge = fouter.insert(fedge, y, halves)
        fnear = finner.insert(fnear, y, halves)
    stage(qf, cell_row, HALO, (fedge, fnear))
    swap(DEEP, qf, rf, near_send.at[STEPS], near_recv.at[STEPS])

    def spread_cells(y, carry):
        spread(cell_row(y), fshifted, CH, padded_at(y))
        return carry

    lax.fori_loop(0, ROWS, spread_cells, 0, unroll=4)

    fmini = None
    for t in range(STEPS):
        here, there = (s0, s1) if t % 2 == 0 else (s1, s0)
        last = t == STEPS - 1

        def gates_of(y, count=1):
            spans = [pl.ds(padded_at(y - 1 + a), COLS * count) for a in range(3)]
            fixed = jnp.ones((16, COLS * count), BF16)
            rhs = jnp.concatenate([here[:, w] for w in spans] + [fshifted[:, w] for w in spans] + [fixed], axis=0)
            return jnp.dot(weight[:, :448], rhs, preferred_element_type=F32)

        def finish_row(y, gates):
            hidden, memory = update(gates, jnp.concatenate(row_at(cells, y + 2, HID), axis=1))
            if not (isinstance(y, int) and 0 <= y < ROWS):
                hidden = jnp.where(in_globe(y), hidden, 0.0) if isinstance(y, int) else hidden
            halves = halves_of(hidden)
            for half, v in enumerate(halves_of(memory)):
                if last:
                    part = slice(half * 128, half * 128 + 128)
                    hout_ref[y, :, part] = halves[half].astype(BF16)
                    cout_ref[y, :, part] = v.astype(BF16)
                else:
                    cells[half, pl.ds(pl.multiple_of((y + 2) * HID, HID), HID)] = v
            if not last:
                spread(halves, there, HID, padded_at(y))
            return halves

        def block(low, buffer, state):
            for r in range(BLOCK - 1, -1, -1):
                halves = finish_row(low + r, buffer[:, r * COLS : r * COLS + COLS])
                state = state if last else inner.take(state, halves)
            return state

        def inside(k, state):
            low = ROWS - 1 - BLOCK - 2 * BLOCK * k
            gb[...] = gates_of(low - BLOCK, BLOCK)
            state = block(low, ga, state)
            ga[...] = gates_of(lax.max(low - 2 * BLOCK, 1), BLOCK)
            return block(low - BLOCK, gb, state)

        ga[...] = gates_of(ROWS - 1 - BLOCK, BLOCK)
        state = 0 if last else inner.empty()
        state = lax.fori_loop(0, (ROWS - 2) // (2 * BLOCK), inside, state)

        if t == 0:
            for k, got in ((0, rh), (STEPS + 1, rc)):
                whole(got, near_send.at[k], near_recv.at[k]).wait_recv()
            halo_rows(rh, here, HID)
            for slot, y in ((1, -2), (3, -1), (5, 32), (7, 33)):
                for half in range(2):
                    cells[half, (y + 2) * HID : (y + 3) * HID] = rc[slot + half].astype(F32)
            edge_cell = frame(HID, edge_cell, rc[0].astype(F32), rc[9].astype(F32))
            mini = deep_taps(edge, near, rh, HID)
            whole(rf, near_send.at[STEPS], near_recv.at[STEPS]).wait_recv()
            halo_rows(rf, fshifted, CH)
            fmini = deep_taps(fedge, fnear, rf, CH)
        depth = STEPS - t
        low, high = gates_of(1 - depth, depth), gates_of(ROWS - 1, depth)
        above = [finish_row(-r, low[:, (depth - 1 - r) * COLS : (depth - r) * COLS]) for r in range(depth)]
        below = [finish_row(ROWS - 1 + r, high[:, r * COLS : (r + 1) * COLS]) for r in range(depth)]
        if t > 0:
            whole(re.at[t - 1], near_send.at[t], near_recv.at[t]).wait_recv()
            half = lanes((HID, 128)) < 64
            sides = roll(jnp.where(half, re[t - 1, 1].astype(F32), re[t - 1, 0].astype(F32)), 64)
            mini = taps_of(edge, near, sides)
        mini = jnp.concatenate([mini, fmini, ones[:, :128]], axis=0)
        gates = jnp.dot(weight[:, :448], mini, preferred_element_type=F32)
        edge, edge_cell = update(gates, edge_cell)
        if last:
            break
        lane = lanes((HID, 128))
        edge = jnp.where(in_globe(jnp.where(lane < 64, lane, lane - 64) - HALO), edge, 0.0)
        qe[t, 0] = edge.astype(BF16)
        for halves in above:
            state = inner.take(state, halves)
        near = inner.place(state, 1 - depth)
        near = jnp.where((lane == 34) | (lane == 98), 0.0, near)
        for r, halves in enumerate(below):
            near = inner.insert(near, ROWS - 1 + r, halves)
        left = {y: roll(edge, (1 - HALO - y) % 128).astype(BF16) for y in range(1 - depth, ROWS + depth)}
        right = {y: roll(edge, (63 - HALO - y) % 128).astype(BF16) for y in range(1 - depth, ROWS + depth)}
        swap(SIDES, qe.at[t], re.at[t], near_send.at[t + 1], near_recv.at[t + 1])
        for y in range(1 - depth, ROWS + depth - 1):
            first = pl.ds(padded_at(y), 128)
            second = pl.ds(padded_at(y) + 128, 128)
            for block_at, where, spot, value in (
                (0, first, 1, left[y]), (1, first, 0, left[y + 1]),
                (1, second, 127, right[y]), (2, second, 126, right[y + 1]),
            ):
                part = there.at[block_at * HID : block_at * HID + HID, where]
                part[...] = jnp.where(lane == spot, value, part[...])

    lane = lanes((HID, 128))
    for columns, to in ((edge, hout_ref), (edge_cell, cout_ref)):
        for y in range(ROWS):
            left = roll(columns, (-(y + HALO)) % 128).astype(BF16)
            right = roll(columns, (63 - HALO - y) % 128).astype(BF16)
            to[y, :, :128] = jnp.where(lane == 0, left, to[y, :, :128])
            to[y, :, 128:] = jnp.where(lane == 127, right, to[y, :, 128:])

    sent = out_buf.at[pl.ds(1, PEERS - 1)]
    pltpu.make_async_remote_copy(
        src_ref=sent, dst_ref=sent, send_sem=far_send, recv_sem=far_recv.at[0],
        device_id=at(ORDER[1]), device_id_type=LOGICAL,
    ).wait_send()
    for k, got in ((0, rh), (1, re.at[0]), (2, re.at[1]), (STEPS, rf), (STEPS + 1, rc)):
        whole(got, near_send.at[k], near_recv.at[k]).wait_send()


def in_hbm(x):
    return pltpu.with_memory_space_constraint(x, pltpu.HBM)


def on_device(
    satellite_blocks, slot_source, slot_weight, slot_target, tile_counts,
    gate_input_weight, gate_state_weight, gate_bias, hidden_init, cell_init,
):
    operands = (
        slot_source.transpose(0, 2, 1), satellite_blocks, slot_weight[0], hidden_init, cell_init,
        slot_target.transpose(0, 2, 1), tile_counts, gate_state_weight.T, gate_input_weight.T, gate_bias.reshape(1, -1),
    )
    vmem = pl.BlockSpec(memory_space=pltpu.VMEM)
    hbm = pl.BlockSpec(memory_space=pltpu.HBM)
    padded = (ROWS + 2 * HALO) * COLS
    hidden, memory = pl.pallas_call(
        body,
        out_shape=[jax.ShapeDtypeStruct((ROWS, HID, COLS), BF16)] * 2,
        in_specs=[hbm] * 10,
        out_specs=[vmem, vmem],
        scratch_shapes=[
            pltpu.SMEM((PEERS,), jnp.int32),
            pltpu.SMEM((1, SLOTS, PEERS), jnp.int32),
            pltpu.VMEM((PEERS, CH, 128), BF16),
            pltpu.VMEM((PEERS, SLOTS, 8, 128), BF16),
            pltpu.VMEM((HID, ROWS, COLS), BF16),
            pltpu.VMEM((HID, ROWS, COLS), BF16),
            pltpu.VMEM((1, SLOTS, PEERS), jnp.int32),
            pltpu.VMEM((1, PEERS), jnp.int32),
            pltpu.VMEM((9 * HID, 128), BF16),
            pltpu.VMEM((9 * CH, 128), BF16),
            pltpu.VMEM((1, 128), F32),
            pltpu.VMEM((128, 512), BF16),
            pltpu.VMEM((PEERS, SLOTS, CH, 128), BF16),
            pltpu.VMEM((PEERS, SLOTS, CH, 128), BF16),
            pltpu.VMEM((max(SIZES) * SLOTS * CH, 128), F32),
            pltpu.VMEM((CH * 64, 128), F32),
            pltpu.VMEM((2, ROWS * HID, 128), F32),
            pltpu.VMEM((3 * HID, padded), BF16),
            pltpu.VMEM((3 * HID, padded), BF16),
            pltpu.VMEM((3 * CH, padded), BF16),
            pltpu.VMEM((2, (ROWS + 4) * HID, 128), F32),
            pltpu.VMEM((128, COLS * BLOCK), F32),
            pltpu.VMEM((128, COLS * BLOCK), F32),
            pltpu.VMEM((14, HID, 128), BF16),
            pltpu.VMEM((22, HID, 128), BF16),
            pltpu.VMEM((2, 1, HID, 128), BF16),
            pltpu.VMEM((2, 2, HID, 128), BF16),
            pltpu.VMEM((14, CH, 128), BF16),
            pltpu.VMEM((22, CH, 128), BF16),
            pltpu.VMEM((9, HID, 128), BF16),
            pltpu.VMEM((10, HID, 128), BF16),
            pltpu.SemaphoreType.DMA((10,)),
            pltpu.SemaphoreType.DMA,
            pltpu.SemaphoreType.DMA((len(SIZES),)),
            pltpu.SemaphoreType.DMA((STEPS + 2,)),
            pltpu.SemaphoreType.DMA((STEPS + 2,)),
        ],
        compiler_params=pltpu.CompilerParams(
            collective_id=0, has_side_effects=True, vmem_limit_bytes=30 * 2**20
        ),
        name="reproject_and_step",
    )(*[in_hbm(v) for v in operands])
    return hidden.transpose(1, 0, 2), memory.transpose(1, 0, 2)


def solution(mesh):
    placed = (
        P(("lat", "lon"), None, None),
        P(("lat", "lon"), None, None),
        P(("lat", "lon"), None, None, None, None),
        P(("lat", "lon"), None, None),
        P(("lat", "lon"), None),
        P(),
        P(),
        P(),
        P(None, "lat", "lon"),
        P(None, "lat", "lon"),
    )
    return jax.shard_map(
        on_device,
        mesh=mesh,
        in_specs=placed,
        out_specs=(P(None, "lat", "lon"), P(None, "lat", "lon")),
        check_vma=False,
    )
```

```python
import itertools
import random

import jax
import jax.numpy as jnp
import numpy as np
from jax import lax
from jax.experimental import pallas as pl
from jax.experimental.pallas import tpu as pltpu
from jax.sharding import PartitionSpec as P

STEPS = 3
MESH = pl.DeviceIdType.MESH
LOGICAL = pl.DeviceIdType.LOGICAL
F32 = jnp.float32
BF16 = jnp.bfloat16
PEERS = 128
SLOTS = 4
SIZES = (64, 32, 16, 16)
STARTS = (0, 64, 96, 112)
GROUP = 8
BARRIER_AT = 16
BLOCK = 5
HALO = 3
ROWS = 32
COLS = 256
CH = 16
HID = 32


def send_order():
    offsets = [d for d in itertools.product(range(4), range(4), range(4), range(2)) if any(d)]
    random.Random(0).shuffle(offsets)
    return [(0, 0, 0, 0)] + offsets


ORDER = send_order()


def coords():
    i = lax.axis_index("lat")
    j = lax.axis_index("lon")
    return (lax.rem(lax.div(j, 2), 4), lax.div(i, 4) * 2 + lax.div(j, 8), lax.rem(i, 4), lax.rem(j, 2))


class Places:
    def __init__(self):
        x, y, z, c = coords()
        ys = [lax.rem(y + d, 4) for d in range(4)]
        self.x = [lax.rem(x + d, 4) * 2 for d in range(4)]
        self.y = [lax.div(v, 2) * 64 + lax.rem(v, 2) * 8 for v in ys]
        self.z = [lax.rem(z + d, 4) * 16 for d in range(4)]
        self.c = [lax.rem(c + d, 2) for d in range(2)]
        self.sums = {}

    def __call__(self, offset, sign=1):
        dx, dy, dz, dc = ((sign * d) % m for d, m in zip(offset, (4, 4, 4, 2)))
        key = (dy, dz, dc)
        if key not in self.sums:
            self.sums[key] = self.z[dz] + self.y[dy] + self.c[dc]
        return self.sums[key] + self.x[dx]


def lanes(shape):
    return lax.broadcasted_iota(jnp.int32, shape, len(shape) - 1)


def sublanes(shape):
    return lax.broadcasted_iota(jnp.int32, shape, len(shape) - 2)


def roll(x, shift):
    return pltpu.roll(x, shift, 1)


def band(n, to, to_index, tab, stab, x_ref, w_ref):
    tile = tab[n]
    lane = lanes((8, 128)) + sublanes((8, 128))
    inside = (lane >= 4) & (lane < 132)
    for s in range(SLOTS):
        x = x_ref[stab[0, s, tile]].astype(F32)
        w = jnp.where(inside, w_ref[tile, s].astype(F32), 0.0)
        total = w[4:5] * x
        for k in (0, 1, 2, 3, 5, 6, 7):
            total = total + w[k : k + 1] * roll(x, (4 - k) % 128)
        to[to_index, s] = total.astype(BF16)


def row_at(rows_ref, y, count):
    row = pl.ds(pl.multiple_of(y * count, count), count)
    return rows_ref[0, row], rows_ref[1, row]


def spread(halves, into, count, at):
    row = jnp.concatenate(halves, axis=1).astype(BF16)
    where = pl.ds(at, COLS)
    into[0:count, where] = roll(row, 1)
    into[count : 2 * count, where] = row
    into[2 * count : 3 * count, where] = roll(row, COLS - 1)


def padded_at(y):
    return (y + HALO) * COLS if isinstance(y, int) else pl.multiple_of((y + HALO) * COLS, COLS)


class Picker:
    def __init__(self, left_lane, right_lane, count):
        self.left, self.right = left_lane, right_lane
        self.shape = (count, 128)

    def empty(self):
        return jnp.zeros(self.shape, F32), jnp.zeros(self.shape, F32)

    def take(self, state, halves):
        lane = lanes(self.shape)
        return (
            jnp.where(lane == self.left, halves[0], roll(state[0], 1)),
            jnp.where(lane == self.right, halves[1], roll(state[1], 1)),
        )

    def place(self, state, lowest=0):
        lane = lanes(self.shape)
        left = roll(state[0], (lowest + HALO - self.left) % 128)
        right = roll(state[1], (lowest + HALO + 64 - self.right) % 128)
        first, last = lowest + HALO, HALO + ROWS - 1
        return jnp.where(
            (lane >= first) & (lane <= last),
            left,
            jnp.where((lane >= first + 64) & (lane <= last + 64), right, 0.0),
        )

    def insert(self, value, y, halves):
        lane = lanes(self.shape)
        at = y + HALO
        value = jnp.where(lane == at, roll(halves[0], (at - self.left) % 128), value)
        return jnp.where(lane == at + 64, roll(halves[1], (at + 64 - self.right) % 128), value)


def corners(edge, y, halves):
    lane = lanes(edge.shape)
    left = roll(edge, (-(y + HALO)) % 128)
    right = roll(edge, (63 - HALO - y) % 128)
    return jnp.where(lane == 0, left, halves[0]), jnp.where(lane == 127, right, halves[1])


def stage(q_ref, row_of, depth, columns):
    top = [h for y in range(depth) for h in row_of(y)]
    bottom = [h for y in range(ROWS - depth, ROWS) for h in row_of(y)]
    for k, v in enumerate((*top, *columns, *bottom)):
        q_ref[k] = v.astype(BF16)


def swap(plan, q_ref, r_ref, send_sem, recv_sem):
    i = lax.axis_index("lat")
    j = lax.axis_index("lon")
    lat = {0: i, -1: lax.rem(i + 7, 8), 1: lax.rem(i + 1, 8)}
    lon = {0: j, -1: lax.rem(j + 15, 16), 1: lax.rem(j + 1, 16)}
    for di, dj, source, size, slot in plan:
        pltpu.make_async_remote_copy(
            src_ref=q_ref.at[pl.ds(source, size)],
            dst_ref=r_ref.at[pl.ds(slot, size)],
            send_sem=send_sem,
            recv_sem=recv_sem,
            device_id=(lat[di], lon[dj]),
            device_id_type=MESH,
        ).start()


DEEP = (
    (-1, 0, 0, 8, 8), (1, 0, 6, 8, 0), (0, -1, 6, 1, 17), (0, 1, 6, 1, 16),
    (-1, -1, 6, 1, 21), (-1, 1, 6, 1, 20), (1, -1, 6, 1, 19), (1, 1, 6, 1, 18),
)
CELLS = ((-1, 0, 0, 5, 5), (1, 0, 4, 5, 0))
SIDES = ((0, -1, 0, 1, 1), (0, 1, 0, 1, 0))


def whole(r_ref, send_sem, recv_sem):
    i = lax.axis_index("lat")
    return pltpu.make_async_remote_copy(
        src_ref=r_ref,
        dst_ref=r_ref,
        send_sem=send_sem,
        recv_sem=recv_sem,
        device_id=(lax.rem(i + 1, 8), lax.axis_index("lon")),
        device_id_type=MESH,
    )


def in_globe(y):
    i = lax.axis_index("lat")
    return ((y >= 0) | (i > 0)) & ((y < ROWS) | (i < 7))


def frame(count, middle, above, below):
    lane = lanes((count, 128))
    y = jnp.where(lane < 64, lane, lane - 64) - HALO
    live = in_globe(y) & (y < ROWS + HALO)
    picked = jnp.where(y < 0, roll(above, 96), jnp.where(y < ROWS, middle, roll(below, 32)))
    return jnp.where(live, picked, 0.0)


def taps_of(edges, nears, sides):
    half = lanes(edges.shape) < 64
    three = (jnp.where(half, sides, nears), edges, jnp.where(half, nears, sides))
    above = [roll(v, 1) for v in three]
    below = [roll(v, 127) for v in three]
    return jnp.concatenate([v.astype(BF16) for v in (*above, *three, *below)], axis=0)


def deep_taps(edge, near, r_ref, count):
    got = lambda k: r_ref[k].astype(F32)
    half = lanes((count, 128)) < 64
    swapped = [roll(jnp.where(half, got(k + 1), got(k)), 64) for k in (16, 18, 20)]
    return taps_of(
        frame(count, edge, got(0), got(14)), frame(count, near, got(1), got(15)), frame(count, *swapped)
    )


def halo_rows(r_ref, into, count):
    for slot, y in ((2, -3), (4, -2), (6, -1), (8, 32), (10, 33), (12, 34)):
        halves = [jnp.where(in_globe(y), r_ref[slot + k].astype(F32), 0.0) for k in range(2)]
        spread(halves, into, count, padded_at(y))


def update(gates, memory):
    ingate = jnp.tanh(gates[0:HID]) * 0.5 + 0.5
    forget = jnp.tanh(gates[HID : 2 * HID]) * 0.5 + 0.5
    outgate = jnp.tanh(gates[2 * HID : 3 * HID]) * 0.5 + 0.5
    memory = forget * memory + ingate * jnp.tanh(gates[3 * HID :])
    return outgate * jnp.tanh(memory), memory


def halves_of(v):
    return v[:, :128], v[:, 128:]


def body(
    stab_hbm, x_hbm, w_hbm, hid_hbm, cell_hbm, target_hbm, count_hbm, state_hbm, input_hbm, bias_hbm,
    hout_ref, cout_ref,
    tab, stab, x_ref, w_ref, hid_ref, cell_ref, target_ref, count_ref, state_ref, input_ref, bias_ref, weight, out_buf, in_buf, wide, sums, rows, s0, s1, fshifted, cells, ga, gb,
    qh, rh, qe, re, qf, rf, qc, rc, load_sem, far_send, far_recv, near_send, near_recv,
):
    loads = [
        pltpu.make_async_copy(a, b, load_sem.at[k])
        for k, (a, b) in enumerate(
            (
                (stab_hbm, stab), (x_hbm, x_ref), (w_hbm, w_ref), (hid_hbm, hid_ref), (cell_hbm, cell_ref),
                (target_hbm, target_ref), (count_hbm, count_ref), (state_hbm, state_ref), (input_hbm, input_ref),
                (bias_hbm, bias_ref),
            )
        )
    ]
    for copy in loads:
        copy.start()
    at = Places()
    barrier = pltpu.get_barrier_semaphore()
    tab[0] = at(ORDER[0])
    for offset in sorted(ORDER[1:], key=lambda d: -sum(min(a, 4 - a) for a in d[:3])):
        pl.semaphore_signal(barrier, inc=1, device_id=at(offset), device_id_type=LOGICAL)
    for n in range(1, PEERS):
        tab[n] = at(ORDER[n])
    for copy in loads[:3]:
        copy.wait()

    def one_band(n, carry):
        band(n, out_buf, n, tab, stab, x_ref, w_ref)
        return carry

    def send(first, last):
        for n in range(max(first, 1), last):
            chunk = max(k for k in range(len(SIZES)) if STARTS[k] <= n)
            pltpu.make_async_remote_copy(
                src_ref=out_buf.at[n],
                dst_ref=in_buf.at[n],
                send_sem=far_send,
                recv_sem=far_recv.at[chunk],
                device_id=at(ORDER[n]),
                device_id_type=LOGICAL,
            ).start()

    band(0, in_buf, 0, tab, stab, x_ref, w_ref)
    lax.fori_loop(1, GROUP, one_band, 0)
    for first in range(GROUP, PEERS, GROUP):
        lax.fori_loop(first, first + GROUP, one_band, 0)
        if first == BARRIER_AT:
            pl.semaphore_wait(barrier, PEERS - 1)
            send(0, first)
        elif first > BARRIER_AT:
            send(first - GROUP, first)
    send(PEERS - GROUP, PEERS)

    loads[3].wait()
    for c in range(HID):
        for half in range(2):
            rows[half, pl.ds(c, ROWS, stride=HID), :] = hid_ref[c, :, half * 128 : half * 128 + 128].astype(F32)
    outer, inner = Picker(0, 127, HID), Picker(1, 126, HID)

    def prepare(k, state):
        y = ROWS - 1 - k
        halves = row_at(rows, y, HID)
        spread(halves, s0, HID, padded_at(y))
        return outer.take(state[0], halves), inner.take(state[1], halves)

    state = lax.fori_loop(0, ROWS, prepare, (outer.empty(), inner.empty()), unroll=2)
    edge, near = outer.place(state[0]), inner.place(state[1])
    stage(qh, lambda y: row_at(rows, y, HID), HALO, (edge, near))
    swap(DEEP, qh, rh, near_send.at[0], near_recv.at[0])
    for copy in loads[4:]:
        copy.wait()
    for c in range(HID):
        for half in range(2):
            cells[half, pl.ds(c + 2 * HID, ROWS, stride=HID), :] = cell_ref[c, :, half * 128 : half * 128 + 128].astype(F32)

    def prepare_cell(k, state):
        return outer.take(state, row_at(cells, ROWS + 1 - k, HID))

    edge_cell = outer.place(lax.fori_loop(0, ROWS, prepare_cell, outer.empty(), unroll=2))

    stage(qc, lambda y: row_at(cells, y + 2, HID), 2, (edge_cell,))
    swap(CELLS, qc, rc, near_send.at[STEPS + 1], near_recv.at[STEPS + 1])

    scale = jnp.where(sublanes((128, 1)) < 3 * HID, 0.5, 1.0)
    bias = jnp.sum(jnp.where(sublanes((128, 128)) == lanes((128, 128)), bias_ref[...], 0.0), axis=1, keepdims=True)
    bias = bias * scale
    high = bias.astype(BF16).astype(F32)
    middle = (bias - high).astype(BF16).astype(F32)
    low = bias - high - middle
    lane = lanes((128, 128))
    extra = jnp.where(lane == 0, high, jnp.where(lane == 1, middle, jnp.where(lane == 2, low, 0.0)))
    taps = jnp.concatenate([state_ref[...].astype(F32), input_ref[...].astype(F32), extra.T[:80]], axis=0)
    deep = lax.broadcasted_iota(jnp.int32, (128, 128), 1)
    for k in range(4):
        part = taps[k * 128 : k * 128 + 128].T
        mult = jnp.where((deep + k * 128 < 432), scale, 1.0)
        weight[:, k * 128 : k * 128 + 128] = (part * mult).astype(BF16)
    ones = jnp.ones((16, COLS), BF16)

    counts = count_ref[...]
    aim4 = jnp.where(sublanes((SLOTS, 128)) < counts, target_ref[0], -1).astype(F32)
    aim8 = jnp.concatenate([aim4, aim4], axis=0).astype(BF16)
    sums[...] = jnp.zeros_like(sums)
    for g, (start, size) in enumerate(zip(STARTS, SIZES)):
        taken = size * SLOTS
        first = max(start, 1)
        got = in_buf.at[pl.ds(first, start + size - first)]
        pltpu.make_async_remote_copy(
            src_ref=got, dst_ref=got, send_sem=far_send, recv_sem=far_recv.at[g],
            device_id=at(ORDER[1]), device_id_type=LOGICAL,
        ).wait_recv()

        def unpack(n, carry):
            block = in_buf[start + n].astype(F32).reshape(SLOTS * CH, 128)
            wide[pl.ds(pl.multiple_of(n * SLOTS * CH, SLOTS * CH), SLOTS * CH)] = block
            return carry

        lax.fori_loop(0, size, unpack, 0, unroll=4)
        which = lax.shift_right_logical(lanes((1, taken)), 2)
        origin = jnp.zeros((1, taken), jnp.int32)
        for n in range(size):
            origin = jnp.where(which == n, at(ORDER[start + n], -1), origin)
        spot = (sublanes((128, taken)) == origin).astype(F32).astype(BF16)
        aims = jnp.dot(aim8, spot, preferred_element_type=F32)
        mine = sublanes((8, taken)) == lanes((8, taken)) % SLOTS
        aim = jnp.sum(jnp.where(mine, aims, 0.0), axis=0, keepdims=True)
        chosen = (sublanes((64, taken)).astype(F32) == aim).astype(F32).astype(BF16)
        for c in range(0, CH, 2):
            pair = [wide[pl.ds(c + k, taken, stride=CH), :].astype(BF16) for k in range(2)]
            part = jnp.dot(chosen, jnp.concatenate(pair, axis=1), preferred_element_type=F32)
            sums[c * 64 : c * 64 + 64] += part[:, :128]
            sums[c * 64 + 64 : c * 64 + 128] += part[:, 128:]

    def cell_row(y):
        return sums[pl.ds(2 * y, CH, stride=64), :], sums[pl.ds(2 * y + 1, CH, stride=64), :]

    fouter, finner = Picker(0, 127, CH), Picker(1, 126, CH)
    fedge = fnear = jnp.zeros((CH, 128), F32)
    for y in range(ROWS):
        halves = cell_row(y)
        fedge = fouter.insert(fedge, y, halves)
        fnear = finner.insert(fnear, y, halves)
    stage(qf, cell_row, HALO, (fedge, fnear))
    swap(DEEP, qf, rf, near_send.at[STEPS], near_recv.at[STEPS])

    def spread_cells(y, carry):
        spread(cell_row(y), fshifted, CH, padded_at(y))
        return carry

    lax.fori_loop(0, ROWS, spread_cells, 0, unroll=4)

    fmini = None
    for t in range(STEPS):
        here, there = (s0, s1) if t % 2 == 0 else (s1, s0)
        last = t == STEPS - 1

        def gates_of(y, count=1):
            spans = [pl.ds(padded_at(y - 1 + a), COLS * count) for a in range(3)]
            fixed = jnp.ones((16, COLS * count), BF16)
            rhs = jnp.concatenate([here[:, w] for w in spans] + [fshifted[:, w] for w in spans] + [fixed], axis=0)
            return jnp.dot(weight[:, :448], rhs, preferred_element_type=F32)

        def finish_row(y, gates):
            hidden, memory = update(gates, jnp.concatenate(row_at(cells, y + 2, HID), axis=1))
            if not (isinstance(y, int) and 0 <= y < ROWS):
                hidden = jnp.where(in_globe(y), hidden, 0.0) if isinstance(y, int) else hidden
            halves = halves_of(hidden)
            for half, v in enumerate(halves_of(memory)):
                if last:
                    part = slice(half * 128, half * 128 + 128)
                    hout_ref[y, :, part] = halves[half].astype(BF16)
                    cout_ref[y, :, part] = v.astype(BF16)
                else:
                    cells[half, pl.ds(pl.multiple_of((y + 2) * HID, HID), HID)] = v
            if not last:
                spread(halves, there, HID, padded_at(y))
            return halves

        def block(low, buffer, state):
            for r in range(BLOCK - 1, -1, -1):
                halves = finish_row(low + r, buffer[:, r * COLS : r * COLS + COLS])
                state = state if last else inner.take(state, halves)
            return state

        def inside(k, state):
            low = ROWS - 1 - BLOCK - 2 * BLOCK * k
            gb[...] = gates_of(low - BLOCK, BLOCK)
            state = block(low, ga, state)
            ga[...] = gates_of(lax.max(low - 2 * BLOCK, 1), BLOCK)
            return block(low - BLOCK, gb, state)

        ga[...] = gates_of(ROWS - 1 - BLOCK, BLOCK)
        state = 0 if last else inner.empty()
        state = lax.fori_loop(0, (ROWS - 2) // (2 * BLOCK), inside, state)

        if t == 0:
            for k, got in ((0, rh), (STEPS + 1, rc)):
                whole(got, near_send.at[k], near_recv.at[k]).wait_recv()
            halo_rows(rh, here, HID)
            for slot, y in ((1, -2), (3, -1), (5, 32), (7, 33)):
                for half in range(2):
                    cells[half, (y + 2) * HID : (y + 3) * HID] = rc[slot + half].astype(F32)
            edge_cell = frame(HID, edge_cell, rc[0].astype(F32), rc[9].astype(F32))
            mini = deep_taps(edge, near, rh, HID)
            whole(rf, near_send.at[STEPS], near_recv.at[STEPS]).wait_recv()
            halo_rows(rf, fshifted, CH)
            fmini = deep_taps(fedge, fnear, rf, CH)
        depth = STEPS - t
        if t > 0:
            whole(re.at[t - 1], near_send.at[t], near_recv.at[t]).wait_recv()
            half = lanes((HID, 128)) < 64
            sides = roll(jnp.where(half, re[t - 1, 1].astype(F32), re[t - 1, 0].astype(F32)), 64)
            mini = taps_of(edge, near, sides)
        mini = jnp.concatenate([mini, fmini, ones[:, :128]], axis=0)
        gates = jnp.dot(weight[:, :448], mini, preferred_element_type=F32)
        edge, edge_cell = update(gates, edge_cell)
        if last:
            low, high = gates_of(1 - depth, depth), gates_of(ROWS - 1, depth)
            above = [finish_row(-r, low[:, (depth - 1 - r) * COLS : (depth - r) * COLS]) for r in range(depth)]
            below = [finish_row(ROWS - 1 + r, high[:, r * COLS : (r + 1) * COLS]) for r in range(depth)]
            break
        lane = lanes((HID, 128))
        edge = jnp.where(in_globe(jnp.where(lane < 64, lane, lane - 64) - HALO), edge, 0.0)
        qe[t, 0] = edge.astype(BF16)
        left = {y: roll(edge, (1 - HALO - y) % 128).astype(BF16) for y in range(1 - depth, ROWS + depth)}
        right = {y: roll(edge, (63 - HALO - y) % 128).astype(BF16) for y in range(1 - depth, ROWS + depth)}
        swap(SIDES, qe.at[t], re.at[t], near_send.at[t + 1], near_recv.at[t + 1])
        low, high = gates_of(1 - depth, depth), gates_of(ROWS - 1, depth)
        above = [finish_row(-r, low[:, (depth - 1 - r) * COLS : (depth - r) * COLS]) for r in range(depth)]
        below = [finish_row(ROWS - 1 + r, high[:, r * COLS : (r + 1) * COLS]) for r in range(depth)]
        for halves in above:
            state = inner.take(state, halves)
        near = inner.place(state, 1 - depth)
        near = jnp.where((lane == 34) | (lane == 98), 0.0, near)
        for r, halves in enumerate(below):
            near = inner.insert(near, ROWS - 1 + r, halves)
        for y in range(1 - depth, ROWS + depth - 1):
            first = pl.ds(padded_at(y), 128)
            second = pl.ds(padded_at(y) + 128, 128)
            for block_at, where, spot, value in (
                (0, first, 1, left[y]), (1, first, 0, left[y + 1]),
                (1, second, 127, right[y]), (2, second, 126, right[y + 1]),
            ):
                part = there.at[block_at * HID : block_at * HID + HID, where]
                part[...] = jnp.where(lane == spot, value, part[...])

    lane = lanes((HID, 128))
    for columns, to in ((edge, hout_ref), (edge_cell, cout_ref)):
        for y in range(ROWS):
            left = roll(columns, (-(y + HALO)) % 128).astype(BF16)
            right = roll(columns, (63 - HALO - y) % 128).astype(BF16)
            to[y, :, :128] = jnp.where(lane == 0, left, to[y, :, :128])
            to[y, :, 128:] = jnp.where(lane == 127, right, to[y, :, 128:])

    sent = out_buf.at[pl.ds(1, PEERS - 1)]
    pltpu.make_async_remote_copy(
        src_ref=sent, dst_ref=sent, send_sem=far_send, recv_sem=far_recv.at[0],
        device_id=at(ORDER[1]), device_id_type=LOGICAL,
    ).wait_send()
    for k, got in ((0, rh), (1, re.at[0]), (2, re.at[1]), (STEPS, rf), (STEPS + 1, rc)):
        whole(got, near_send.at[k], near_recv.at[k]).wait_send()


def in_hbm(x):
    return pltpu.with_memory_space_constraint(x, pltpu.HBM)


def on_device(
    satellite_blocks, slot_source, slot_weight, slot_target, tile_counts,
    gate_input_weight, gate_state_weight, gate_bias, hidden_init, cell_init,
):
    operands = (
        slot_source.transpose(0, 2, 1), satellite_blocks, slot_weight[0], hidden_init, cell_init,
        slot_target.transpose(0, 2, 1), tile_counts, gate_state_weight.T, gate_input_weight.T, gate_bias.reshape(1, -1),
    )
    vmem = pl.BlockSpec(memory_space=pltpu.VMEM)
    hbm = pl.BlockSpec(memory_space=pltpu.HBM)
    padded = (ROWS + 2 * HALO) * COLS
    hidden, memory = pl.pallas_call(
        body,
        out_shape=[jax.ShapeDtypeStruct((ROWS, HID, COLS), BF16)] * 2,
        in_specs=[hbm] * 10,
        out_specs=[vmem, vmem],
        scratch_shapes=[
            pltpu.SMEM((PEERS,), jnp.int32),
            pltpu.SMEM((1, SLOTS, PEERS), jnp.int32),
            pltpu.VMEM((PEERS, CH, 128), BF16),
            pltpu.VMEM((PEERS, SLOTS, 8, 128), BF16),
            pltpu.VMEM((HID, ROWS, COLS), BF16),
            pltpu.VMEM((HID, ROWS, COLS), BF16),
            pltpu.VMEM((1, SLOTS, PEERS), jnp.int32),
            pltpu.VMEM((1, PEERS), jnp.int32),
            pltpu.VMEM((9 * HID, 128), BF16),
            pltpu.VMEM((9 * CH, 128), BF16),
            pltpu.VMEM((1, 128), F32),
            pltpu.VMEM((128, 512), BF16),
            pltpu.VMEM((PEERS, SLOTS, CH, 128), BF16),
            pltpu.VMEM((PEERS, SLOTS, CH, 128), BF16),
            pltpu.VMEM((max(SIZES) * SLOTS * CH, 128), F32),
            pltpu.VMEM((CH * 64, 128), F32),
            pltpu.VMEM((2, ROWS * HID, 128), F32),
            pltpu.VMEM((3 * HID, padded), BF16),
            pltpu.VMEM((3 * HID, padded), BF16),
            pltpu.VMEM((3 * CH, padded), BF16),
            pltpu.VMEM((2, (ROWS + 4) * HID, 128), F32),
            pltpu.VMEM((128, COLS * BLOCK), F32),
            pltpu.VMEM((128, COLS * BLOCK), F32),
            pltpu.VMEM((14, HID, 128), BF16),
            pltpu.VMEM((22, HID, 128), BF16),
            pltpu.VMEM((2, 1, HID, 128), BF16),
            pltpu.VMEM((2, 2, HID, 128), BF16),
            pltpu.VMEM((14, CH, 128), BF16),
            pltpu.VMEM((22, CH, 128), BF16),
            pltpu.VMEM((9, HID, 128), BF16),
            pltpu.VMEM((10, HID, 128), BF16),
            pltpu.SemaphoreType.DMA((10,)),
            pltpu.SemaphoreType.DMA,
            pltpu.SemaphoreType.DMA((len(SIZES),)),
            pltpu.SemaphoreType.DMA((STEPS + 2,)),
            pltpu.SemaphoreType.DMA((STEPS + 2,)),
        ],
        compiler_params=pltpu.CompilerParams(
            collective_id=0, has_side_effects=True, vmem_limit_bytes=30 * 2**20
        ),
        name="reproject_and_step",
    )(*[in_hbm(v) for v in operands])
    return hidden.transpose(1, 0, 2), memory.transpose(1, 0, 2)


def solution(mesh):
    placed = (
        P(("lat", "lon"), None, None),
        P(("lat", "lon"), None, None),
        P(("lat", "lon"), None, None, None, None),
        P(("lat", "lon"), None, None),
        P(("lat", "lon"), None),
        P(),
        P(),
        P(),
        P(None, "lat", "lon"),
        P(None, "lat", "lon"),
    )
    return jax.shard_map(
        on_device,
        mesh=mesh,
        in_specs=placed,
        out_specs=(P(None, "lat", "lon"), P(None, "lat", "lon")),
        check_vma=False,
    )
```
